32 devices in a mesh: dp: 8 (over z, x), tensor: 4 (over y, core).
Axes of the slice: x: 2, y: 2, z: 4, core: 2. Of those that a mesh axis runs over, the one named last changes fastest.
Arguments:
- tokens: bfloat16 [16, 1088, 1024], P('dp', 'tensor'), may hold values from -12 to 12
- cotangent: bfloat16 [16, 1088, 1024], P('dp', 'tensor'), may hold values from -6 to 6
- lengths: int32 [16], P('dp'), may hold values from 544 to 1088, as said below
- groups: int32 [16], P('dp'), may hold values from 0 to 3, as said below
- w_qkv: bfloat16 [1024, 3, 1024], P(None, None, 'tensor'), may hold values from -0.1875 to 0.1875
- w_out: bfloat16 [1024, 1024], P('tensor'), may hold values from -0.75 to 0.75
- w_up: bfloat16 [1024, 4096], P(None, 'tensor'), may hold values from -0.1875 to 0.1875
- w_down: bfloat16 [4096, 1024], P('tensor'), may hold values from -0.09375 to 0.09375
- gains: float32 [4, 1024], replicated, may hold values from 0.25 to 1.75
- biases: float32 [4, 1024], replicated, may hold values from -1.5 to 1.5
Outputs:
- output: bfloat16 [16, 1088, 1024], P('dp', 'tensor')
- input_grad: bfloat16 [16, 1088, 1024], P('dp', 'tensor')
- grad_qkv: float32 [1024, 3, 1024], P(None, None, 'tensor')
- grad_out: float32 [1024, 1024], P('tensor')
- grad_up: float32 [1024, 4096], P(None, 'tensor')
- grad_down: float32 [4096, 1024], P('tensor')
- grad_gains: float32 [4, 1024], replicated
- grad_biases: float32 [4, 1024], replicated
- group_rms: float32 [4, 3], replicated
The draws below stay inside these ranges and needn't reach their ends.
Inputs may be any that keep to these rules, and one draw needn't show every extreme that they name: `lengths`: some row has all 1088 slots valid. `groups`: every group has at least one row.
All inputs are finite; a program needn't handle non-finite values.
Results may differ from the reference program's by a relative error of at most 0.013.
Values may be sent and summed in bfloat16 or wider, within the bound.
No kernel may reach another device: no remote copies, remote signals or barrier semaphores. Data moves between devices by JAX's collectives and lax.ppermute only.
A program may use at most 192 MiB of HBM per device.

```python
import jax
import jax.numpy as jnp
from jax import lax

D = 1024
HEADS = 16
HEAD_DIM = 64
FF = 4096
SLOTS = 1088
QBLOCK = 544
GROUPS = 4
ROWS = 16


def draw_tokens(key, part):
    scale_key = jax.random.fold_in(key, 11)
    value_key = jax.random.fold_in(key, 13)
    row_scale = jnp.exp(jax.random.uniform(scale_key, (ROWS, 1, 1), jnp.float32, jnp.log(0.5), jnp.log(3.0)))
    base = jnp.clip(jax.random.normal(value_key, (ROWS, SLOTS, D), jnp.float32), -4.0, 4.0)
    return (base * row_scale).astype(jnp.bfloat16)


def draw_lengths(key, part):
    drawn = jax.random.randint(key, (ROWS,), SLOTS // 2, SLOTS + 1, dtype=jnp.int32)
    row_index = jnp.arange(ROWS, dtype=jnp.int32)
    return jnp.where(row_index == 0, SLOTS, drawn).astype(jnp.int32)


def draw_groups(key, part):
    drawn = jax.random.randint(jax.random.fold_in(key, 7), (ROWS,), 0, 16, dtype=jnp.int32)
    uneven = jnp.zeros((ROWS,), jnp.int32)
    for level_index in range(1, GROUPS):
        uneven = uneven + (drawn >= 16 - 16 // 2 ** level_index).astype(jnp.int32)
    row_index = jnp.arange(ROWS, dtype=jnp.int32)
    return jnp.where(row_index < GROUPS, row_index, uneven).astype(jnp.int32)


def block_levels(own_key, extent, pieces, smallest, largest):
    loudness, own = 1.0, jax.random.fold_in(own_key, 6)
    for position, blocks in pieces:
        heights = jnp.exp(jax.random.uniform(jax.random.fold_in(own, position), (blocks,), jnp.float32, smallest / len(pieces), largest / len(pieces)))
        loudness = loudness * jnp.repeat(heights, extent[position] // blocks).reshape([-1 if axis == position else 1 for axis in range(len(extent))])
    return loudness


def normal_values(stream_key, extent, width, limit, cuts=(), held_as=jnp.bfloat16):
    values = jax.random.normal(stream_key, extent, jnp.float32) * width
    if len(cuts) > 0:
        values = block_levels(stream_key, extent, cuts, -0.22, 0.18) * values
    return jnp.clip(values, min=-limit, max=limit).astype(held_as)


def setup_inputs(seed: int = 0) -> dict:
    keys = jax.random.split(jax.random.key(seed), 11)
    tokens = draw_tokens(jax.random.fold_in(keys[10], 71), 0)
    cotangent = normal_values(keys[1], (ROWS, SLOTS, D), 1.0, 6.0, ((0, 8), (1, 4)))
    lengths = draw_lengths(jax.random.fold_in(keys[10], 71), 0)
    groups = draw_groups(jax.random.fold_in(keys[10], 71), 0)
    w_qkv = normal_values(keys[4], (D, 3, D), D ** -0.5, 0.1875, ((2, 4),))
    w_out = normal_values(keys[5], (D, D), (D // 16) ** -0.5, 0.75, ((0, 4),))
    w_up = normal_values(keys[6], (D, FF), D ** -0.5, 0.1875, ((1, 4),))
    w_down = normal_values(keys[7], (FF, D), FF ** -0.5, 0.09375, ((0, 4),))
    gains = jnp.clip(1.0 + 0.15 * jax.random.normal(keys[8], (4, D), jnp.float32), 0.25, 1.75)
    biases = normal_values(keys[9], (4, D), 0.3, 1.5, (), jnp.float32)
    return dict(tokens=tokens, cotangent=cotangent, lengths=lengths, groups=groups, w_qkv=w_qkv, w_out=w_out, w_up=w_up, w_down=w_down, gains=gains, biases=biases)


highest = lax.Precision.HIGHEST
epsilon = 1e-05
negative_fill = -1e+30
relax_alpha = 32.0

@jax.custom_vjp
def low(v):
    return lax.optimization_barrier(v.astype(jnp.bfloat16)).astype(jnp.float32)

@jax.custom_vjp
def low_back(v):
    return v

def low_keep(v):
    return (low(v), None)

def low_pass(kept, grad):
    return (grad,)

def back_keep(v):
    return (v, None)

def back_low(kept, grad):
    return (low(grad),)
low.defvjp(low_keep, low_pass)
low_back.defvjp(back_keep, back_low)

def layer_norm(values, scale_vec, shift_vec):
    center = values - lax.optimization_barrier(jnp.mean(values, axis=-1, keepdims=True))
    spread = lax.optimization_barrier(jnp.mean(center * center, axis=-1, keepdims=True))
    return center * lax.rsqrt(spread + epsilon) * scale_vec + shift_vec

def attend_block(query_block, keys_all, values_all, block_index, length):
    scores = jnp.einsum('qhd,khd->hqk', query_block, keys_all, precision=highest) * (1.0 / (relax_alpha * HEAD_DIM ** 0.5))
    scores = low_back(scores)
    key_index = jnp.arange(SLOTS, dtype=jnp.int32)
    query_index = block_index * QBLOCK + jnp.arange(QBLOCK, dtype=jnp.int32)
    allowed = (key_index[None, :] <= query_index[:, None]) & (key_index[None, :] < length)
    masked = jnp.where(allowed[None], scores, negative_fill)
    row_max = lax.optimization_barrier(jnp.max(masked, axis=-1, keepdims=True))
    relaxed = relax_alpha * (masked - row_max)
    probs = jax.nn.softmax(relaxed, axis=-1)
    return jnp.einsum('hqk,khd->qhd', low(probs), values_all, precision=highest)

def attend(queries, keys_all, values_all, length):
    block_count = SLOTS // QBLOCK
    query_blocks = queries.reshape(block_count, QBLOCK, HEADS, HEAD_DIM)
    checked = jax.checkpoint(attend_block)

    def one_block(block_pair):
        return checked(block_pair[0], keys_all, values_all, block_pair[1], length)
    outputs = lax.map(one_block, (query_blocks, jnp.arange(block_count, dtype=jnp.int32)))
    return outputs.reshape(SLOTS, HEADS * HEAD_DIM)

def row_forward(inputs_row, weight_qkv, weight_out, weight_up, weight_down, gain_rows, bias_rows, length):
    normed = low(layer_norm(inputs_row, gain_rows[0], bias_rows[0]))
    projected = jnp.einsum('sd,dtc->stc', normed, weight_qkv, precision=highest)
    projected = low_back(low(projected))
    queries = projected[:, 0].reshape(SLOTS, HEADS, HEAD_DIM)
    keys_all = projected[:, 1].reshape(SLOTS, HEADS, HEAD_DIM)
    values_all = projected[:, 2].reshape(SLOTS, HEADS, HEAD_DIM)
    attended = low_back(low(attend(queries, keys_all, values_all, length)))
    attn_sum = low_back(jnp.dot(attended, weight_out, precision=highest))
    attn_branch = layer_norm(attn_sum, gain_rows[1], bias_rows[1])
    middle = inputs_row + attn_branch
    ffn_in = low(layer_norm(middle, gain_rows[2], bias_rows[2]))
    hidden = low_back(jnp.dot(ffn_in, weight_up, precision=highest))
    activated = low(jax.nn.gelu(hidden, approximate=True))
    ffn_sum = low_back(jnp.dot(activated, weight_down, precision=highest))
    ffn_branch = layer_norm(ffn_sum, gain_rows[3], bias_rows[3])
    return (middle + ffn_branch, attn_branch, ffn_branch)

def reference(tokens, cotangent, lengths, groups, w_qkv, w_out, w_up, w_down, gains, biases):
    params = (w_qkv.astype(jnp.float32), w_out.astype(jnp.float32), w_up.astype(jnp.float32), w_down.astype(jnp.float32), gains.astype(jnp.float32), biases.astype(jnp.float32))

    def row_step(totals, row_inputs):
        token_row, cot_row, length = row_inputs
        valid = (jnp.arange(SLOTS, dtype=jnp.int32) < length).astype(jnp.float32)

        def forward(inputs_row, weight_qkv, weight_out, weight_up, weight_down, gain_rows, bias_rows):
            return row_forward(inputs_row, weight_qkv, weight_out, weight_up, weight_down, gain_rows, bias_rows, length)
        (result, attn_branch, ffn_branch), backward = jax.vjp(forward, token_row.astype(jnp.float32), *params)
        grads = backward((cot_row.astype(jnp.float32) * valid[:, None], jnp.zeros_like(attn_branch), jnp.zeros_like(ffn_branch)))
        totals = tuple((total_grad + new_grad for total_grad, new_grad in zip(totals, grads[1:])))
        squares = jnp.stack([jnp.sum(valid * lax.optimization_barrier(jnp.sum(branch_out * branch_out, axis=-1))) for branch_out in (result, attn_branch, ffn_branch)])
        return (totals, (result.astype(jnp.bfloat16), grads[0].astype(jnp.bfloat16), squares))
    initial = tuple((jnp.zeros_like(param_array) for param_array in params))
    totals, (output, input_grad, squares) = lax.scan(row_step, initial, (tokens, cotangent, lengths))
    member = (groups[:, None] == jnp.arange(GROUPS, dtype=jnp.int32)[None, :]).astype(jnp.float32)
    group_sums = lax.optimization_barrier(jnp.sum(member[:, :, None] * squares[:, None, :], axis=0))
    group_counts = lax.optimization_barrier(jnp.sum(member * lengths.astype(jnp.float32)[:, None], axis=0))
    group_rms = jnp.sqrt(group_sums / (group_counts[:, None] * D))
    return (output, input_grad, totals[0], totals[1], totals[2], totals[3], totals[4], totals[5], group_rms)
```

```python
import functools

import jax
import jax.numpy as jnp
from jax import lax
from jax.experimental import pallas as pl
from jax.experimental.pallas import tpu as pltpu
from jax.sharding import PartitionSpec as P

HEAD_DIM = 64
GROUPS = 4
MIN_LENGTH = 544
F32 = jnp.float32
B16 = jnp.bfloat16

epsilon = 1e-05
negative_fill = -1e30
log2_e = 1.4426950408889634
gelu_scale = 0.7978845608028654
gelu_cubic = 0.044715


def nt(left, right):
    return lax.dot_general(
        left, right, (((1,), (1,)), ((), ())), preferred_element_type=F32
    )


def nn(left, right):
    return lax.dot_general(
        left, right, (((1,), (0,)), ((), ())), preferred_element_type=F32
    )


def tn(left, right):
    return lax.dot_general(
        left, right, (((0,), (0,)), ((), ())), preferred_element_type=F32
    )


def tiles(extent, size):
    return [(start, min(size, extent - start)) for start in range(0, extent, size)]


def lane_half(shape, half):
    return (lax.broadcasted_iota(jnp.int32, shape, 1) // HEAD_DIM) == half


def mask_tile(scores, key_start, query_start, length):
    key_count, query_count = scores.shape
    key_index = key_start + lax.broadcasted_iota(jnp.int32, scores.shape, 0)
    allowed = None
    if key_start + key_count - 1 > query_start:
        query_index = query_start + lax.broadcasted_iota(jnp.int32, scores.shape, 1)
        allowed = key_index <= query_index
    if key_start + key_count > MIN_LENGTH:
        inside = key_index < length
        allowed = inside if allowed is None else allowed & inside
    return scores if allowed is None else jnp.where(allowed, scores, negative_fill)


def attend_kernel(slots, chunk, parts, query_tile, key_tile, meta, *refs):
    inputs = refs[:parts]
    outputs = refs[parts : 2 * parts]
    lse_ref = refs[2 * parts]
    q_ref, k_ref, vt_ref, s_ref, p_ref, ot_ref = refs[2 * parts + 1 :]
    half = pl.program_id(0) % 2
    length = meta[0]
    per = inputs[0].shape[0] // chunk

    @pl.when(half == 0)
    def _():
        for part, source in enumerate(inputs):
            for piece in range(per):
                place = pl.multiple_of(meta[1 + part * per + piece], 16)
                rows = pl.ds(piece * chunk, chunk)
                q_ref[pl.ds(place, chunk), :] = source[rows, 0:128]
                k_ref[pl.ds(place, chunk), :] = source[rows, 128:256]
                p_ref[pl.ds(place, chunk), 0:128] = source[rows, 256:384]
        vt_ref[...] = p_ref[0:slots, 0:128].T

    scale = log2_e / HEAD_DIM**0.5
    base = pl.multiple_of(half * HEAD_DIM, HEAD_DIM)
    for q0, qn in tiles(slots, query_tile):
        query = q_ref[q0 : q0 + qn, :]
        query = jnp.where(lane_half(query.shape, half), query, jnp.zeros_like(query))
        extent = q0 + qn
        top = jnp.full((1, qn), negative_fill, F32)
        for k0, kn in tiles(extent, key_tile):
            scores = mask_tile(nt(k_ref[k0 : k0 + kn, :], query), k0, q0, length)
            s_ref[k0 : k0 + kn, 0:qn] = scores
            top = jnp.maximum(top, jnp.max(scores, axis=0, keepdims=True))
        total = jnp.zeros((1, qn), F32)
        for k0, kn in tiles(extent, key_tile):
            weights = jnp.exp2((s_ref[k0 : k0 + kn, 0:qn] - top) * scale)
            total = total + jnp.sum(weights, axis=0, keepdims=True)
            p_ref[k0 : k0 + kn, 0:qn] = weights.astype(B16)
        out_t = nn(vt_ref[pl.ds(base, HEAD_DIM), 0:extent], p_ref[0:extent, 0:qn])
        ot_ref[pl.ds(base, HEAD_DIM), q0 : q0 + qn] = out_t * (1.0 / total)
        lse_ref[0, :, q0 : q0 + qn] = top * scale + jnp.log2(total)

    @pl.when(half == 1)
    def _():
        q_ref[...] = ot_ref[...].T.astype(B16)
        for part, target in enumerate(outputs):
            for piece in range(per):
                place = pl.multiple_of(meta[1 + part * per + piece], 16)
                target[pl.ds(piece * chunk, chunk), :] = q_ref[pl.ds(place, chunk), :]


def attend(meta, projected, chunk):
    parts = len(projected)
    rows, width = projected[0].shape
    pairs = width // 384
    slots, heads = rows * parts, 2 * pairs
    return pl.pallas_call(
        functools.partial(attend_kernel, slots, chunk, parts, 256, 128),
        out_shape=[jax.ShapeDtypeStruct((rows, pairs * 128), B16)] * parts
        + [jax.ShapeDtypeStruct((heads, 1, slots), F32)],
        grid_spec=pltpu.PrefetchScalarGridSpec(
            num_scalar_prefetch=1,
            grid=(heads,),
            in_specs=[pl.BlockSpec((rows, 384), lambda h, m: (0, h // 2))] * parts,
            out_specs=[pl.BlockSpec((rows, 128), lambda h, m: (0, h // 2))] * parts
            + [pl.BlockSpec((1, 1, slots), lambda h, m: (h, 0, 0))],
            scratch_shapes=[
                pltpu.VMEM((slots, 128), B16),
                pltpu.VMEM((slots, 128), B16),
                pltpu.VMEM((128, slots), B16),
                pltpu.VMEM((slots, 256), F32),
                pltpu.VMEM((slots, 256), B16),
                pltpu.VMEM((128, slots), F32),
            ],
        ),
        compiler_params=pltpu.CompilerParams(
            dimension_semantics=("arbitrary",), vmem_limit_bytes=24 << 20
        ),
        cost_estimate=pl.CostEstimate(
            flops=heads * slots * slots * HEAD_DIM * 16,
            bytes_accessed=slots * pairs * 1024,
            transcendentals=heads * slots * slots // 2,
        ),
        name="attend",
    )(meta, *projected)


def attend_back_kernel(slots, chunk, parts, query_tile, key_tile, meta, *refs):
    inputs = refs[:parts]
    attended = refs[parts : 2 * parts]
    grads = refs[2 * parts : 3 * parts]
    lse_ref = refs[3 * parts]
    outputs = refs[3 * parts + 1 : 4 * parts + 1]
    q_ref, k_ref, v_ref, g_ref, kt_ref, inner_ref, dk_ref, dv_ref, dqt_ref, t_ref = refs[
        4 * parts + 1 :
    ]
    half = pl.program_id(0) % 2
    length = meta[0]
    per = inputs[0].shape[0] // chunk

    @pl.when(half == 0)
    def _():
        for part, source in enumerate(inputs):
            for piece in range(per):
                place = pl.multiple_of(meta[1 + part * per + piece], 16)
                rows, target = pl.ds(piece * chunk, chunk), pl.ds(place, chunk)
                q_ref[target, :] = source[rows, 0:128]
                k_ref[target, :] = source[rows, 128:256]
                v_ref[target, :] = source[rows, 256:384]
                g_ref[target, :] = grads[part][rows, :]
                t_ref[target, :] = attended[part][rows, :].astype(F32) * grads[part][
                    rows, :
                ].astype(F32)
        kt_ref[...] = k_ref[...].T
        products = t_ref[...].T
        inner_ref[0:1, :] = jnp.sum(products[0:HEAD_DIM], axis=0, keepdims=True)
        inner_ref[1:2, :] = jnp.sum(products[HEAD_DIM:], axis=0, keepdims=True)
        dk_ref[...] = jnp.zeros_like(dk_ref)
        dv_ref[...] = jnp.zeros_like(dv_ref)

    scale = log2_e / HEAD_DIM**0.5
    base = pl.multiple_of(half * HEAD_DIM, HEAD_DIM)
    for q0, qn in tiles(slots, query_tile):
        keep = lane_half((qn, 128), half)
        query = q_ref[q0 : q0 + qn, :]
        query = jnp.where(keep, query, jnp.zeros_like(query))
        grad = g_ref[q0 : q0 + qn, :]
        grad = jnp.where(keep, grad, jnp.zeros_like(grad))
        lse = lse_ref[0, :, q0 : q0 + qn]
        inner = jnp.where(
            half == 0, inner_ref[0:1, q0 : q0 + qn], inner_ref[1:2, q0 : q0 + qn]
        )
        dq_t = jnp.zeros((HEAD_DIM, qn), F32)
        for k0, kn in tiles(q0 + qn, key_tile):
            scores = mask_tile(nt(k_ref[k0 : k0 + kn, :], query), k0, q0, length)
            probs = jnp.exp2(scores * scale - lse)
            dv_ref[k0 : k0 + kn, :] += nn(probs.astype(B16), grad)
            probs_grad = nt(v_ref[k0 : k0 + kn, :], grad)
            scores_grad = (probs * (probs_grad - inner)).astype(B16)
            dk_ref[k0 : k0 + kn, :] += nn(scores_grad, query)
            dq_t = dq_t + nn(kt_ref[pl.ds(base, HEAD_DIM), k0 : k0 + kn], scores_grad)
        dqt_ref[pl.ds(base, HEAD_DIM), q0 : q0 + qn] = dq_t

    @pl.when(half == 1)
    def _():
        factor = 1.0 / HEAD_DIM**0.5
        q_ref[...] = (dqt_ref[...].T * factor).astype(B16)
        k_ref[...] = (dk_ref[...] * factor).astype(B16)
        v_ref[...] = dv_ref[...].astype(B16)
        for part, target in enumerate(outputs):
            for piece in range(per):
                place = pl.multiple_of(meta[1 + part * per + piece], 16)
                rows, source = pl.ds(piece * chunk, chunk), pl.ds(place, chunk)
                target[rows, 0:128] = q_ref[source, :]
                target[rows, 128:256] = k_ref[source, :]
                target[rows, 256:384] = v_ref[source, :]


def attend_back(meta, projected, attended, grads, lse, chunk):
    parts = len(projected)
    rows, width = projected[0].shape
    pairs = width // 384
    slots, heads = rows * parts, 2 * pairs
    wide = pl.BlockSpec((rows, 384), lambda h, m: (0, h // 2))
    narrow = pl.BlockSpec((rows, 128), lambda h, m: (0, h // 2))
    return pl.pallas_call(
        functools.partial(attend_back_kernel, slots, chunk, parts, 256, 128),
        out_shape=[jax.ShapeDtypeStruct((rows, width), B16)] * parts,
        grid_spec=pltpu.PrefetchScalarGridSpec(
            num_scalar_prefetch=1,
            grid=(heads,),
            in_specs=[wide] * parts
            + [narrow] * (2 * parts)
            + [pl.BlockSpec((1, 1, slots), lambda h, m: (h, 0, 0))],
            out_specs=[wide] * parts,
            scratch_shapes=[pltpu.VMEM((slots, 128), B16)] * 4
            + [
                pltpu.VMEM((128, slots), B16),
                pltpu.VMEM((8, slots), F32),
                pltpu.VMEM((slots, 128), F32),
                pltpu.VMEM((slots, 128), F32),
                pltpu.VMEM((128, slots), F32),
                pltpu.VMEM((slots, 128), F32),
            ],
        ),
        compiler_params=pltpu.CompilerParams(
            dimension_semantics=("arbitrary",), vmem_limit_bytes=24 << 20
        ),
        cost_estimate=pl.CostEstimate(
            flops=heads * slots * slots * HEAD_DIM * 32,
            bytes_accessed=slots * pairs * 2560,
            transcendentals=heads * slots * slots // 2,
        ),
        name="attend_back",
    )(meta, *projected, *attended, *grads, lse)


def up_kernel(x_ref, w_ref, act_ref, slope_ref):
    hidden = nn(x_ref[...], w_ref[...])
    square = hidden * hidden
    bent = jnp.tanh(gelu_scale * hidden * (1.0 + gelu_cubic * square))
    upper = 0.5 * (1.0 + bent)
    act_ref[...] = (hidden * upper).astype(B16)
    slope = upper + (0.5 * gelu_scale) * hidden * (1.0 - bent * bent) * (
        1.0 + (3.0 * gelu_cubic) * square
    )
    slope_ref[...] = slope.astype(B16)


def up_project(x, w):
    rows, depth = x.shape
    width = w.shape[1]
    step = min(256, width)
    return pl.pallas_call(
        up_kernel,
        out_shape=[jax.ShapeDtypeStruct((rows, width), B16)] * 2,
        grid=(width // step,),
        in_specs=[
            pl.BlockSpec((rows, depth), lambda i: (0, 0)),
            pl.BlockSpec((depth, step), lambda i: (0, i)),
        ],
        out_specs=[pl.BlockSpec((rows, step), lambda i: (0, i))] * 2,
        compiler_params=pltpu.CompilerParams(vmem_limit_bytes=24 << 20),
        cost_estimate=pl.CostEstimate(
            flops=2 * rows * depth * width * 2,
            bytes_accessed=2 * (rows * depth + depth * width + 2 * rows * width),
            transcendentals=rows * width,
        ),
        name="up_project",
    )(x, w)


def outer_kernel(count, *refs):
    total = None
    for left, right in zip(refs[:count], refs[count : 2 * count]):
        term = tn(left[...], right[...])
        total = term if total is None else total + term
    refs[2 * count][...] = total.astype(B16)


def outer_sum(lefts, rights):
    count = len(lefts)
    rows, height = lefts[0].shape
    width = rights[0].shape[1]
    step = min(256, height)
    return pl.pallas_call(
        functools.partial(outer_kernel, count),
        out_shape=jax.ShapeDtypeStruct((height, width), B16),
        grid=(height // step,),
        in_specs=[pl.BlockSpec((rows, step), lambda i: (0, i))] * count
        + [pl.BlockSpec((rows, width), lambda i: (0, 0))] * count,
        out_specs=pl.BlockSpec((step, width), lambda i: (i, 0)),
        compiler_params=pltpu.CompilerParams(vmem_limit_bytes=32 << 20),
        cost_estimate=pl.CostEstimate(
            flops=2 * count * rows * height * width * 2,
            bytes_accessed=2 * (count * rows * (height + width) + height * width),
            transcendentals=0,
        ),
        name="outer_sum",
    )(*lefts, *rights)


def place_kernel(order, *refs):
    pieces, out_ref = refs[:-1], refs[-1]
    which = order[pl.program_id(0)]
    for index, piece in enumerate(pieces):

        @pl.when(which == index)
        def _(piece=piece):
            out_ref[...] = piece[...].astype(F32)


def place(order, pieces):
    count = len(pieces)
    rows, width = pieces[0].shape
    return pl.pallas_call(
        place_kernel,
        out_shape=jax.ShapeDtypeStruct((count * rows, width), F32),
        grid_spec=pltpu.PrefetchScalarGridSpec(
            num_scalar_prefetch=1,
            grid=(count,),
            in_specs=[pl.BlockSpec((rows, width), lambda i, o: (0, 0))] * count,
            out_specs=pl.BlockSpec((rows, width), lambda i, o: (i, 0)),
        ),
        compiler_params=pltpu.CompilerParams(vmem_limit_bytes=32 << 20),
        cost_estimate=pl.CostEstimate(
            flops=0, bytes_accessed=count * rows * width * 6, transcendentals=0
        ),
        name="place",
    )(order, *pieces)


def shift_dp(value, shift, size):
    return lax.ppermute(value, "dp", [(d, (d + shift) % size) for d in range(size)])


def block(value, index, rows):
    return lax.dynamic_slice_in_dim(value, index * rows, rows, axis=0)


def sum_over_dp(partial):
    size = lax.axis_size("dp")
    if size != 8:
        return lax.psum(partial, "dp").astype(F32)
    d = lax.axis_index("dp")
    z, x = d // 2, d % 2
    rows = partial.shape[0] // 8
    swap = [(i, i ^ 1) for i in range(8)]
    sent = block(partial, 1 - x, 4 * rows)
    got = lax.ppermute(sent, "dp", swap)
    mine = (block(partial, x, 4 * rows).astype(F32) + got.astype(F32)).astype(B16)
    total = block(mine, z, rows).astype(F32)
    for s in (1, 2, 3):
        total = total + shift_dp(block(mine, (z + s) % 4, rows), 2 * s, 8).astype(F32)
    total = total.astype(B16)
    quarter = [total] + [shift_dp(total, 2 * s, 8) for s in (1, 2, 3)]
    other = [lax.ppermute(piece, "dp", swap) for piece in quarter]
    slot = jnp.arange(8, dtype=jnp.int32)
    order = (z - slot % 4) % 4 + 4 * (slot // 4 != x).astype(jnp.int32)
    return place(order, quarter + other)


def sum_over_all(values):
    t_size, d_size = lax.axis_size("tensor"), lax.axis_size("dp")
    if t_size & (t_size - 1) or d_size & (d_size - 1):
        return lax.psum(values, ("dp", "tensor"))
    for axis, size in (("tensor", t_size), ("dp", d_size)):
        step = 1
        while step < size:
            values = values + lax.ppermute(
                values, axis, [(i, i ^ step) for i in range(size)]
            )
            step *= 2
    return values


class Tensor:
    def __init__(self, share):
        self.share = share
        self.size = lax.axis_size("tensor")
        self.split = self.size == 4 and share % 16 == 0
        t = lax.axis_index("tensor")
        if self.split:
            self.order = jnp.stack([t, t ^ 1, t ^ 2, t ^ 3]) * share
            self.chunk = share
        else:
            self.order = jnp.zeros((1,), jnp.int32)
            self.chunk = share * self.size

    def core(self, value):
        return lax.ppermute(value, "tensor", [(0, 1), (1, 0), (2, 3), (3, 2)])

    def chip(self, value):
        return lax.ppermute(value, "tensor", [(0, 2), (2, 0), (1, 3), (3, 1)])

    def gather(self, own):
        if not self.split:
            return [lax.all_gather(own, "tensor", axis=0, tiled=True)]
        far = self.chip(own)
        near = jnp.concatenate([own, self.core(own)], axis=0)
        return [near, jnp.concatenate([far, self.core(far)], axis=0)]

    def reduce(self, terms):
        if not self.split:
            return lax.psum_scatter(
                terms[0](), "tensor", scatter_dimension=0, tiled=True
            )
        share = self.share
        far = terms[1]()
        far_sum = far[:share] + self.core(far[share:].astype(B16)).astype(F32)
        arriving = self.chip(far_sum.astype(B16))
        near = terms[0]()
        near_sum = near[:share] + self.core(near[share:].astype(B16)).astype(F32)
        return near_sum + arriving.astype(F32)


def normalize(values):
    center = values - jnp.mean(values, axis=-1, keepdims=True)
    inverse = lax.rsqrt(jnp.mean(center * center, axis=-1, keepdims=True) + epsilon)
    return center * inverse, inverse


def normalize_back(grad, gain, vhat, inverse):
    scaled = grad * gain
    mean_scaled = jnp.mean(scaled, axis=-1, keepdims=True)
    mean_product = jnp.mean(scaled * vhat, axis=-1, keepdims=True)
    values_grad = (scaled - mean_scaled - vhat * mean_product) * inverse
    return values_grad, jnp.sum(grad * vhat, axis=0), jnp.sum(grad, axis=0)


def per_device(tokens, cotangent, lengths, groups, w_qkv, w_out, w_up, w_down, gains, biases):
    row_count, share, width = tokens.shape
    cols = w_qkv.shape[2]
    pairs = cols // 128
    tensor = Tensor(share)
    t = lax.axis_index("tensor")
    positions = t * share + jnp.arange(share, dtype=jnp.int32)
    w_qkv = w_qkv.reshape(width, 3, pairs, 128).transpose(0, 2, 1, 3)
    w_qkv = w_qkv.reshape(width, 3 * cols)
    rows = range(row_count)

    def product(weight):
        return lambda part: nn(part, weight)

    def product_back(weight):
        return lambda part: nt(part, weight)

    def reduce(parts, function):
        return tensor.reduce([functools.partial(function, part) for part in parts])

    x, valid, meta = [], [], []
    for r in rows:
        x.append(tokens[r].astype(F32))
        valid.append((positions < lengths[r]).astype(F32)[:, None])
        meta.append(jnp.concatenate([lengths[r][None], tensor.order]).astype(jnp.int32))

    xhat, xinv, attn_in, projected, attended, lse = [], [], [], [], [], []
    for r in rows:
        hat, inv = normalize(x[r])
        xhat.append(hat)
        xinv.append(inv)
        attn_in.append(tensor.gather((hat * gains[0] + biases[0]).astype(B16)))
    for r in rows:
        projected.append([nn(part, w_qkv).astype(B16) for part in attn_in[r]])
        *parts, row_lse = attend(meta[r], projected[r], tensor.chunk)
        attended.append(parts)
        lse.append(row_lse)
    middle, ahat, ainv, mhat, minv, ffn_in = [], [], [], [], [], []
    squares = [[] for _ in rows]
    for r in rows:
        attn_sum = reduce(attended[r], product(w_out))
        hat, inv = normalize(attn_sum)
        ahat.append(hat)
        ainv.append(inv)
        branch = hat * gains[1] + biases[1]
        squares[r].append(jnp.sum(branch * branch * valid[r]))
        middle.append(x[r] + branch)
        hat, inv = normalize(middle[r])
        mhat.append(hat)
        minv.append(inv)
        ffn_in.append(tensor.gather((hat * gains[2] + biases[2]).astype(B16)))
    activated, slope, fhat, finv, output = [], [], [], [], []
    for r in rows:
        pieces = [up_project(part, w_up) for part in ffn_in[r]]
        activated.append([piece[0] for piece in pieces])
        slope.append([piece[1] for piece in pieces])
        ffn_sum = reduce(activated[r], product(w_down))
        hat, inv = normalize(ffn_sum)
        fhat.append(hat)
        finv.append(inv)
        branch = hat * gains[3] + biases[3]
        result = middle[r] + branch
        output.append(result.astype(B16))
        squares[r].append(jnp.sum(branch * branch * valid[r]))
        squares[r].insert(0, jnp.sum(result * result * valid[r]))

    gain_grads = [[0.0] * 4 for _ in rows]
    bias_grads = [[0.0] * 4 for _ in rows]
    out_grad, ffn_grad, hidden_grad, middle_grad, attn_grad = [], [], [], [], []
    for r in rows:
        out_grad.append(cotangent[r].astype(F32) * valid[r])
        grad, gain_grads[r][3], bias_grads[r][3] = normalize_back(
            out_grad[r], gains[3], fhat[r], finv[r]
        )
        ffn_grad.append(tensor.gather(grad.astype(B16)))
    grad_down = outer_sum(sum(activated, []), sum(ffn_grad, []))
    for r in rows:
        hidden_grad.append(
            [
                (nt(part, w_down) * bend.astype(F32)).astype(B16)
                for part, bend in zip(ffn_grad[r], slope[r])
            ]
        )
        ffn_in_grad = reduce(hidden_grad[r], product_back(w_up))
        grad, gain_grads[r][2], bias_grads[r][2] = normalize_back(
            ffn_in_grad, gains[2], mhat[r], minv[r]
        )
        middle_grad.append(out_grad[r] + grad)
        grad, gain_grads[r][1], bias_grads[r][1] = normalize_back(
            middle_grad[r], gains[1], ahat[r], ainv[r]
        )
        attn_grad.append(tensor.gather(grad.astype(B16)))
    grad_up = outer_sum(sum(ffn_in, []), sum(hidden_grad, []))
    grad_down = sum_over_dp(grad_down)
    grad_up = sum_over_dp(grad_up)
    grad_out = outer_sum(sum(attended, []), sum(attn_grad, []))
    projected_grad, input_grad = [], []
    for r in rows:
        grads = [nt(part, w_out).astype(B16) for part in attn_grad[r]]
        projected_grad.append(
            list(attend_back(meta[r], projected[r], attended[r], grads, lse[r], tensor.chunk))
        )
        attn_in_grad = reduce(projected_grad[r], product_back(w_qkv))
        grad, gain_grads[r][0], bias_grads[r][0] = normalize_back(
            attn_in_grad, gains[0], xhat[r], xinv[r]
        )
        input_grad.append((middle_grad[r] + grad).astype(B16))
    grad_qkv = outer_sum(sum(attn_in, []), sum(projected_grad, []))
    grad_out = sum_over_dp(grad_out)
    grad_qkv = sum_over_dp(grad_qkv)
    grad_qkv = grad_qkv.reshape(width, pairs, 3, 128).transpose(0, 2, 1, 3)
    grad_qkv = grad_qkv.reshape(width, 3, cols)

    member = (groups[:, None] == jnp.arange(GROUPS, dtype=jnp.int32)[None, :]).astype(F32)
    sums = jnp.stack([jnp.stack(row) for row in squares])
    counts = jnp.stack([jnp.sum(v) for v in valid])
    sums = jnp.concatenate([sums, counts[:, None]], axis=1)
    sums = jnp.sum(member[:, :, None] * sums[:, None, :], axis=0).reshape(1, GROUPS * 4)
    sums = jnp.pad(sums, ((0, 0), (0, width - GROUPS * 4)))
    small = jnp.stack(
        [sum(gain_grads[r][n] for r in rows) for n in range(4)]
        + [sum(bias_grads[r][n] for r in rows) for n in range(4)]
    )
    small = sum_over_all(jnp.concatenate([small, sums], axis=0))
    sums = small[8, : GROUPS * 4].reshape(GROUPS, 4)
    group_rms = jnp.sqrt(sums[:, :3] / (sums[:, 3:] * width))
    return (
        jnp.stack(output),
        jnp.stack(input_grad),
        grad_qkv,
        grad_out,
        grad_up,
        grad_down,
        small[:4],
        small[4:8],
        group_rms,
    )


def solution(mesh):
    placed = (
        P("dp", "tensor", None),
        P("dp", "tensor", None),
        P("dp"),
        P("dp"),
        P(None, None, "tensor"),
        P("tensor", None),
        P(None, "tensor"),
        P("tensor", None),
        P(),
        P(),
    )
    return jax.shard_map(
        per_device,
        mesh=mesh,
        in_specs=placed,
        out_specs=(
            P("dp", "tensor", None),
            P("dp", "tensor", None),
            P(None, None, "tensor"),
            P("tensor", None),
            P(None, "tensor"),
            P("tensor", None),
            P(),
            P(),
            P(),
        ),
        check_vma=False,
    )
```

```python
import functools

import jax
import jax.numpy as jnp
from jax import lax
from jax.experimental import pallas as pl
from jax.experimental.pallas import tpu as pltpu
from jax.sharding import PartitionSpec as P

HEAD_DIM = 64
GROUPS = 4
MIN_LENGTH = 544
F32 = jnp.float32
B16 = jnp.bfloat16

epsilon = 1e-05
negative_fill = -1e30
log2_e = 1.4426950408889634
gelu_scale = 0.7978845608028654
gelu_cubic = 0.044715

BASE, TENSOR, Z, X, LENGTH = 0, 1, 2, 3, 4


def nt(left, right):
    return lax.dot_general(
        left, right, (((1,), (1,)), ((), ())), preferred_element_type=F32
    )


def nn(left, right):
    return lax.dot_general(
        left, right, (((1,), (0,)), ((), ())), preferred_element_type=F32
    )


def tn(left, right):
    return lax.dot_general(
        left, right, (((0,), (0,)), ((), ())), preferred_element_type=F32
    )


def tiles(extent, size):
    return [(start, min(size, extent - start)) for start in range(0, extent, size)]


def whole(shape):
    return pl.BlockSpec(shape, lambda *_: (0,) * len(shape))


def once(shape):
    return pl.BlockSpec(
        shape, lambda *_: (0,) * len(shape), pipeline_mode=pl.Buffered(buffer_count=1)
    )


def anywhere():
    return pl.BlockSpec(memory_space=pl.ANY)


def call(kernel, name, scalars, inputs, outs, in_specs=None, out_specs=None, grid=(1,), scratch=(), limit=20, flops=0, aliases={}):
    values = sum(v.size for v in inputs)
    in_specs = in_specs or [once(v.shape) for v in inputs]
    out_specs = out_specs or [whole(shape) for shape, _ in outs]
    return list(
        pl.pallas_call(
            kernel,
            out_shape=[jax.ShapeDtypeStruct(shape, dtype) for shape, dtype in outs],
            grid_spec=pltpu.PrefetchScalarGridSpec(
                num_scalar_prefetch=1,
                grid=grid,
                in_specs=in_specs,
                out_specs=out_specs,
                scratch_shapes=list(scratch),
            ),
            input_output_aliases=aliases,
            compiler_params=pltpu.CompilerParams(
                dimension_semantics=("arbitrary",) * len(grid), vmem_limit_bytes=limit << 20
            ),
            cost_estimate=pl.CostEstimate(
                flops=flops // 16, bytes_accessed=values // 16, transcendentals=0
            ),
            name=name,
        )(scalars, *inputs)
    )


def lane_half(shape, half):
    return (lax.broadcasted_iota(jnp.int32, shape, 1) // HEAD_DIM) == half


def mask_tile(scores, query_start, length):
    key_index = lax.broadcasted_iota(jnp.int32, scores.shape, 0)
    query_index = query_start + lax.broadcasted_iota(jnp.int32, scores.shape, 1)
    allowed = key_index <= query_index
    if scores.shape[0] > MIN_LENGTH:
        allowed = allowed & (key_index < length)
    return jnp.where(allowed, scores, negative_fill)


def place_of(scalars, parts, number, chunk):
    if parts == 1:
        return 0
    return pl.multiple_of(lax.bitwise_xor(scalars[TENSOR], number) * chunk, 16)


def halves_of(refs, number, chunk):
    return refs[number % len(refs)].at[pl.ds(number // len(refs) * chunk, chunk), :]


def attend_kernel(row, chunk, parts, query_tile, scalars, *refs):
    queries, keys, values = (refs[i * parts : (i + 1) * parts] for i in range(3))
    count = 1 if parts == 1 else 2
    outputs = refs[3 * parts : 3 * parts + count]
    lse_ref, q_ref, k_ref, v_ref, vt_ref, ot_ref = refs[3 * parts + count :]
    slots = q_ref.shape[0]
    length = scalars[LENGTH + row]
    for number in range(parts):
        target = pl.ds(place_of(scalars, parts, number, chunk), chunk)
        q_ref[target, :] = queries[number][...]
        k_ref[target, :] = keys[number][...]
        v_ref[target, :] = values[number][...]
    vt_ref[...] = v_ref[...].T
    scale = log2_e / HEAD_DIM**0.5
    for q0, qn in tiles(slots, query_tile):
        extent = q0 + qn
        for half in (0, 1):
            query = q_ref[q0 : q0 + qn, :]
            query = jnp.where(lane_half(query.shape, half), query, jnp.zeros_like(query))
            scores = mask_tile(nt(k_ref[0:extent, :], query), q0, length)
            top = jnp.max(scores, axis=0, keepdims=True)
            weights = jnp.exp2((scores - top) * scale)
            total = jnp.sum(weights, axis=0, keepdims=True)
            lanes = slice(half * HEAD_DIM, half * HEAD_DIM + HEAD_DIM)
            out_t = nn(vt_ref[lanes, 0:extent], weights.astype(B16))
            ot_ref[lanes, q0 : q0 + qn] = out_t * (1.0 / total)
            lse_ref[half, :, q0 : q0 + qn] = top * scale + jnp.log2(total)
    q_ref[...] = ot_ref[...].T.astype(B16)
    for number in range(parts):
        source = pl.ds(place_of(scalars, parts, number, chunk), chunk)
        halves_of(outputs, number, chunk)[...] = q_ref[source, :]


def column(rows, position):
    return pl.BlockSpec((rows, 128), position)


def attend(scalars, row, projected):
    parts = len(projected)
    chunk, width = projected[0].shape
    pairs = width // 384
    slots = chunk * parts
    count = 1 if parts == 1 else 2
    columns = []
    for kind in range(3):
        spot = column(chunk, lambda p, s, kind=kind: (0, kind * pairs + p))
        columns += [spot] * parts
    return call(
        functools.partial(attend_kernel, row, chunk, parts, 512),
        "attend",
        scalars,
        [*projected, *projected, *projected],
        [((slots // count, pairs * 128), B16)] * count + [((2 * pairs, 1, slots), F32)],
        columns,
        [column(slots // count, lambda p, s: (0, p))] * count
        + [pl.BlockSpec((2, 1, slots), lambda p, s: (p, 0, 0))],
        (pairs,),
        [pltpu.VMEM((slots, 128), B16)] * 3
        + [pltpu.VMEM((128, slots), B16), pltpu.VMEM((128, slots), F32)],
        limit=24,
        flops=4 * slots * slots * 128 * pairs,
    )


def attend_back_kernel(row, chunk, parts, query_tile, scalars, *refs):
    queries, keys, values = (refs[i * parts : (i + 1) * parts] for i in range(3))
    count = 1 if parts == 1 else 2
    refs = refs[3 * parts :]
    attended, grads, lse_ref = refs[:count], refs[count : 2 * count], refs[2 * count]
    outputs = refs[2 * count + 1 : 3 * count + 1]
    q_ref, k_ref, v_ref, g_ref, kt_ref, inner_ref, dk_ref, dv_ref, dqt_ref, t_ref = refs[
        3 * count + 1 :
    ]
    slots = q_ref.shape[0]
    half = pl.program_id(0)
    length = scalars[LENGTH + row]

    @pl.when(half == 0)
    def _():
        for number in range(parts):
            target = pl.ds(place_of(scalars, parts, number, chunk), chunk)
            grad = halves_of(grads, number, chunk)[...]
            out = halves_of(attended, number, chunk)[...]
            q_ref[target, :] = queries[number][...]
            k_ref[target, :] = keys[number][...]
            v_ref[target, :] = values[number][...]
            g_ref[target, :] = grad
            t_ref[target, :] = out.astype(F32) * grad.astype(F32)
        kt_ref[...] = k_ref[...].T
        products = t_ref[...].T
        inner_ref[0:1, :] = jnp.sum(products[0:HEAD_DIM], axis=0, keepdims=True)
        inner_ref[1:2, :] = jnp.sum(products[HEAD_DIM:], axis=0, keepdims=True)
        dk_ref[...] = jnp.zeros_like(dk_ref)
        dv_ref[...] = jnp.zeros_like(dv_ref)

    scale = log2_e / HEAD_DIM**0.5
    base = pl.multiple_of(half * HEAD_DIM, HEAD_DIM)
    for q0, qn in tiles(slots, query_tile):
        extent = q0 + qn
        keep = lane_half((qn, 128), half)
        query = q_ref[q0 : q0 + qn, :]
        query = jnp.where(keep, query, jnp.zeros_like(query))
        grad = g_ref[q0 : q0 + qn, :]
        grad = jnp.where(keep, grad, jnp.zeros_like(grad))
        lse = lse_ref[0, :, q0 : q0 + qn]
        inner = jnp.where(
            half == 0, inner_ref[0:1, q0 : q0 + qn], inner_ref[1:2, q0 : q0 + qn]
        )
        scores = mask_tile(nt(k_ref[0:extent, :], query), q0, length)
        probs = jnp.exp2(scores * scale - lse)
        dv_ref[0:extent, :] += nn(probs.astype(B16), grad)
        probs_grad = nt(v_ref[0:extent, :], grad)
        scores_grad = (probs * (probs_grad - inner)).astype(B16)
        dk_ref[0:extent, :] += nn(scores_grad, query)
        dqt_ref[pl.ds(base, HEAD_DIM), q0 : q0 + qn] = nn(
            kt_ref[pl.ds(base, HEAD_DIM), 0:extent], scores_grad
        )

    @pl.when(half == 1)
    def _():
        factor = 1.0 / HEAD_DIM**0.5
        q_ref[...] = (dqt_ref[...].T * factor).astype(B16)
        k_ref[...] = (dk_ref[...] * factor).astype(B16)
        v_ref[...] = dv_ref[...].astype(B16)
        for number in range(parts):
            source = pl.ds(place_of(scalars, parts, number, chunk), chunk)
            target = halves_of(outputs, number, chunk)
            target[:, 0:128] = q_ref[source, :]
            target[:, 128:256] = k_ref[source, :]
            target[:, 256:384] = v_ref[source, :]


def attend_back(scalars, row, projected, attended, grads, lse, pair):
    parts = len(projected)
    chunk, width = projected[0].shape
    pairs = width // 384
    slots = chunk * parts
    count = len(attended)
    rows = slots // count
    columns = []
    for kind in range(3):
        columns += [column(chunk, lambda h, s, kind=kind: (0, kind * pairs + pair))] * parts
    columns += [column(rows, lambda h, s: (0, pair))] * (2 * count)
    columns += [pl.BlockSpec((1, 1, slots), lambda h, s: (2 * pair + h, 0, 0))]
    return call(
        functools.partial(attend_back_kernel, row, chunk, parts, 384),
        "attend_back",
        scalars,
        [*projected, *projected, *projected, *attended, *grads, lse],
        [((rows, 384), B16)] * count,
        columns,
        [whole((rows, 384))] * count,
        (2,),
        [pltpu.VMEM((slots, 128), B16)] * 4
        + [pltpu.VMEM((128, slots), B16), pltpu.VMEM((8, slots), F32)]
        + [pltpu.VMEM((slots, 128), F32)] * 2
        + [pltpu.VMEM((128, slots), F32), pltpu.VMEM((slots, 128), F32)],
        limit=24,
        flops=10 * slots * slots * 128,
    )


def sum_of(terms):
    total = terms[0]
    for term in terms[1:]:
        total = total + term
    return total


def project_kernel(count, scalars, x_ref, *refs):
    for w_ref, out_ref in zip(refs[:count], refs[count:]):
        cols = w_ref.shape[2]
        for kind in range(3):
            columns = slice(kind * cols, kind * cols + cols)
            out_ref[:, columns] = nn(x_ref[...], w_ref[kind]).astype(B16)


def project(scalars, x, ws):
    rows, depth = x.shape
    cols = ws[0].shape[2]
    return call(
        functools.partial(project_kernel, len(ws)),
        "project",
        scalars,
        [x, *ws],
        [((rows, 3 * cols), B16)] * len(ws),
        flops=6 * rows * depth * cols * len(ws),
    )


def out_kernel(count, scalars, *refs):
    xs, ws, outs = refs[:count], refs[count : 2 * count], refs[2 * count :]
    n = outs[0].shape[0]
    for index, out in enumerate(outs):
        rows = slice(index * n, index * n + n)
        total = sum_of([nn(x[rows, :], w[...]) for x, w in zip(xs, ws)])
        out[...] = total.astype(out.dtype)


def partial_shapes(share, width, split):
    return [((share, width), F32)] + ([((share, width), B16)] if split else [])


def out_project(scalars, xs, ws):
    split = len(ws) == 2
    rows, depth = xs[0].shape
    width = ws[0].shape[1]
    return call(
        functools.partial(out_kernel, len(ws)),
        "out_project",
        scalars,
        [*xs, *ws],
        partial_shapes(rows // len(ws), width, split),
        flops=2 * rows * depth * width * len(ws),
    )


def feed_kernel(count, scalars, x_ref, *refs):
    ups, downs, refs = refs[:count], refs[count : 2 * count], refs[2 * count :]
    acts, slopes, out_ref = refs[:count], refs[count : 2 * count], refs[2 * count]
    for start, size in tiles(x_ref.shape[0], 272):
        rows = slice(start, start + size)
        terms = []
        for up, down, act_ref, slope_ref in zip(ups, downs, acts, slopes):
            hidden = nn(x_ref[rows, :], up[...])
            square = hidden * hidden
            bent = jnp.tanh(hidden * (gelu_scale + (gelu_scale * gelu_cubic) * square))
            upper = 0.5 + 0.5 * bent
            act = (hidden * upper).astype(B16)
            act_ref[rows, :] = act
            slope = upper + hidden * (1.0 - bent * bent) * (
                0.5 * gelu_scale + (1.5 * gelu_scale * gelu_cubic) * square
            )
            slope_ref[rows, :] = slope.astype(B16)
            terms.append(nn(act, down[...]))
        out_ref[rows, :] = sum_of(terms).astype(out_ref.dtype)


def feed(scalars, x, ups, downs, dtype):
    rows, depth = x.shape
    units, width = downs[0].shape
    count = len(ups)
    out = call(
        functools.partial(feed_kernel, count),
        "feed",
        scalars,
        [x, *ups, *downs],
        [((rows, units), B16)] * (2 * count) + [((rows, width), dtype)],
        limit=28,
        flops=4 * rows * depth * units * count,
    )
    return out[:count], out[count : 2 * count], out[2 * count]


def feed_back_kernel(count, scalars, x_ref, *refs):
    slopes, ups, downs = (refs[i * count : (i + 1) * count] for i in range(3))
    grads, out_ref = refs[3 * count : 4 * count], refs[4 * count]
    for start, size in tiles(x_ref.shape[0], 272):
        rows = slice(start, start + size)
        terms = []
        for slope, up, down, grad_ref in zip(slopes, ups, downs, grads):
            grad = nt(x_ref[rows, :], down[...]) * slope[rows, :].astype(F32)
            grad = grad.astype(B16)
            grad_ref[rows, :] = grad
            terms.append(nt(grad, up[...]))
        out_ref[rows, :] = sum_of(terms).astype(out_ref.dtype)


def feed_back(scalars, x, slopes, ups, downs, dtype):
    rows, width = x.shape
    depth, units = ups[0].shape
    count = len(ups)
    out = call(
        functools.partial(feed_back_kernel, count),
        "feed_back",
        scalars,
        [x, *slopes, *ups, *downs],
        [((rows, units), B16)] * count + [((rows, depth), dtype)],
        limit=28,
        flops=4 * rows * depth * units * count,
    )
    return out[:count], out[count]


def out_back_kernel(count, scalars, *refs):
    xs, ws, outs = refs[: len(refs) - 2 * count], refs[-2 * count : -count], refs[-count:]
    for w_ref, out_ref in zip(ws, outs):
        for index, x in enumerate(xs):
            n = x.shape[0]
            out_ref[index * n : index * n + n, :] = nt(x[...], w_ref[...]).astype(B16)


def out_back(scalars, xs, ws):
    rows, depth = len(xs) * xs[0].shape[0], xs[0].shape[1]
    cols = ws[0].shape[0]
    return call(
        functools.partial(out_back_kernel, len(ws)),
        "out_back",
        scalars,
        [*xs, *ws],
        [((rows, cols), B16)] * len(ws),
        flops=2 * rows * depth * cols * len(ws),
    )


def project_back_kernel(pairs, count, scalars, *refs):
    sides = [refs[i * pairs : (i + 1) * pairs] for i in range(count)]
    ws, outs = refs[pairs * count : (pairs + 1) * count], refs[(pairs + 1) * count :]
    n = outs[0].shape[0]
    for index, out in enumerate(outs):
        terms = []
        for grads, w_ref in zip(sides, ws):
            for kind in range(3):
                columns = [
                    grad[index * n : index * n + n, kind * 128 : kind * 128 + 128]
                    for grad in grads
                ]
                left = columns[0] if pairs == 1 else jnp.concatenate(columns, axis=1)
                terms.append(nt(left, w_ref[kind]))
        out[...] = sum_of(terms).astype(out.dtype)


def project_back(scalars, sides, ws):
    split = len(ws) == 2
    rows = sides[0][0].shape[0]
    depth, cols = ws[0].shape[1:]
    return call(
        functools.partial(project_back_kernel, len(sides[0]), len(ws)),
        "project_back",
        scalars,
        [v for side in sides for v in side] + list(ws),
        partial_shapes(rows // len(ws), depth, split),
        limit=24,
        flops=6 * rows * depth * cols * len(ws),
    )


def block_of(scalars, index, staged):
    if not staged:
        return index
    z = lax.rem(scalars[Z] + lax.rem(index, 4), 4)
    x = jnp.where(index < 4, scalars[X], 1 - scalars[X])
    return 4 * x + z


def outer_kernel(counts, staged, scalars, *refs):
    products = []
    for left_count, right_count in counts:
        products.append((refs[:left_count], refs[left_count : left_count + right_count]))
        refs = refs[left_count + right_count :]
    outs, refs = refs[: 2 if staged else 1], refs[2 if staged else 1 :]
    buffers = [(refs[2 * i], refs[2 * i + 1]) for i in range(len(products))]
    sems = refs[2 * len(products)]
    step = pl.program_id(0)

    @pl.when(step == 0)
    def _():
        copies = []
        for sources, targets in zip(products, buffers):
            for pieces, target in zip(sources, targets):
                start = 0
                for piece in pieces:
                    rows = piece.shape[0]
                    copies.append(
                        pltpu.make_async_copy(
                            piece, target.at[pl.ds(start, rows), :], sems.at[len(copies)]
                        )
                    )
                    start += rows
        for copy in copies:
            copy.start()
        for copy in copies:
            copy.wait()

    first = 0
    for left_ref, right_ref in buffers:
        if staged:
            spots = [block_of(scalars, 2 * step + i, True) for i in (0, 1)]
            columns = [pl.ds(pl.multiple_of(spot * 128, 128), 128) for spot in spots]
            left = jnp.concatenate([left_ref[:, c] for c in columns], axis=1)
        else:
            left = left_ref[:, pl.ds(pl.multiple_of(step * 256, 256), 256)]
        value = tn(left, right_ref[...]).astype(B16)
        lanes = slice(first, first + value.shape[1])
        if staged:

            @pl.when(step < 2)
            def _(value=value, lanes=lanes):
                outs[0][:, lanes] = value

            @pl.when(step >= 2)
            def _(value=value, lanes=lanes):
                outs[1][:, lanes] = value

        else:
            outs[0][:, lanes] = value
        first += value.shape[1]


def outer_sum(scalars, products, staged):
    inputs, counts, scratch = [], [], []
    height, width = products[0][0][0].shape[1], 0
    flops = 0
    for lefts, rights in products:
        slots = sum(left.shape[0] for left in lefts)
        inputs += [*lefts, *rights]
        counts.append((len(lefts), len(rights)))
        scratch += [pltpu.VMEM((slots, height), B16)]
        scratch += [pltpu.VMEM((slots, rights[0].shape[1]), B16)]
        width += rights[0].shape[1]
        flops += 2 * slots * height * rights[0].shape[1]
    if staged:
        outs = [((height // 2, width), B16)] * 2
        specs = [
            pl.BlockSpec((256, width), lambda i, s: (jnp.minimum(i, 1), 0)),
            pl.BlockSpec((256, width), lambda i, s: (jnp.maximum(i - 2, 0), 0)),
        ]
    else:
        outs = [((height, width), B16)]
        specs = [pl.BlockSpec((256, width), lambda i, s: (i, 0))]
    return call(
        functools.partial(outer_kernel, counts, staged),
        "outer_sum",
        scalars,
        inputs,
        outs,
        [anywhere() for _ in inputs],
        specs,
        (height // 256,),
        scratch + [pltpu.SemaphoreType.DMA((len(inputs),))],
        limit=24,
        flops=flops,
    )


def quarter_kernel(scalars, keep_ref, got_ref, *outs):
    rows = outs[0].shape[0]
    for index, out in enumerate(outs):
        at = slice(index * rows, index * rows + rows)
        out[...] = (keep_ref[at, :].astype(F32) + got_ref[at, :].astype(F32)).astype(B16)


def place_blocks(scalars, quarter, other):
    rows = quarter[0].shape[0]
    result = []
    for half in (0, 1):
        x = scalars[X] if half == 0 else 1 - scalars[X]
        for index in range(4):
            z = lax.rem(scalars[Z] + 4 - index, 4)
            at = slice(index * rows, index * rows + rows)
            value = quarter[index][...] if half == 0 else other[at, :]
            result.append((value, 4 * x + z))
    return result


def place_kernel(scalars, *refs):
    quarter, other, out_ref, buffer, sems = refs[:4], refs[4], refs[5], refs[6], refs[7]
    rows = quarter[0].shape[0]
    copies = []
    for index, (value, spot) in enumerate(place_blocks(scalars, quarter, other)):
        buffer[index] = value.astype(F32)
        target = out_ref.at[pl.ds(pl.multiple_of(spot * rows, rows), rows), :]
        copy = pltpu.make_async_copy(buffer.at[index], target, sems.at[index])
        copy.start()
        copies.append(copy)
    for copy in copies:
        copy.wait()


def place(scalars, quarter, other):
    rows, width = quarter[0].shape
    (out,) = call(
        place_kernel,
        "place",
        scalars,
        [*quarter, other],
        [((8 * rows, width), F32)],
        out_specs=[anywhere()],
        scratch=[pltpu.VMEM((8, rows, width), F32), pltpu.SemaphoreType.DMA((8,))],
    )
    return out


def place_heads_kernel(pair, has_out, aliased, scalars, *refs):
    quarter, other = refs[:4], refs[4]
    refs = refs[5 + aliased :]
    qkv_ref, refs = refs[0], refs[1:]
    if has_out:
        out_ref, buffer, turned, sems = refs
    else:
        buffer, sems = refs
    rows = quarter[0].shape[0]
    copies = []
    for index, (value, spot) in enumerate(place_blocks(scalars, quarter, other)):
        at = pl.ds(pl.multiple_of(spot * rows, rows), rows)
        for kind in range(3):
            buffer[kind, index] = value[:, kind * 128 : kind * 128 + 128].astype(F32)
            copies.append(
                pltpu.make_async_copy(
                    buffer.at[kind, index],
                    qkv_ref.at[kind, at, pl.ds(pair * 128, 128)],
                    sems.at[len(copies)],
                )
            )
            copies[-1].start()
        if has_out:
            turned[index] = value[:, 384:].astype(F32).T
            copies.append(
                pltpu.make_async_copy(turned.at[index], out_ref.at[:, at], sems.at[len(copies)])
            )
            copies[-1].start()
    for copy in copies:
        copy.wait()


def place_heads(scalars, quarter, other, pair, pairs, into):
    rows, width = quarter[0].shape
    has_out = width > 384
    inputs = [*quarter, other] + ([] if into is None else [into])
    in_specs = [whole(v.shape) for v in [*quarter, other]]
    in_specs += [] if into is None else [anywhere()]
    outs = [((3, 8 * rows, pairs * 128), F32)]
    scratch = [pltpu.VMEM((3, 8, rows, 128), F32)]
    if has_out:
        outs.append(((width - 384, 8 * rows), F32))
        scratch.append(pltpu.VMEM((8, width - 384, rows), F32))
    return call(
        functools.partial(place_heads_kernel, pair, has_out, int(into is not None)),
        "place_heads",
        scalars,
        inputs,
        outs,
        in_specs,
        [anywhere() for _ in outs],
        scratch=scratch + [pltpu.SemaphoreType.DMA((32,))],
        aliases={} if into is None else {6: 0},
    )


class DpSum:
    swap = [(i, i ^ 1) for i in range(8)]

    def __init__(self, scalars, order, keep, send):
        self.scalars, self.order, self.keep = scalars, order, keep
        self.got = lax.ppermute(send, "dp", self.swap)

    def shifted(self, value, steps):
        size = 8
        pairs = [(d, (d + 2 * steps) % size) for d in range(size)]
        return lax.ppermute(value, "dp", pairs)

    def scatter(self):
        (got,) = self.order.enter(self.got)
        rows, width = self.keep.shape
        self.own, *sent = call(
            quarter_kernel,
            "quarter",
            self.scalars,
            [self.keep, got],
            [((rows // 4, width), B16)] * 4,
        )
        self.order.leave(*sent)
        self.got = [self.shifted(v, s) for v, s in zip(sent, (1, 2, 3))]

    def collect(self):
        got = self.order.enter(*self.got)
        total = self.own.astype(F32)
        for piece in got:
            total = total + piece.astype(F32)
        total = total.astype(B16)
        self.order.leave(total)
        self.quarter = [total] + [self.shifted(total, s) for s in (1, 2, 3)]

    def spread(self):
        quarter = self.order.enter(*self.quarter)
        half = jnp.concatenate(quarter, axis=0)
        self.order.leave(half)
        self.other = lax.ppermute(half, "dp", self.swap)


class Order:
    def __init__(self):
        self.last = ()

    def enter(self, *values):
        return lax.optimization_barrier(tuple(values) + self.last)[: len(values)]

    def leave(self, *values):
        self.last = tuple(values)


def normalize(values):
    center = values - jnp.mean(values, axis=-1, keepdims=True)
    inverse = lax.rsqrt(jnp.mean(center * center, axis=-1, keepdims=True) + epsilon)
    return center * inverse, inverse


def values_back(grad, gain, vhat, inverse):
    scaled = grad * gain
    mean_scaled = jnp.mean(scaled, axis=-1, keepdims=True)
    mean_product = jnp.mean(scaled * vhat, axis=-1, keepdims=True)
    return (scaled - mean_scaled - vhat * mean_product) * inverse


def added(refs, rows):
    total = refs[0][rows, :].astype(F32)
    for ref in refs[1:]:
        total = total + ref[rows, :].astype(F32)
    return total


def fold(values):
    return jnp.sum(values.reshape(-1, 8, values.shape[-1]), axis=0)


def over_slots(share, width, sums, body):
    tile = 16 if share % 16 == 0 else 8
    totals = [jnp.zeros((8, width), F32)] * sums
    for start in range(0, share, tile):
        terms = body(pl.ds(start, tile), start, tile)
        totals = [total + fold(term) for total, term in zip(totals, terms)]
    return totals


def valid_rows(scalars, row, start, tile):
    slot = scalars[BASE] + start + lax.broadcasted_iota(jnp.int32, (tile, 1), 0)
    return (slot < scalars[LENGTH + row]).astype(F32)


def keep_sums(ref, totals):
    for index, total in enumerate(totals):
        ref[index : index + 1, :] = jnp.sum(total, axis=0, keepdims=True)


def first_kernel(scalars, x_ref, gains, biases, *outs):
    share, width = outs[0].shape
    for row, out in enumerate(outs):

        def body(rows, start, tile, row=row, out=out):
            vhat, _ = normalize(x_ref[row, rows, :].astype(F32))
            out[rows, :] = (vhat * gains[0:1, :] + biases[0:1, :]).astype(B16)
            return []

        over_slots(share, width, 0, body)


def middle_kernel(row, count, scalars, *refs):
    addends = refs[:count]
    x_ref, gains, biases, sum_ref, middle_ref, normed_ref, stat_ref = refs[count:]
    share, width = sum_ref.shape

    def body(rows, start, tile):
        attn_sum = added(addends, rows)
        sum_ref[rows, :] = attn_sum
        vhat, _ = normalize(attn_sum)
        branch = vhat * gains[1:2, :] + biases[1:2, :]
        middle = x_ref[0, rows, :].astype(F32) + branch
        middle_ref[rows, :] = middle
        vhat, _ = normalize(middle)
        normed_ref[rows, :] = (vhat * gains[2:3, :] + biases[2:3, :]).astype(B16)
        return [branch * branch * valid_rows(scalars, row, start, tile)]

    keep_sums(stat_ref, over_slots(share, width, 1, body))


def last_kernel(row, count, scalars, *refs):
    addends = refs[:count]
    middle_ref, cot_ref, gains, biases, out_ref, grad_ref, stat_ref = refs[count:]
    share, width = out_ref.shape

    def body(rows, start, tile):
        vhat, inverse = normalize(added(addends, rows))
        branch = vhat * gains[3:4, :] + biases[3:4, :]
        result = middle_ref[rows, :] + branch
        out_ref[rows, :] = result.astype(B16)
        valid = valid_rows(scalars, row, start, tile)
        out_grad = cot_ref[0, rows, :].astype(F32) * valid
        grad_ref[rows, :] = values_back(out_grad, gains[3:4, :], vhat, inverse).astype(B16)
        return [
            result * result * valid,
            branch * branch * valid,
            out_grad * vhat,
            out_grad,
        ]

    keep_sums(stat_ref, over_slots(share, width, 4, body))


def middle_back_kernel(row, count, scalars, *refs):
    addends = refs[:count]
    sum_ref, middle_ref, cot_ref, gains, carry_ref, grad_ref, stat_ref = refs[count:]
    share, width = sum_ref.shape

    def body(rows, start, tile):
        normed_grad = added(addends, rows)
        mhat, inverse = normalize(middle_ref[rows, :])
        out_grad = cot_ref[0, rows, :].astype(F32) * valid_rows(scalars, row, start, tile)
        carry = out_grad + values_back(normed_grad, gains[2:3, :], mhat, inverse)
        carry_ref[rows, :] = carry
        ahat, inverse = normalize(sum_ref[rows, :])
        grad_ref[rows, :] = values_back(carry, gains[1:2, :], ahat, inverse).astype(B16)
        return [normed_grad * mhat, normed_grad, carry * ahat, carry]

    keep_sums(stat_ref, over_slots(share, width, 4, body))


def first_back_kernel(row, count, scalars, *refs):
    addends = refs[:count]
    x_ref, carry_ref, gains, out_ref, stat_ref = refs[count:]
    share, width = out_ref.shape

    def body(rows, start, tile):
        grad = added(addends, rows)
        vhat, inverse = normalize(x_ref[0, rows, :].astype(F32))
        back = values_back(grad, gains[0:1, :], vhat, inverse)
        out_ref[rows, :] = (carry_ref[rows, :] + back).astype(B16)
        return [grad * vhat, grad]

    keep_sums(stat_ref, over_slots(share, width, 2, body))


def small_kernel(row_count, share, scalars, *refs):
    firsts, middles, lasts, backs = (
        refs[i * row_count : (i + 1) * row_count] for i in range(4)
    )
    out_ref = refs[4 * row_count]
    width = out_ref.shape[1]
    spots = ((firsts, 0), (backs, 2), (backs, 0), (lasts, 2))
    spots += ((firsts, 1), (backs, 3), (backs, 1), (lasts, 3))
    for index, (source, line) in enumerate(spots):
        total = source[0][line : line + 1, :]
        for ref in source[1:]:
            total = total + ref[line : line + 1, :]
        out_ref[index : index + 1, :] = total
    lane = lax.broadcasted_iota(jnp.int32, (1, width), 1)
    totals = [jnp.zeros((1, width), F32)] * GROUPS
    for row in range(row_count):
        count = jnp.clip(scalars[LENGTH + row] - scalars[BASE], 0, share).astype(F32)
        values = jnp.where(lane == 3, count, 0.0)
        sources = (lasts[row][0:1, :], middles[row][0:1, :], lasts[row][1:2, :])
        for index, source in enumerate(sources):
            values = jnp.where(lane == index, jnp.sum(source, axis=1, keepdims=True), values)
        group = scalars[LENGTH + row_count + row]
        for index in range(GROUPS):
            totals[index] = totals[index] + jnp.where(group == index, values, 0.0)
    for index, total in enumerate(totals):
        out_ref[8 + index : 9 + index, :] = total
    out_ref[12:16, :] = jnp.zeros((4, width), F32)


def swap_core(value):
    return lax.ppermute(value, "tensor", [(0, 1), (1, 0), (2, 3), (3, 2)])


def swap_chip(value):
    return lax.ppermute(value, "tensor", [(0, 2), (2, 0), (1, 3), (3, 1)])


class Row:
    def __init__(self, index, order, split, scalars, tokens, cotangent, gains, biases, pairs):
        self.index, self.order, self.split, self.scalars = index, order, split, scalars
        self.tokens, self.cotangent = tokens, cotangent
        self.gains, self.biases = gains, biases
        self.shape = tokens.shape[1:]
        self.projected, self.act, self.slope, self.hidden_grad = [], [], [], []
        self.projected_grad = [None] * pairs

    def gather(self, own):
        if self.split:
            return [own, swap_chip(own)]
        return [lax.all_gather(own, "tensor", axis=0, tiled=True)]

    def reduce(self, own, far):
        if self.split:
            return [own, swap_chip(far)]
        return [lax.psum_scatter(own, "tensor", scatter_dimension=0, tiled=True)]

    def both(self, pieces):
        return [*pieces, *[swap_core(v) for v in pieces]] if self.split else list(pieces)

    def mixed(self, pieces):
        first = [piece[0] for piece in pieces]
        return first + [swap_core(piece[1]) for piece in pieces] if self.split else first

    def over_row(self, kernel, name, inputs, outs):
        addends = self.order.enter(*self.addends)
        inputs = [*addends, *inputs]
        row = pl.BlockSpec((1, *self.shape), lambda i, s: (self.index, 0, 0))
        specs = [row if v.ndim == 3 else whole(v.shape) for v in inputs]
        return call(
            functools.partial(kernel, self.index, len(addends)),
            name,
            self.scalars,
            inputs,
            outs,
            specs,
        )

    def project(self, part, ws):
        (x,) = self.order.enter(self.attn_in[part])
        own, *other = project(self.scalars, x, ws)
        self.order.leave(own, *other)
        self.projected += [own, *[swap_core(v) for v in other]]

    def attend(self):
        projected = self.order.enter(*self.projected)
        *self.attended, self.lse = attend(self.scalars, self.index, projected)
        self.order.leave(*self.attended)
        self.heads = [self.attended[0]] + [swap_core(v) for v in self.attended[1:]]

    def out_project(self, ws):
        xs = self.order.enter(*self.heads)
        own, *far = out_project(self.scalars, xs, ws)
        self.order.leave(own, *far)
        self.addends = self.reduce(own, *(far or [None]))

    def middle(self):
        self.attn_sum, self.mid, normed, self.stat_middle = self.over_row(
            middle_kernel,
            "middle",
            [self.tokens, self.gains, self.biases],
            [(self.shape, F32)] * 2 + [(self.shape, B16), ((1, self.shape[1]), F32)],
        )
        self.order.leave(normed)
        self.ffn_in = self.gather(normed)

    def feed(self, part, ups, downs):
        (x,) = self.order.enter(self.ffn_in[part])
        act, slope, out = feed(self.scalars, x, ups, downs, B16 if part else F32)
        self.order.leave(out)
        self.act.append(act)
        self.slope.append(slope)
        if part == 0:
            self.own = out
        if part == len(self.ffn_in) - 1:
            self.addends = self.reduce(self.own, out)

    def last(self):
        self.output, grad, self.stat_last = self.over_row(
            last_kernel,
            "last",
            [self.mid, self.cotangent, self.gains, self.biases],
            [(self.shape, B16)] * 2 + [((4, self.shape[1]), F32)],
        )
        self.order.leave(grad)
        self.ffn_grad = self.gather(grad)

    def feed_back(self, part, ups, downs):
        (x,) = self.order.enter(self.ffn_grad[part])
        grad, out = feed_back(
            self.scalars, x, self.slope[part], ups, downs, B16 if part else F32
        )
        self.order.leave(out)
        self.hidden_grad.append(grad)
        if part == 0:
            self.own = out
        if part == len(self.ffn_grad) - 1:
            self.addends = self.reduce(self.own, out)

    def middle_back(self):
        self.carry, grad, self.stat_back = self.over_row(
            middle_back_kernel,
            "middle_back",
            [self.attn_sum, self.mid, self.cotangent, self.gains],
            [(self.shape, F32), (self.shape, B16), ((4, self.shape[1]), F32)],
        )
        self.order.leave(grad)
        self.attn_grad = self.gather(grad)

    def out_back(self, ws):
        xs = self.order.enter(*self.attn_grad)
        own, *other = out_back(self.scalars, xs, ws)
        self.order.leave(own, *other)
        self.attended_grad = [own] + [swap_core(v) for v in other]

    def attend_back(self, pair):
        grads = self.order.enter(*self.attended_grad)
        out = attend_back(
            self.scalars, self.index, self.projected, self.attended, grads, self.lse, pair
        )
        self.projected_grad[pair] = out
        self.order.leave(*out)

    def project_back(self, ws):
        sides = [[grad[0] for grad in self.projected_grad]]
        if self.split:
            sides.append([swap_core(grad[1]) for grad in self.projected_grad])
        flat = self.order.enter(*[v for side in sides for v in side])
        pairs = len(self.projected_grad)
        sides = [flat[i * pairs : (i + 1) * pairs] for i in range(len(sides))]
        own, *far = project_back(self.scalars, sides, ws)
        self.order.leave(own, *far)
        self.addends = self.reduce(own, *(far or [None]))

    def first_back(self):
        self.input_grad, self.stat_first = self.over_row(
            first_back_kernel,
            "first_back",
            [self.tokens, self.carry, self.gains],
            [(self.shape, B16), ((2, self.shape[1]), F32)],
        )
        self.order.leave(self.input_grad)


def doubling(values, axis, step):
    size = lax.axis_size(axis)
    return values + lax.ppermute(values, axis, [(i, i ^ step) for i in range(size)])


def per_device(tokens, cotangent, lengths, groups, w_qkv, w_out, w_up, w_down, gains, biases):
    row_count, share, width = tokens.shape
    t_size, d_size = lax.axis_size("tensor"), lax.axis_size("dp")
    pairs = w_qkv.shape[2] // 128
    split = t_size == 4 and share % 16 == 0
    staged = d_size == 8
    t, d = lax.axis_index("tensor"), lax.axis_index("dp")
    both = lambda w: [w, swap_core(w)] if split else [w]
    qkvs = [w.transpose(1, 0, 2) for w in both(w_qkv)]
    outs, ups, downs = both(w_out), both(w_up), both(w_down)
    parts = range(2 if split else 1)
    spots = jnp.stack([t * share, t, d // 2, d % 2]).astype(jnp.int32)
    scalars = jnp.concatenate([spots, lengths, groups])
    order = Order()
    rows = [
        Row(r, order, split, scalars, tokens, cotangent, gains, biases, pairs)
        for r in range(row_count)
    ]
    normed = call(
        first_kernel,
        "first",
        scalars,
        [tokens, gains, biases],
        [((share, width), B16)] * row_count,
    )
    order.leave(*normed)
    for row, own in zip(rows, normed):
        row.attn_in = row.gather(own)

    def outer(*products):
        flat = [v for lefts, rights in products for v in (*lefts, *rights)]
        values = list(order.enter(*flat))
        again = []
        for lefts, rights in products:
            taken, values = values[: len(lefts) + len(rights)], values[len(lefts) + len(rights) :]
            again.append((taken[: len(lefts)], taken[len(lefts) :]))
        return again

    def both_cores(name):
        return [v for row in rows for v in row.both(getattr(row, name))]

    def own_columns(name):
        return [v for row in rows for v in row.mixed(getattr(row, name))]

    def listed(values):
        return [v for value in values for v in value]

    def summed(products, manual=True):
        products = outer(*products)
        out = outer_sum(scalars, products, staged and manual)
        order.leave(*out)
        if staged and manual:
            return DpSum(scalars, order, *out)
        return out[0] if staged is False else lax.psum(out[0], "dp")

    lead, *others = rows
    lead.project(0, qkvs)
    for row in others:
        row.project(0, qkvs)
    if split:
        lead.project(1, qkvs)
    lead.attend()
    if split:
        for row in others:
            row.project(1, qkvs)
    lead.out_project(outs)
    for row in others:
        row.attend()
    lead.middle()
    for row in others:
        row.out_project(outs)
    lead.feed(0, ups, downs)
    if split:
        lead.feed(1, ups, downs)
    for row in others:
        row.middle()
        row.feed(0, ups, downs)
    lead.last()
    lead.feed_back(0, ups, downs)
    if split:
        for row in others:
            row.feed(1, ups, downs)
    if split:
        lead.feed_back(1, ups, downs)
    for row in others:
        row.last()
        row.feed_back(0, ups, downs)
    lead.middle_back()
    if split:
        for row in others:
            row.feed_back(1, ups, downs)
    grad_down = summed([(own_columns("act"), both_cores("ffn_grad"))], manual=False)
    lead.out_back(outs)
    for row in others:
        row.middle_back()
    up = summed([(both_cores("ffn_in"), own_columns("hidden_grad"))])
    lead.attend_back(0)
    for row in others:
        row.out_back(outs)
    if staged:
        up.scatter()
    for row in others:
        row.attend_back(0)

    attn_in = both_cores("attn_in")

    def qkv_product(pair):
        return (attn_in, listed(row.projected_grad[pair] for row in rows))

    attended = listed(row.attended for row in rows)
    heads = [summed([qkv_product(0), (both_cores("attn_grad"), attended)])]
    if staged:
        up.collect()
    for pair in range(1, pairs):
        lead.attend_back(pair)
        if staged:
            heads[0].scatter()
        if pair == pairs - 1:
            lead.project_back(qkvs)
        if staged:
            up.spread()
        for row in others:
            row.attend_back(pair)
        heads.append(summed([qkv_product(pair)]))
    if pairs == 1:
        lead.project_back(qkvs)
    for row in others:
        row.project_back(qkvs)
    if staged:
        heads[0].collect()
    lead.first_back()
    if staged:
        (grad_down,) = order.enter(grad_down)
        grad_down = grad_down.astype(F32)
        order.leave(grad_down)
        for total in heads[1:]:
            total.scatter()
        heads[0].spread()
        (got,) = order.enter(up.other)
        grad_up = place(scalars, up.quarter, got)
        order.leave(grad_up)
    for row in others:
        row.first_back()
    if staged:
        for total in heads[1:]:
            total.collect()
    stats = [row.stat_first for row in rows] + [row.stat_middle for row in rows]
    stats += [row.stat_last for row in rows] + [row.stat_back for row in rows]
    (small,) = call(
        functools.partial(small_kernel, row_count, share),
        "small",
        scalars,
        list(order.enter(*stats)),
        [((16, width), F32)],
    )
    order.leave(small)
    steps = [("tensor", 1 << i) for i in range(t_size.bit_length() - 1)]
    steps += [("dp", 1 << i) for i in range(d_size.bit_length() - 1)]
    powers = t_size & (t_size - 1) == 0 and d_size & (d_size - 1) == 0
    if powers:
        for axis, step in steps[:2]:
            small = doubling(small, axis, step)
        steps = steps[2:]
    if staged:
        (got,) = order.enter(heads[0].other)
        grad_qkv, grad_out = place_heads(scalars, heads[0].quarter, got, 0, pairs, None)
        order.leave(grad_out)
        for total in heads[1:]:
            total.spread()
    if powers:
        for axis, step in steps:
            small = doubling(small, axis, step)
    else:
        small = lax.psum(small, ("dp", "tensor"))
    if staged:
        for pair in range(1, pairs):
            (grad_qkv,) = place_heads(
                scalars, heads[pair].quarter, heads[pair].other, pair, pairs, grad_qkv
            )
        grad_qkv = grad_qkv.transpose(1, 0, 2)
    else:
        grad_down, grad_up, *blocks = [
            v.astype(F32) for v in lax.psum((grad_down, up, *heads), "dp")
        ]
        grad_out = blocks[0][:, 384:].T
        blocks = [grad[:, :384].reshape(width, 3, 128) for grad in blocks]
        grad_qkv = jnp.concatenate(blocks, axis=2)
    sums = small[8 : 8 + GROUPS]
    group_rms = jnp.sqrt(sums[:, :3] / (sums[:, 3:4] * width))
    return (
        jnp.stack([row.output for row in rows]),
        jnp.stack([row.input_grad for row in rows]),
        grad_qkv,
        grad_out,
        grad_up,
        grad_down.astype(F32),
        small[:4],
        small[4:8],
        group_rms,
    )


def solution(mesh):
    placed = (
        P("dp", "tensor", None),
        P("dp", "tensor", None),
        P("dp"),
        P("dp"),
        P(None, None, "tensor"),
        P("tensor", None),
        P(None, "tensor"),
        P("tensor", None),
        P(),
        P(),
    )
    return jax.shard_map(
        per_device,
        mesh=mesh,
        in_specs=placed,
        out_specs=(
            P("dp", "tensor", None),
            P("dp", "tensor", None),
            P(None, None, "tensor"),
            P("tensor", None),
            P(None, "tensor"),
            P("tensor", None),
            P(),
            P(),
            P(),
        ),
        check_vma=False,
    )
```

```python
import functools

import jax
import jax.numpy as jnp
from jax import lax
from jax.experimental import pallas as pl
from jax.experimental.pallas import tpu as pltpu
from jax.sharding import PartitionSpec as P

HEAD_DIM = 64
GROUPS = 4
MIN_LENGTH = 544
F32 = jnp.float32
B16 = jnp.bfloat16

epsilon = 1e-05
negative_fill = -1e30
log2_e = 1.4426950408889634
gelu_scale = 0.7978845608028654
gelu_cubic = 0.044715

BASE, TENSOR, Z, X, LENGTH = 0, 1, 2, 3, 4


def nt(left, right):
    return lax.dot_general(
        left, right, (((1,), (1,)), ((), ())), preferred_element_type=F32
    )


def nn(left, right):
    return lax.dot_general(
        left, right, (((1,), (0,)), ((), ())), preferred_element_type=F32
    )


def tn(left, right):
    return lax.dot_general(
        left, right, (((0,), (0,)), ((), ())), preferred_element_type=F32
    )


def tiles(extent, size):
    return [(start, min(size, extent - start)) for start in range(0, extent, size)]


def whole(shape):
    return pl.BlockSpec(shape, lambda *_: (0,) * len(shape))


def once(shape):
    return pl.BlockSpec(
        shape, lambda *_: (0,) * len(shape), pipeline_mode=pl.Buffered(buffer_count=1)
    )


def anywhere():
    return pl.BlockSpec(memory_space=pl.ANY)


def call(kernel, name, scalars, inputs, outs, in_specs=None, out_specs=None, grid=(1,), scratch=(), limit=10, flops=0, aliases={}):
    values = sum(v.size for v in inputs)
    in_specs = in_specs or [once(v.shape) for v in inputs]
    out_specs = out_specs or [whole(shape) for shape, _ in outs]
    return list(
        pl.pallas_call(
            kernel,
            out_shape=[jax.ShapeDtypeStruct(shape, dtype) for shape, dtype in outs],
            grid_spec=pltpu.PrefetchScalarGridSpec(
                num_scalar_prefetch=1,
                grid=grid,
                in_specs=in_specs,
                out_specs=out_specs,
                scratch_shapes=list(scratch),
            ),
            input_output_aliases=aliases,
            compiler_params=pltpu.CompilerParams(
                dimension_semantics=("arbitrary",) * len(grid), vmem_limit_bytes=limit << 20
            ),
            cost_estimate=pl.CostEstimate(
                flops=flops // 16, bytes_accessed=values // 16, transcendentals=0
            ),
            name=name,
        )(scalars, *inputs)
    )


def lane_half(shape, half):
    return (lax.broadcasted_iota(jnp.int32, shape, 1) // HEAD_DIM) == half


def mask_tile(scores, query_start, length):
    key_index = lax.broadcasted_iota(jnp.int32, scores.shape, 0)
    query_index = query_start + lax.broadcasted_iota(jnp.int32, scores.shape, 1)
    allowed = key_index <= query_index
    if scores.shape[0] > MIN_LENGTH:
        allowed = allowed & (key_index < length)
    return jnp.where(allowed, scores, negative_fill)


def place_of(scalars, parts, number, chunk):
    if parts == 1:
        return 0
    return pl.multiple_of(lax.bitwise_xor(scalars[TENSOR], number) * chunk, 16)


def halves_of(refs, number, chunk):
    return refs[number % len(refs)].at[pl.ds(number // len(refs) * chunk, chunk), :]


def attend_kernel(row, chunk, parts, query_tile, scalars, *refs):
    queries, keys, values = (refs[i * parts : (i + 1) * parts] for i in range(3))
    count = 1 if parts == 1 else 2
    outputs = refs[3 * parts : 3 * parts + count]
    lse_ref, q_ref, k_ref, v_ref, vt_ref, ot_ref = refs[3 * parts + count :]
    slots = q_ref.shape[0]
    length = scalars[LENGTH + row]
    for number in range(parts):
        target = pl.ds(place_of(scalars, parts, number, chunk), chunk)
        q_ref[target, :] = queries[number][...]
        k_ref[target, :] = keys[number][...]
        v_ref[target, :] = values[number][...]
    vt_ref[...] = v_ref[...].T
    scale = log2_e / HEAD_DIM**0.5
    for q0, qn in tiles(slots, query_tile):
        extent = q0 + qn
        for half in (0, 1):
            query = q_ref[q0 : q0 + qn, :]
            query = jnp.where(lane_half(query.shape, half), query, jnp.zeros_like(query))
            scores = mask_tile(nt(k_ref[0:extent, :], query), q0, length)
            top = jnp.max(scores, axis=0, keepdims=True)
            weights = jnp.exp2((scores - top) * scale)
            total = jnp.sum(weights, axis=0, keepdims=True)
            lanes = slice(half * HEAD_DIM, half * HEAD_DIM + HEAD_DIM)
            out_t = nn(vt_ref[lanes, 0:extent], weights.astype(B16))
            ot_ref[lanes, q0 : q0 + qn] = out_t * (1.0 / total)
            lse_ref[half, :, q0 : q0 + qn] = top * scale + jnp.log2(total)
    q_ref[...] = ot_ref[...].T.astype(B16)
    for number in range(parts):
        source = pl.ds(place_of(scalars, parts, number, chunk), chunk)
        halves_of(outputs, number, chunk)[...] = q_ref[source, :]


def column(rows, position):
    return pl.BlockSpec((rows, 128), position)


def attend(scalars, row, projected):
    parts = len(projected)
    chunk, width = projected[0].shape
    pairs = width // 384
    slots = chunk * parts
    count = 1 if parts == 1 else 2
    columns = []
    for kind in range(3):
        spot = column(chunk, lambda p, s, kind=kind: (0, kind * pairs + p))
        columns += [spot] * parts
    return call(
        functools.partial(attend_kernel, row, chunk, parts, 512),
        "attend",
        scalars,
        [*projected, *projected, *projected],
        [((slots // count, pairs * 128), B16)] * count + [((2 * pairs, 1, slots), F32)],
        columns,
        [column(slots // count, lambda p, s: (0, p))] * count
        + [pl.BlockSpec((2, 1, slots), lambda p, s: (p, 0, 0))],
        (pairs,),
        [pltpu.VMEM((slots, 128), B16)] * 3
        + [pltpu.VMEM((128, slots), B16), pltpu.VMEM((128, slots), F32)],
        limit=14,
        flops=4 * slots * slots * 128 * pairs,
    )


def attend_back_kernel(row, chunk, parts, query_tile, scalars, *refs):
    queries, keys, values = (refs[i * parts : (i + 1) * parts] for i in range(3))
    count = 1 if parts == 1 else 2
    refs = refs[3 * parts :]
    attended, grads, lse_ref = refs[:count], refs[count : 2 * count], refs[2 * count]
    outputs = refs[2 * count + 1 : 3 * count + 1]
    q_ref, k_ref, v_ref, g_ref, kt_ref, inner_ref, dk_ref, dv_ref, dqt_ref, t_ref = refs[
        3 * count + 1 :
    ]
    slots = q_ref.shape[0]
    half = pl.program_id(0)
    length = scalars[LENGTH + row]

    @pl.when(half == 0)
    def _():
        for number in range(parts):
            target = pl.ds(place_of(scalars, parts, number, chunk), chunk)
            grad = halves_of(grads, number, chunk)[...]
            out = halves_of(attended, number, chunk)[...]
            q_ref[target, :] = queries[number][...]
            k_ref[target, :] = keys[number][...]
            v_ref[target, :] = values[number][...]
            g_ref[target, :] = grad
            t_ref[target, :] = out.astype(F32) * grad.astype(F32)
        kt_ref[...] = k_ref[...].T
        products = t_ref[...].T
        inner_ref[0:1, :] = jnp.sum(products[0:HEAD_DIM], axis=0, keepdims=True)
        inner_ref[1:2, :] = jnp.sum(products[HEAD_DIM:], axis=0, keepdims=True)
        dk_ref[...] = jnp.zeros_like(dk_ref)
        dv_ref[...] = jnp.zeros_like(dv_ref)

    scale = log2_e / HEAD_DIM**0.5
    base = pl.multiple_of(half * HEAD_DIM, HEAD_DIM)
    for q0, qn in tiles(slots, query_tile):
        extent = q0 + qn
        keep = lane_half((qn, 128), half)
        query = q_ref[q0 : q0 + qn, :]
        query = jnp.where(keep, query, jnp.zeros_like(query))
        grad = g_ref[q0 : q0 + qn, :]
        grad = jnp.where(keep, grad, jnp.zeros_like(grad))
        lse = lse_ref[0, :, q0 : q0 + qn]
        inner = jnp.where(
            half == 0, inner_ref[0:1, q0 : q0 + qn], inner_ref[1:2, q0 : q0 + qn]
        )
        scores = mask_tile(nt(k_ref[0:extent, :], query), q0, length)
        probs = jnp.exp2(scores * scale - lse)
        dv_ref[0:extent, :] += nn(probs.astype(B16), grad)
        probs_grad = nt(v_ref[0:extent, :], grad)
        scores_grad = (probs * (probs_grad - inner)).astype(B16)
        dk_ref[0:extent, :] += nn(scores_grad, query)
        dqt_ref[pl.ds(base, HEAD_DIM), q0 : q0 + qn] = nn(
            kt_ref[pl.ds(base, HEAD_DIM), 0:extent], scores_grad
        )

    @pl.when(half == 1)
    def _():
        factor = 1.0 / HEAD_DIM**0.5
        q_ref[...] = (dqt_ref[...].T * factor).astype(B16)
        k_ref[...] = (dk_ref[...] * factor).astype(B16)
        v_ref[...] = dv_ref[...].astype(B16)
        for number in range(parts):
            source = pl.ds(place_of(scalars, parts, number, chunk), chunk)
            target = halves_of(outputs, number, chunk)
            target[:, 0:128] = q_ref[source, :]
            target[:, 128:256] = k_ref[source, :]
            target[:, 256:384] = v_ref[source, :]


def attend_back(scalars, row, projected, attended, grads, lse, pair):
    parts = len(projected)
    chunk, width = projected[0].shape
    pairs = width // 384
    slots = chunk * parts
    count = len(attended)
    rows = slots // count
    columns = []
    for kind in range(3):
        columns += [column(chunk, lambda h, s, kind=kind: (0, kind * pairs + pair))] * parts
    columns += [column(rows, lambda h, s: (0, pair))] * (2 * count)
    columns += [pl.BlockSpec((1, 1, slots), lambda h, s: (2 * pair + h, 0, 0))]
    return call(
        functools.partial(attend_back_kernel, row, chunk, parts, 384),
        "attend_back",
        scalars,
        [*projected, *projected, *projected, *attended, *grads, lse],
        [((rows, 384), B16)] * count,
        columns,
        [whole((rows, 384))] * count,
        (2,),
        [pltpu.VMEM((slots, 128), B16)] * 4
        + [pltpu.VMEM((128, slots), B16), pltpu.VMEM((8, slots), F32)]
        + [pltpu.VMEM((slots, 128), F32)] * 2
        + [pltpu.VMEM((128, slots), F32), pltpu.VMEM((slots, 128), F32)],
        limit=14,
        flops=10 * slots * slots * 128,
    )


def sum_of(terms):
    total = terms[0]
    for term in terms[1:]:
        total = total + term
    return total


def project_kernel(count, scalars, x_ref, *refs):
    for w_ref, out_ref in zip(refs[:count], refs[count:]):
        cols = w_ref.shape[2]
        for kind in range(3):
            columns = slice(kind * cols, kind * cols + cols)
            out_ref[:, columns] = nn(x_ref[...], w_ref[kind]).astype(B16)


def project(scalars, x, ws):
    rows, depth = x.shape
    cols = ws[0].shape[2]
    return call(
        functools.partial(project_kernel, len(ws)),
        "project",
        scalars,
        [x, *ws],
        [((rows, 3 * cols), B16)] * len(ws),
        flops=6 * rows * depth * cols * len(ws),
    )


def out_kernel(count, scalars, *refs):
    xs, ws, outs = refs[:count], refs[count : 2 * count], refs[2 * count :]
    n = outs[0].shape[0]
    for index, out in enumerate(outs):
        rows = slice(index * n, index * n + n)
        total = sum_of([nn(x[rows, :], w[...]) for x, w in zip(xs, ws)])
        out[...] = total.astype(out.dtype)


def partial_shapes(share, width, split):
    return [((share, width), F32)] + ([((share, width), B16)] if split else [])


def out_project(scalars, xs, ws):
    split = len(ws) == 2
    rows, depth = xs[0].shape
    width = ws[0].shape[1]
    return call(
        functools.partial(out_kernel, len(ws)),
        "out_project",
        scalars,
        [*xs, *ws],
        partial_shapes(rows // len(ws), width, split),
        flops=2 * rows * depth * width * len(ws),
    )


def feed_kernel(count, scalars, x_ref, *refs):
    ups, downs, refs = refs[:count], refs[count : 2 * count], refs[2 * count :]
    acts, slopes, out_ref = refs[:count], refs[count : 2 * count], refs[2 * count]
    for start, size in tiles(x_ref.shape[0], 272):
        rows = slice(start, start + size)
        terms = []
        for up, down, act_ref, slope_ref in zip(ups, downs, acts, slopes):
            hidden = nn(x_ref[rows, :], up[...])
            square = hidden * hidden
            bent = jnp.tanh(hidden * (gelu_scale + (gelu_scale * gelu_cubic) * square))
            upper = 0.5 + 0.5 * bent
            act = (hidden * upper).astype(B16)
            act_ref[rows, :] = act
            slope = upper + hidden * (1.0 - bent * bent) * (
                0.5 * gelu_scale + (1.5 * gelu_scale * gelu_cubic) * square
            )
            slope_ref[rows, :] = slope.astype(B16)
            terms.append(nn(act, down[...]))
        out_ref[rows, :] = sum_of(terms).astype(out_ref.dtype)


def feed(scalars, x, ups, downs, dtype):
    rows, depth = x.shape
    units, width = downs[0].shape
    count = len(ups)
    out = call(
        functools.partial(feed_kernel, count),
        "feed",
        scalars,
        [x, *ups, *downs],
        [((rows, units), B16)] * (2 * count) + [((rows, width), dtype)],
        limit=18,
        flops=4 * rows * depth * units * count,
    )
    return out[:count], out[count : 2 * count], out[2 * count]


def feed_back_kernel(count, scalars, x_ref, *refs):
    slopes, ups, downs = (refs[i * count : (i + 1) * count] for i in range(3))
    grads, out_ref = refs[3 * count : 4 * count], refs[4 * count]
    for start, size in tiles(x_ref.shape[0], 272):
        rows = slice(start, start + size)
        terms = []
        for slope, up, down, grad_ref in zip(slopes, ups, downs, grads):
            grad = nt(x_ref[rows, :], down[...]) * slope[rows, :].astype(F32)
            grad = grad.astype(B16)
            grad_ref[rows, :] = grad
            terms.append(nt(grad, up[...]))
        out_ref[rows, :] = sum_of(terms).astype(out_ref.dtype)


def feed_back(scalars, x, slopes, ups, downs, dtype):
    rows, width = x.shape
    depth, units = ups[0].shape
    count = len(ups)
    out = call(
        functools.partial(feed_back_kernel, count),
        "feed_back",
        scalars,
        [x, *slopes, *ups, *downs],
        [((rows, units), B16)] * count + [((rows, depth), dtype)],
        limit=18,
        flops=4 * rows * depth * units * count,
    )
    return out[:count], out[count]


def out_back_kernel(count, scalars, *refs):
    xs, ws, outs = refs[: len(refs) - 2 * count], refs[-2 * count : -count], refs[-count:]
    for w_ref, out_ref in zip(ws, outs):
        for index, x in enumerate(xs):
            n = x.shape[0]
            out_ref[index * n : index * n + n, :] = nt(x[...], w_ref[...]).astype(B16)


def out_back(scalars, xs, ws):
    rows, depth = len(xs) * xs[0].shape[0], xs[0].shape[1]
    cols = ws[0].shape[0]
    return call(
        functools.partial(out_back_kernel, len(ws)),
        "out_back",
        scalars,
        [*xs, *ws],
        [((rows, cols), B16)] * len(ws),
        flops=2 * rows * depth * cols * len(ws),
    )


def project_back_kernel(pairs, count, scalars, *refs):
    sides = [refs[i * pairs : (i + 1) * pairs] for i in range(count)]
    ws, outs = refs[pairs * count : (pairs + 1) * count], refs[(pairs + 1) * count :]
    n = outs[0].shape[0]
    for index, out in enumerate(outs):
        terms = []
        for grads, w_ref in zip(sides, ws):
            for kind in range(3):
                columns = [
                    grad[index * n : index * n + n, kind * 128 : kind * 128 + 128]
                    for grad in grads
                ]
                left = columns[0] if pairs == 1 else jnp.concatenate(columns, axis=1)
                terms.append(nt(left, w_ref[kind]))
        out[...] = sum_of(terms).astype(out.dtype)


def project_back(scalars, sides, ws):
    split = len(ws) == 2
    rows = sides[0][0].shape[0]
    depth, cols = ws[0].shape[1:]
    return call(
        functools.partial(project_back_kernel, len(sides[0]), len(ws)),
        "project_back",
        scalars,
        [v for side in sides for v in side] + list(ws),
        partial_shapes(rows // len(ws), depth, split),
        limit=12,
        flops=6 * rows * depth * cols * len(ws),
    )


def block_of(scalars, index, staged):
    if not staged:
        return index
    z = lax.rem(scalars[Z] + lax.rem(index, 4), 4)
    x = jnp.where(index < 4, scalars[X], 1 - scalars[X])
    return 4 * x + z


def gathered(pieces, target, sems, first):
    copies, start = [], 0
    for index, piece in enumerate(pieces):
        rows = piece.shape[0]
        spot = target.at[pl.ds(start, rows), :]
        copies.append(pltpu.make_async_copy(piece, spot, sems.at[first + index]))
        start += rows
    return copies


def outer_kernel(count, staged, scalars, *refs):
    lefts, rights = refs[:count], refs[count : 2 * count]
    outs, (left_ref, right_ref, sems) = refs[2 * count : -3], refs[-3:]
    step = pl.program_id(0)

    @pl.when(step == 0)
    def _():
        copies = gathered(lefts, left_ref, sems, 0) + gathered(rights, right_ref, sems, count)
        for copy in copies:
            copy.start()
        for copy in copies:
            copy.wait()

    if staged:
        spots = [block_of(scalars, 2 * step + i, True) for i in (0, 1)]
        columns = [pl.ds(pl.multiple_of(spot * 128, 128), 128) for spot in spots]
        left = jnp.concatenate([left_ref[:, c] for c in columns], axis=1)
    else:
        left = left_ref[:, pl.ds(pl.multiple_of(step * 256, 256), 256)]
    value = tn(left, right_ref[...]).astype(B16)
    if staged:

        @pl.when(step < 2)
        def _():
            outs[0][...] = value

        @pl.when(step >= 2)
        def _():
            outs[1][...] = value

    else:
        outs[0][...] = value


def outer_sum(scalars, lefts, rights, staged):
    slots = sum(left.shape[0] for left in lefts)
    height, width = lefts[0].shape[1], rights[0].shape[1]
    if staged:
        outs = [((height // 2, width), B16)] * 2
        specs = [
            pl.BlockSpec((256, width), lambda i, s: (jnp.minimum(i, 1), 0)),
            pl.BlockSpec((256, width), lambda i, s: (jnp.maximum(i - 2, 0), 0)),
        ]
    else:
        outs = [((height, width), B16)]
        specs = [pl.BlockSpec((256, width), lambda i, s: (i, 0))]
    inputs = [*lefts, *rights]
    return call(
        functools.partial(outer_kernel, len(lefts), staged),
        "outer_sum",
        scalars,
        inputs,
        outs,
        [anywhere() for _ in inputs],
        specs,
        (height // 256,),
        [pltpu.VMEM((slots, height), B16), pltpu.VMEM((slots, width), B16)]
        + [pltpu.SemaphoreType.DMA((len(inputs),))],
        limit=18,
        flops=2 * slots * height * width,
    )


def head_outer_kernel(counts, staged, scalars, *refs):
    products = []
    for left_count, right_count in counts:
        products.append((refs[:left_count], refs[left_count : left_count + right_count]))
        refs = refs[left_count + right_count :]
    outs, refs = refs[: 2 if staged else 1], refs[2 if staged else 1 :]
    buffers = [(refs[2 * i], refs[2 * i + 1]) for i in range(len(products))]
    total_ref, sems = refs[2 * len(products) :]
    step = pl.program_id(0)

    @pl.when(step == 0)
    def _():
        copies = []
        for sources, targets in zip(products, buffers):
            for pieces, target in zip(sources, targets):
                copies += gathered(pieces, target, sems, len(copies))
        for copy in copies:
            copy.start()
        for copy in copies:
            copy.wait()

    first = 0
    for left_ref, right_ref in buffers:
        right = right_ref[:, pl.ds(pl.multiple_of(step * 256, 256), 256)]
        height = left_ref.shape[1]
        total_ref[first : first + height, :] = tn(left_ref[...], right).astype(B16)
        first += height
    if staged:
        rows = total_ref.shape[0] // 8
        for index in range(8):
            source = pl.ds(pl.multiple_of(block_of(scalars, index, True) * rows, 16), rows)
            at = index % 4 * rows
            outs[index // 4][at : at + rows, :] = total_ref[source, :]
    else:
        outs[0][...] = total_ref[...]


def head_outer(scalars, products, staged):
    inputs, counts, scratch = [], [], []
    height, width, flops = 0, products[0][1][0].shape[1], 0
    for lefts, rights in products:
        slots = sum(left.shape[0] for left in lefts)
        inputs += [*lefts, *rights]
        counts.append((len(lefts), len(rights)))
        scratch += [pltpu.VMEM((slots, lefts[0].shape[1]), B16)]
        scratch += [pltpu.VMEM((slots, width), B16)]
        height += lefts[0].shape[1]
        flops += 2 * slots * lefts[0].shape[1] * width
    parts = 2 if staged else 1
    return call(
        functools.partial(head_outer_kernel, counts, staged),
        "head_outer",
        scalars,
        inputs,
        [((height // parts, width), B16)] * parts,
        [anywhere() for _ in inputs],
        [pl.BlockSpec((height // parts, 256), lambda i, s: (0, i))] * parts,
        (width // 256,),
        scratch + [pltpu.VMEM((height, 256), B16), pltpu.SemaphoreType.DMA((len(inputs),))],
        limit=20,
        flops=flops,
    )


def quarter_kernel(scalars, keep_ref, got_ref, *outs):
    rows = outs[0].shape[0]
    for index, out in enumerate(outs):
        at = slice(index * rows, index * rows + rows)
        out[...] = (keep_ref[at, :].astype(F32) + got_ref[at, :].astype(F32)).astype(B16)


def place_blocks(scalars, quarter, other):
    rows = quarter[0].shape[0]
    result = []
    for half in (0, 1):
        x = scalars[X] if half == 0 else 1 - scalars[X]
        for index in range(4):
            z = lax.rem(scalars[Z] + 4 - index, 4)
            at = slice(index * rows, index * rows + rows)
            value = quarter[index][...] if half == 0 else other[at, :]
            result.append((value, 4 * x + z))
    return result


def place_kernel(scalars, *refs):
    quarter, other, out_ref, buffer, sems = refs[:4], refs[4], refs[5], refs[6], refs[7]
    rows = quarter[0].shape[0]
    copies = []
    for index, (value, spot) in enumerate(place_blocks(scalars, quarter, other)):
        buffer[index] = value.astype(F32)
        target = out_ref.at[pl.ds(pl.multiple_of(spot * rows, rows), rows), :]
        copy = pltpu.make_async_copy(buffer.at[index], target, sems.at[index])
        copy.start()
        copies.append(copy)
    for copy in copies:
        copy.wait()


def place(scalars, quarter, other):
    rows, width = quarter[0].shape
    (out,) = call(
        place_kernel,
        "place",
        scalars,
        [*quarter, other],
        [((8 * rows, width), F32)],
        out_specs=[anywhere()],
        scratch=[pltpu.VMEM((8, rows, width), F32), pltpu.SemaphoreType.DMA((8,))],
    )
    return out


def place_heads_kernel(pair, has_out, aliased, scalars, *refs):
    quarter, other = refs[:4], refs[4]
    refs = refs[5 + aliased :]
    qkv_ref, refs = refs[0], refs[1:]
    out_ref, (rows_ref, buffer, sems) = refs[0] if has_out else None, refs[-3:]
    rows = quarter[0].shape[0]
    for value, spot in place_blocks(scalars, quarter, other):
        rows_ref[pl.ds(pl.multiple_of(spot * rows, 16), rows), :] = value.astype(F32)
    copies = []
    if has_out:
        copies.append(
            pltpu.make_async_copy(
                rows_ref.at[pl.ds(384, rows_ref.shape[0] - 384), :], out_ref, sems.at[3]
            )
        )
        copies[-1].start()
    for kind in range(3):
        buffer[kind] = rows_ref[kind * 128 : kind * 128 + 128, :].T
        target = qkv_ref.at[kind, :, pl.ds(pair * 128, 128)]
        copies.append(pltpu.make_async_copy(buffer.at[kind], target, sems.at[kind]))
        copies[-1].start()
    for copy in copies:
        copy.wait()


def place_heads(scalars, quarter, other, pair, pairs, into):
    rows, width = quarter[0].shape
    total = 8 * rows
    has_out = total > 384
    inputs = [*quarter, other] + ([] if into is None else [into])
    in_specs = [once(v.shape) for v in [*quarter, other]]
    in_specs += [] if into is None else [anywhere()]
    outs = [((3, width, pairs * 128), F32)]
    outs += [((total - 384, width), F32)] if has_out else []
    return call(
        functools.partial(place_heads_kernel, pair, has_out, int(into is not None)),
        "place_heads",
        scalars,
        inputs,
        outs,
        in_specs,
        [anywhere() for _ in outs],
        scratch=[
            pltpu.VMEM((total, width), F32),
            pltpu.VMEM((3, width, 128), F32),
            pltpu.SemaphoreType.DMA((4,)),
        ],
        aliases={} if into is None else {6: 0},
    )


class DpSum:
    swap = [(i, i ^ 1) for i in range(8)]

    def __init__(self, scalars, order, keep, send):
        self.scalars, self.order, self.keep = scalars, order, keep
        self.got = lax.ppermute(send, "dp", self.swap)
        self.steps = self.run()

    def shifted(self, value):
        return lax.ppermute(value, "dp", [(d, (d + 2) % 8) for d in range(8)])

    def run(self):
        order = self.order
        (got,) = order.enter(self.got)
        rows, width = self.keep.shape
        blocks = call(
            quarter_kernel,
            "quarter",
            self.scalars,
            [self.keep, got],
            [((rows // 4, width), B16)] * 4,
        )
        order.leave(*blocks)
        got = self.shifted(blocks[3])
        yield
        for block in (blocks[2], blocks[1], blocks[0]):
            (got,) = order.enter(got)
            total = (block.astype(F32) + got.astype(F32)).astype(B16)
            order.leave(total)
            got = self.shifted(total)
            yield
        self.quarter = [total]
        for _ in range(2):
            (got,) = order.enter(got)
            order.leave(got)
            self.quarter.append(got)
            got = self.shifted(got)
            yield
        (got,) = order.enter(got)
        self.quarter.append(got)
        half = jnp.concatenate(self.quarter, axis=0)
        order.leave(half)
        self.other = lax.ppermute(half, "dp", self.swap)


class Order:
    def __init__(self):
        self.last, self.fresh, self.due = (), (), ()

    def enter(self, *values):
        count = len(values)
        values = lax.optimization_barrier(tuple(values) + self.last + self.due)
        self.due, self.fresh = self.fresh, ()
        return values[:count]

    def leave(self, *values):
        self.last = tuple(values)

    def soon(self, values):
        self.fresh = self.fresh + tuple(values)
        return list(values)


def normalize(values):
    center = values - jnp.mean(values, axis=-1, keepdims=True)
    inverse = lax.rsqrt(jnp.mean(center * center, axis=-1, keepdims=True) + epsilon)
    return center * inverse, inverse


def values_back(grad, gain, vhat, inverse):
    scaled = grad * gain
    mean_scaled = jnp.mean(scaled, axis=-1, keepdims=True)
    mean_product = jnp.mean(scaled * vhat, axis=-1, keepdims=True)
    return (scaled - mean_scaled - vhat * mean_product) * inverse


def added(refs, rows):
    total = refs[0][rows, :].astype(F32)
    for ref in refs[1:]:
        total = total + ref[rows, :].astype(F32)
    return total


def fold(values):
    return jnp.sum(values.reshape(-1, 8, values.shape[-1]), axis=0)


def over_slots(share, width, sums, body):
    tile = 16 if share % 16 == 0 else 8
    totals = [jnp.zeros((8, width), F32)] * sums
    for start in range(0, share, tile):
        terms = body(pl.ds(start, tile), start, tile)
        totals = [total + fold(term) for total, term in zip(totals, terms)]
    return totals


def valid_rows(scalars, row, start, tile):
    slot = scalars[BASE] + start + lax.broadcasted_iota(jnp.int32, (tile, 1), 0)
    return (slot < scalars[LENGTH + row]).astype(F32)


def keep_sums(ref, totals):
    for index, total in enumerate(totals):
        ref[index : index + 1, :] = jnp.sum(total, axis=0, keepdims=True)


def first_kernel(scalars, x_ref, gains, biases, *outs):
    share, width = outs[0].shape
    for row, out in enumerate(outs):

        def body(rows, start, tile, row=row, out=out):
            vhat, _ = normalize(x_ref[row, rows, :].astype(F32))
            out[rows, :] = (vhat * gains[0:1, :] + biases[0:1, :]).astype(B16)
            return []

        over_slots(share, width, 0, body)


def middle_kernel(row, count, scalars, *refs):
    addends = refs[:count]
    x_ref, gains, biases, sum_ref, middle_ref, normed_ref, stat_ref = refs[count:]
    share, width = sum_ref.shape

    def body(rows, start, tile):
        attn_sum = added(addends, rows)
        sum_ref[rows, :] = attn_sum
        vhat, _ = normalize(attn_sum)
        branch = vhat * gains[1:2, :] + biases[1:2, :]
        middle = x_ref[0, rows, :].astype(F32) + branch
        middle_ref[rows, :] = middle
        vhat, _ = normalize(middle)
        normed_ref[rows, :] = (vhat * gains[2:3, :] + biases[2:3, :]).astype(B16)
        return [branch * branch * valid_rows(scalars, row, start, tile)]

    keep_sums(stat_ref, over_slots(share, width, 1, body))


def last_kernel(row, count, scalars, *refs):
    addends = refs[:count]
    middle_ref, cot_ref, gains, biases, out_ref, grad_ref, stat_ref = refs[count:]
    share, width = out_ref.shape

    def body(rows, start, tile):
        vhat, inverse = normalize(added(addends, rows))
        branch = vhat * gains[3:4, :] + biases[3:4, :]
        result = middle_ref[rows, :] + branch
        out_ref[rows, :] = result.astype(B16)
        valid = valid_rows(scalars, row, start, tile)
        out_grad = cot_ref[0, rows, :].astype(F32) * valid
        grad_ref[rows, :] = values_back(out_grad, gains[3:4, :], vhat, inverse).astype(B16)
        return [
            result * result * valid,
            branch * branch * valid,
            out_grad * vhat,
            out_grad,
        ]

    keep_sums(stat_ref, over_slots(share, width, 4, body))


def middle_back_kernel(row, count, scalars, *refs):
    addends = refs[:count]
    sum_ref, middle_ref, cot_ref, gains, carry_ref, grad_ref, stat_ref = refs[count:]
    share, width = sum_ref.shape

    def body(rows, start, tile):
        normed_grad = added(addends, rows)
        mhat, inverse = normalize(middle_ref[rows, :])
        out_grad = cot_ref[0, rows, :].astype(F32) * valid_rows(scalars, row, start, tile)
        carry = out_grad + values_back(normed_grad, gains[2:3, :], mhat, inverse)
        carry_ref[rows, :] = carry
        ahat, inverse = normalize(sum_ref[rows, :])
        grad_ref[rows, :] = values_back(carry, gains[1:2, :], ahat, inverse).astype(B16)
        return [normed_grad * mhat, normed_grad, carry * ahat, carry]

    keep_sums(stat_ref, over_slots(share, width, 4, body))


def first_back_kernel(row, count, scalars, *refs):
    addends = refs[:count]
    x_ref, carry_ref, gains, out_ref, stat_ref = refs[count:]
    share, width = out_ref.shape

    def body(rows, start, tile):
        grad = added(addends, rows)
        vhat, inverse = normalize(x_ref[0, rows, :].astype(F32))
        back = values_back(grad, gains[0:1, :], vhat, inverse)
        out_ref[rows, :] = (carry_ref[rows, :] + back).astype(B16)
        return [grad * vhat, grad]

    keep_sums(stat_ref, over_slots(share, width, 2, body))


def small_kernel(row_count, share, scalars, *refs):
    firsts, middles, lasts, backs = (
        refs[i * row_count : (i + 1) * row_count] for i in range(4)
    )
    out_ref = refs[4 * row_count]
    width = out_ref.shape[1]
    spots = ((firsts, 0), (backs, 2), (backs, 0), (lasts, 2))
    spots += ((firsts, 1), (backs, 3), (backs, 1), (lasts, 3))
    for index, (source, line) in enumerate(spots):
        total = source[0][line : line + 1, :]
        for ref in source[1:]:
            total = total + ref[line : line + 1, :]
        out_ref[index : index + 1, :] = total
    lane = lax.broadcasted_iota(jnp.int32, (1, width), 1)
    totals = [jnp.zeros((1, width), F32)] * GROUPS
    for row in range(row_count):
        count = jnp.clip(scalars[LENGTH + row] - scalars[BASE], 0, share).astype(F32)
        values = jnp.where(lane == 3, count, 0.0)
        sources = (lasts[row][0:1, :], middles[row][0:1, :], lasts[row][1:2, :])
        for index, source in enumerate(sources):
            values = jnp.where(lane == index, jnp.sum(source, axis=1, keepdims=True), values)
        group = scalars[LENGTH + row_count + row]
        for index in range(GROUPS):
            totals[index] = totals[index] + jnp.where(group == index, values, 0.0)
    for index, total in enumerate(totals):
        out_ref[8 + index : 9 + index, :] = total
    out_ref[12:16, :] = jnp.zeros((4, width), F32)


def swap_core(value):
    return lax.ppermute(value, "tensor", [(0, 1), (1, 0), (2, 3), (3, 2)])


def swap_chip(value):
    return lax.ppermute(value, "tensor", [(0, 2), (2, 0), (1, 3), (3, 1)])


class Row:
    def __init__(self, index, order, split, scalars, tokens, cotangent, gains, biases, pairs):
        self.index, self.order, self.split, self.scalars = index, order, split, scalars
        self.tokens, self.cotangent = tokens, cotangent
        self.gains, self.biases = gains, biases
        self.shape = tokens.shape[1:]
        self.count = 2 if split else 1
        self.projected, self.slope = [], []
        self.all = {name: [] for name in ("attn_in", "act", "ffn_in", "ffn_grad")}
        self.all.update(hidden_grad=[], attn_grad=[])
        self.projected_grad = [None] * pairs
        self.other_heads = [None] * pairs

    def gather(self, own):
        if self.split:
            return [own, swap_chip(own)]
        return [lax.all_gather(own, "tensor", axis=0, tiled=True)]

    def reduce(self, own, far):
        if self.split:
            return [own, swap_chip(far)]
        return [lax.psum_scatter(own, "tensor", scatter_dimension=0, tiled=True)]

    def keep(self, name, values):
        own = values[0]
        pair = [own]
        if self.split:
            pair += self.order.soon([swap_core(values[-1])])
        self.all[name].append(pair)

    def over_row(self, kernel, name, inputs, outs):
        addends = self.order.enter(*self.addends)
        inputs = [*addends, *inputs]
        row = pl.BlockSpec((1, *self.shape), lambda i, s: (self.index, 0, 0))
        specs = [row if v.ndim == 3 else whole(v.shape) for v in inputs]
        return call(
            functools.partial(kernel, self.index, len(addends)),
            name,
            self.scalars,
            inputs,
            outs,
            specs,
        )

    def project(self, part, ws):
        (x,) = self.order.enter(self.attn_in[part])
        own, *other = project(self.scalars, x, ws)
        self.order.leave(own, *other)
        self.projected += [own, *[swap_core(v) for v in other]]
        self.keep("attn_in", [x])

    def attend(self):
        projected = self.order.enter(*self.projected)
        *self.attended, self.lse = attend(self.scalars, self.index, projected)
        self.order.leave(*self.attended)
        self.heads = [self.attended[0]] + [swap_core(v) for v in self.attended[1:]]

    def out_project(self, ws):
        xs = self.order.enter(*self.heads)
        own, *far = out_project(self.scalars, xs, ws)
        self.order.leave(own, *far)
        self.addends = self.reduce(own, *(far or [None]))

    def middle(self):
        self.attn_sum, self.mid, normed, self.stat_middle = self.over_row(
            middle_kernel,
            "middle",
            [self.tokens, self.gains, self.biases],
            [(self.shape, F32)] * 2 + [(self.shape, B16), ((1, self.shape[1]), F32)],
        )
        self.order.leave(normed)
        self.ffn_in = self.gather(normed)

    def feed(self, part, ups, downs):
        (x,) = self.order.enter(self.ffn_in[part])
        act, slope, out = feed(self.scalars, x, ups, downs, B16 if part else F32)
        self.order.leave(out)
        self.keep("act", act)
        self.keep("ffn_in", [x])
        self.slope.append(slope)
        if part == 0:
            self.own = out
        if part == len(self.ffn_in) - 1:
            self.addends = self.reduce(self.own, out)

    def last(self):
        self.output, grad, self.stat_last = self.over_row(
            last_kernel,
            "last",
            [self.mid, self.cotangent, self.gains, self.biases],
            [(self.shape, B16)] * 2 + [((4, self.shape[1]), F32)],
        )
        self.order.leave(grad)
        self.ffn_grad = self.gather(grad)

    def feed_back(self, part, ups, downs):
        (x,) = self.order.enter(self.ffn_grad[part])
        grad, out = feed_back(
            self.scalars, x, self.slope[part], ups, downs, B16 if part else F32
        )
        self.order.leave(out)
        self.keep("hidden_grad", grad)
        self.keep("ffn_grad", [x])
        if part == 0:
            self.own = out
        if part == len(self.ffn_grad) - 1:
            self.addends = self.reduce(self.own, out)

    def middle_back(self):
        self.carry, grad, self.stat_back = self.over_row(
            middle_back_kernel,
            "middle_back",
            [self.attn_sum, self.mid, self.cotangent, self.gains],
            [(self.shape, F32), (self.shape, B16), ((4, self.shape[1]), F32)],
        )
        self.order.leave(grad)
        self.attn_grad = self.gather(grad)

    def out_back(self, ws):
        xs = self.order.enter(*self.attn_grad)
        own, *other = out_back(self.scalars, xs, ws)
        self.order.leave(own, *other)
        self.attended_grad = [own] + [swap_core(v) for v in other]
        for x in xs:
            self.keep("attn_grad", [x])

    def attend_back(self, pair):
        grads = self.order.enter(*self.attended_grad)
        out = attend_back(
            self.scalars, self.index, self.projected, self.attended, grads, self.lse, pair
        )
        self.projected_grad[pair] = out
        self.order.leave(*out)
        if self.split:
            self.other_heads[pair : pair + 1] = self.order.soon([swap_core(out[1])])

    def project_back(self, ws):
        sides = [[grad[0] for grad in self.projected_grad]]
        if self.split:
            sides.append(self.other_heads)
        flat = self.order.enter(*[v for side in sides for v in side])
        pairs = len(self.projected_grad)
        sides = [flat[i * pairs : (i + 1) * pairs] for i in range(len(sides))]
        own, *far = project_back(self.scalars, sides, ws)
        self.order.leave(own, *far)
        self.addends = self.reduce(own, *(far or [None]))

    def first_back(self):
        self.input_grad, self.stat_first = self.over_row(
            first_back_kernel,
            "first_back",
            [self.tokens, self.carry, self.gains],
            [(self.shape, B16), ((2, self.shape[1]), F32)],
        )
        self.order.leave(self.input_grad)


def doubling(values, axis, step):
    size = lax.axis_size(axis)
    return values + lax.ppermute(values, axis, [(i, i ^ step) for i in range(size)])


def per_device(tokens, cotangent, lengths, groups, w_qkv, w_out, w_up, w_down, gains, biases):
    row_count, share, width = tokens.shape
    t_size, d_size = lax.axis_size("tensor"), lax.axis_size("dp")
    pairs = w_qkv.shape[2] // 128
    split = t_size == 4 and share % 16 == 0
    staged = d_size == 8
    t, d = lax.axis_index("tensor"), lax.axis_index("dp")
    both = lambda w: [w, swap_core(w)] if split else [w]
    qkvs = [w.transpose(1, 0, 2) for w in both(w_qkv)]
    outs, ups, downs = both(w_out), both(w_up), both(w_down)
    parts = range(2 if split else 1)
    spots = jnp.stack([t * share, t, d // 2, d % 2]).astype(jnp.int32)
    scalars = jnp.concatenate([spots, lengths, groups])
    order = Order()
    rows = [
        Row(r, order, split, scalars, tokens, cotangent, gains, biases, pairs)
        for r in range(row_count)
    ]
    normed = call(
        first_kernel,
        "first",
        scalars,
        [tokens, gains, biases],
        [((share, width), B16)] * row_count,
    )
    order.leave(*normed)
    for row, own in zip(rows, normed):
        row.attn_in = row.gather(own)

    def listed(values):
        return [v for value in values for v in value]

    def kept(name):
        return [pair[i] for row in rows for i in range(row.count) for pair in row.all[name]]

    def started(out):
        order.leave(*out)
        return DpSum(scalars, order, *out) if staged else out[0]

    def summed(lefts, rights):
        values = order.enter(*lefts, *rights)
        count = len(lefts)
        return started(outer_sum(scalars, values[:count], values[count:], staged))

    def heads_summed(pair, attended):
        products = [(listed(row.projected_grad[pair] for row in rows), kept("attn_in"))]
        if attended:
            products.append((listed(row.attended for row in rows), kept("attn_grad")))
        values = list(order.enter(*[v for two in products for side in two for v in side]))
        again = []
        for two in products:
            again.append([[values.pop(0) for _ in side] for side in two])
        return started(head_outer(scalars, again, staged))

    def tick(*totals):
        if staged:
            for total in totals:
                next(total.steps, None)

    def placed(total):
        (got,) = order.enter(total.other)
        out = place(scalars, total.quarter, got)
        order.leave(out)
        return out

    lead, *others = rows
    lead.project(0, qkvs)
    for row in others:
        row.project(0, qkvs)
    if split:
        lead.project(1, qkvs)
    lead.attend()
    if split:
        for row in others:
            row.project(1, qkvs)
    lead.out_project(outs)
    for row in others:
        row.attend()
    lead.middle()
    for row in others:
        row.out_project(outs)
    lead.feed(0, ups, downs)
    if split:
        lead.feed(1, ups, downs)
    for row in others:
        row.middle()
        row.feed(0, ups, downs)
    lead.last()
    lead.feed_back(0, ups, downs)
    if split:
        for row in others:
            row.feed(1, ups, downs)
    if split:
        lead.feed_back(1, ups, downs)
    for row in others:
        row.last()
        row.feed_back(0, ups, downs)
    lead.middle_back()
    for row in others:
        if split:
            row.feed_back(1, ups, downs)
    downs_sum = summed(kept("act"), kept("ffn_grad"))
    ups_sum = summed(kept("ffn_in"), kept("hidden_grad"))
    lead.out_back(outs)
    lead.attend_back(0)
    for row in others:
        row.middle_back()
    tick(downs_sum)
    for pair in range(1, pairs):
        lead.attend_back(pair)
    tick(downs_sum)
    for row in others:
        row.out_back(outs)
        row.attend_back(0)
    tick(downs_sum, ups_sum)
    heads = [heads_summed(0, True)]
    tick(downs_sum, ups_sum)
    lead.project_back(qkvs)
    tick(ups_sum, downs_sum)
    for pair in range(1, pairs):
        for row in others:
            row.attend_back(pair)
        tick(downs_sum, ups_sum)
        heads.append(heads_summed(pair, False))
    tick(heads[0], downs_sum, ups_sum)
    for row in others:
        row.project_back(qkvs)
    tick(heads[0], ups_sum)
    lead.first_back()
    tick(*heads, ups_sum)
    for row in others:
        row.first_back()
    tick(*heads)
    stats = [row.stat_first for row in rows] + [row.stat_middle for row in rows]
    stats += [row.stat_last for row in rows] + [row.stat_back for row in rows]
    (small,) = call(
        functools.partial(small_kernel, row_count, share),
        "small",
        scalars,
        list(order.enter(*stats)),
        [((16, width), F32)],
    )
    order.leave(small)
    steps = [("tensor", 1 << i) for i in range(t_size.bit_length() - 1)]
    steps += [("dp", 1 << i) for i in range(d_size.bit_length() - 1)]
    powers = t_size & (t_size - 1) == 0 and d_size & (d_size - 1) == 0
    if powers:
        for index, (axis, step) in enumerate(steps):
            small = doubling(small, axis, step)
            (small,) = order.enter(small)
            order.leave(small)
            tick(*heads)
            if index == 2 and staged:
                grad_down = placed(downs_sum)
    else:
        small = lax.psum(small, ("dp", "tensor"))
    if staged:
        tick(*heads)
        grad_up = placed(ups_sum)
        (got,) = order.enter(heads[0].other)
        grad_qkv, grad_out = place_heads(scalars, heads[0].quarter, got, 0, pairs, None)
        order.leave(grad_out)
        for pair in range(1, pairs):
            (grad_qkv,) = place_heads(
                scalars, heads[pair].quarter, heads[pair].other, pair, pairs, grad_qkv
            )
        grad_qkv = grad_qkv.transpose(1, 0, 2)
    else:
        grad_down, grad_up, *blocks = [
            v.astype(F32) for v in lax.psum((downs_sum, ups_sum, *heads), "dp")
        ]
        grad_out = blocks[0][384:]
        blocks = [grad[:384].reshape(3, 128, width) for grad in blocks]
        grad_qkv = jnp.concatenate(blocks, axis=1).transpose(2, 0, 1)
    sums = small[8 : 8 + GROUPS]
    group_rms = jnp.sqrt(sums[:, :3] / (sums[:, 3:4] * width))
    return (
        jnp.stack([row.output for row in rows]),
        jnp.stack([row.input_grad for row in rows]),
        grad_qkv,
        grad_out,
        grad_up,
        grad_down,
        small[:4],
        small[4:8],
        group_rms,
    )


def solution(mesh):
    placed = (
        P("dp", "tensor", None),
        P("dp", "tensor", None),
        P("dp"),
        P("dp"),
        P(None, None, "tensor"),
        P("tensor", None),
        P(None, "tensor"),
        P("tensor", None),
        P(),
        P(),
    )
    return jax.shard_map(
        per_device,
        mesh=mesh,
        in_specs=placed,
        out_specs=(
            P("dp", "tensor", None),
            P("dp", "tensor", None),
            P(None, None, "tensor"),
            P("tensor", None),
            P(None, "tensor"),
            P("tensor", None),
            P(),
            P(),
            P(),
        ),
        check_vma=False,
    )
```

```python
import functools

import jax
import jax.numpy as jnp
from jax import lax
from jax.experimental import pallas as pl
from jax.experimental.pallas import tpu as pltpu
from jax.sharding import PartitionSpec as P

HEAD_DIM = 64
GROUPS = 4
MIN_LENGTH = 544
F32 = jnp.float32
B16 = jnp.bfloat16

epsilon = 1e-05
negative_fill = -1e30
log2_e = 1.4426950408889634
gelu_scale = 0.7978845608028654
gelu_cubic = 0.044715

BASE, TENSOR, Z, X, LENGTH = 0, 1, 2, 3, 4


STAGES = (
    "FB1",
    "OB0",
    "WD",
    "WU",
    "MB1",
    "AB00",
    "AB01",
    "D",
    "OB1",
    "AB10",
    "D",
    "HP",
    "U",
    "PB0",
    "D",
    "AB11",
    "U",
    "HQ",
    "D",
    "PB1",
    "P",
    "Q",
    "U",
    "D",
    "P",
    "U",
    "FL0",
    "P",
    "Q",
    "U",
    "FL1",
    "PD",
    "Q",
    "P",
    "SM",
    "S",
    "P",
    "Q",
    "S",
    "Q",
    "S",
    "S",
    "S",
    "PU",
)


def nt(left, right):
    return lax.dot_general(
        left, right, (((1,), (1,)), ((), ())), preferred_element_type=F32
    )


def nn(left, right):
    return lax.dot_general(
        left, right, (((1,), (0,)), ((), ())), preferred_element_type=F32
    )


def tn(left, right):
    return lax.dot_general(
        left, right, (((0,), (0,)), ((), ())), preferred_element_type=F32
    )


def tiles(extent, size):
    return [(start, min(size, extent - start)) for start in range(0, extent, size)]


def whole(shape):
    return pl.BlockSpec(shape, lambda *_: (0,) * len(shape))


def once(shape):
    return pl.BlockSpec(
        shape, lambda *_: (0,) * len(shape), pipeline_mode=pl.Buffered(buffer_count=1)
    )


def anywhere():
    return pl.BlockSpec(memory_space=pl.ANY)


def call(kernel, name, scalars, inputs, outs, in_specs=None, out_specs=None, grid=(1,), scratch=(), limit=10, flops=0, aliases={}):
    values = sum(v.size for v in inputs)
    in_specs = in_specs or [once(v.shape) for v in inputs]
    out_specs = out_specs or [whole(shape) for shape, _ in outs]
    return list(
        pl.pallas_call(
            kernel,
            out_shape=[jax.ShapeDtypeStruct(shape, dtype) for shape, dtype in outs],
            grid_spec=pltpu.PrefetchScalarGridSpec(
                num_scalar_prefetch=1,
                grid=grid,
                in_specs=in_specs,
                out_specs=out_specs,
                scratch_shapes=list(scratch),
            ),
            input_output_aliases=aliases,
            compiler_params=pltpu.CompilerParams(
                dimension_semantics=("arbitrary",) * len(grid), vmem_limit_bytes=limit << 20
            ),
            cost_estimate=pl.CostEstimate(
                flops=flops // 16, bytes_accessed=values // 16, transcendentals=0
            ),
            name=name,
        )(scalars, *inputs)
    )


def lane_half(shape, half):
    return (lax.broadcasted_iota(jnp.int32, shape, 1) // HEAD_DIM) == half


def mask_tile(scores, query_start, length):
    key_index = lax.broadcasted_iota(jnp.int32, scores.shape, 0)
    query_index = query_start + lax.broadcasted_iota(jnp.int32, scores.shape, 1)
    allowed = key_index <= query_index
    if scores.shape[0] > MIN_LENGTH:
        allowed = allowed & (key_index < length)
    return jnp.where(allowed, scores, negative_fill)


def place_of(scalars, parts, number, chunk):
    if parts == 1:
        return 0
    return pl.multiple_of(lax.bitwise_xor(scalars[TENSOR], number) * chunk, 16)


def halves_of(refs, number, chunk):
    return refs[number % len(refs)].at[pl.ds(number // len(refs) * chunk, chunk), :]


def attend_kernel(row, chunk, parts, query_tile, scalars, *refs):
    queries, keys, values = (refs[i * parts : (i + 1) * parts] for i in range(3))
    count = 1 if parts == 1 else 2
    outputs = refs[3 * parts : 3 * parts + count]
    lse_ref, q_ref, k_ref, v_ref, vt_ref, ot_ref = refs[3 * parts + count :]
    slots = q_ref.shape[0]
    length = scalars[LENGTH + row]
    for number in range(parts):
        target = pl.ds(place_of(scalars, parts, number, chunk), chunk)
        q_ref[target, :] = queries[number][...]
        k_ref[target, :] = keys[number][...]
        v_ref[target, :] = values[number][...]
    vt_ref[...] = v_ref[...].T
    scale = log2_e / HEAD_DIM**0.5
    for q0, qn in tiles(slots, query_tile):
        extent = q0 + qn
        for half in (0, 1):
            query = q_ref[q0 : q0 + qn, :]
            query = jnp.where(lane_half(query.shape, half), query, jnp.zeros_like(query))
            scores = mask_tile(nt(k_ref[0:extent, :], query), q0, length)
            top = jnp.max(scores, axis=0, keepdims=True)
            weights = jnp.exp2((scores - top) * scale)
            total = jnp.sum(weights, axis=0, keepdims=True)
            lanes = slice(half * HEAD_DIM, half * HEAD_DIM + HEAD_DIM)
            out_t = nn(vt_ref[lanes, 0:extent], weights.astype(B16))
            ot_ref[lanes, q0 : q0 + qn] = out_t * (1.0 / total)
            lse_ref[half, :, q0 : q0 + qn] = top * scale + jnp.log2(total)
    q_ref[...] = ot_ref[...].T.astype(B16)
    for number in range(parts):
        source = pl.ds(place_of(scalars, parts, number, chunk), chunk)
        halves_of(outputs, number, chunk)[...] = q_ref[source, :]


def column(rows, position):
    return pl.BlockSpec((rows, 128), position)


def attend(scalars, row, projected):
    parts = len(projected)
    chunk, width = projected[0].shape
    pairs = width // 384
    slots = chunk * parts
    count = 1 if parts == 1 else 2
    columns = []
    for kind in range(3):
        spot = column(chunk, lambda p, s, kind=kind: (0, kind * pairs + p))
        columns += [spot] * parts
    return call(
        functools.partial(attend_kernel, row, chunk, parts, 512),
        "attend",
        scalars,
        [*projected, *projected, *projected],
        [((slots // count, pairs * 128), B16)] * count + [((2 * pairs, 1, slots), F32)],
        columns,
        [column(slots // count, lambda p, s: (0, p))] * count
        + [pl.BlockSpec((2, 1, slots), lambda p, s: (p, 0, 0))],
        (pairs,),
        [pltpu.VMEM((slots, 128), B16)] * 3
        + [pltpu.VMEM((128, slots), B16), pltpu.VMEM((128, slots), F32)],
        limit=14,
        flops=4 * slots * slots * 128 * pairs,
    )


def attend_back_kernel(row, chunk, parts, query_tile, scalars, *refs):
    queries, keys, values = (refs[i * parts : (i + 1) * parts] for i in range(3))
    count = 1 if parts == 1 else 2
    refs = refs[3 * parts :]
    attended, grads, lse_ref = refs[:count], refs[count : 2 * count], refs[2 * count]
    outputs = refs[2 * count + 1 : 3 * count + 1]
    q_ref, k_ref, v_ref, g_ref, kt_ref, inner_ref, dk_ref, dv_ref, dqt_ref, t_ref = refs[
        3 * count + 1 :
    ]
    slots = q_ref.shape[0]
    half = pl.program_id(0)
    length = scalars[LENGTH + row]

    @pl.when(half == 0)
    def _():
        for number in range(parts):
            target = pl.ds(place_of(scalars, parts, number, chunk), chunk)
            grad = halves_of(grads, number, chunk)[...]
            out = halves_of(attended, number, chunk)[...]
            q_ref[target, :] = queries[number][...]
            k_ref[target, :] = keys[number][...]
            v_ref[target, :] = values[number][...]
            g_ref[target, :] = grad
            t_ref[target, :] = out.astype(F32) * grad.astype(F32)
        kt_ref[...] = k_ref[...].T
        products = t_ref[...].T
        inner_ref[0:1, :] = jnp.sum(products[0:HEAD_DIM], axis=0, keepdims=True)
        inner_ref[1:2, :] = jnp.sum(products[HEAD_DIM:], axis=0, keepdims=True)
        dk_ref[...] = jnp.zeros_like(dk_ref)
        dv_ref[...] = jnp.zeros_like(dv_ref)

    scale = log2_e / HEAD_DIM**0.5
    base = pl.multiple_of(half * HEAD_DIM, HEAD_DIM)
    for q0, qn in tiles(slots, query_tile):
        extent = q0 + qn
        keep = lane_half((qn, 128), half)
        query = q_ref[q0 : q0 + qn, :]
        query = jnp.where(keep, query, jnp.zeros_like(query))
        grad = g_ref[q0 : q0 + qn, :]
        grad = jnp.where(keep, grad, jnp.zeros_like(grad))
        lse = lse_ref[0, :, q0 : q0 + qn]
        inner = jnp.where(
            half == 0, inner_ref[0:1, q0 : q0 + qn], inner_ref[1:2, q0 : q0 + qn]
        )
        scores = mask_tile(nt(k_ref[0:extent, :], query), q0, length)
        probs = jnp.exp2(scores * scale - lse)
        dv_ref[0:extent, :] += nn(probs.astype(B16), grad)
        probs_grad = nt(v_ref[0:extent, :], grad)
        scores_grad = (probs * (probs_grad - inner)).astype(B16)
        dk_ref[0:extent, :] += nn(scores_grad, query)
        dqt_ref[pl.ds(base, HEAD_DIM), q0 : q0 + qn] = nn(
            kt_ref[pl.ds(base, HEAD_DIM), 0:extent], scores_grad
        )

    @pl.when(half == 1)
    def _():
        factor = 1.0 / HEAD_DIM**0.5
        q_ref[...] = (dqt_ref[...].T * factor).astype(B16)
        k_ref[...] = (dk_ref[...] * factor).astype(B16)
        v_ref[...] = dv_ref[...].astype(B16)
        for number in range(parts):
            source = pl.ds(place_of(scalars, parts, number, chunk), chunk)
            target = halves_of(outputs, number, chunk)
            target[:, 0:128] = q_ref[source, :]
            target[:, 128:256] = k_ref[source, :]
            target[:, 256:384] = v_ref[source, :]


def attend_back(scalars, row, projected, attended, grads, lse, pair):
    parts = len(projected)
    chunk, width = projected[0].shape
    pairs = width // 384
    slots = chunk * parts
    count = len(attended)
    rows = slots // count
    columns = []
    for kind in range(3):
        columns += [column(chunk, lambda h, s, kind=kind: (0, kind * pairs + pair))] * parts
    columns += [column(rows, lambda h, s: (0, pair))] * (2 * count)
    columns += [pl.BlockSpec((1, 1, slots), lambda h, s: (2 * pair + h, 0, 0))]
    return call(
        functools.partial(attend_back_kernel, row, chunk, parts, 384),
        "attend_back",
        scalars,
        [*projected, *projected, *projected, *attended, *grads, lse],
        [((rows, 384), B16)] * count,
        columns,
        [whole((rows, 384))] * count,
        (2,),
        [pltpu.VMEM((slots, 128), B16)] * 4
        + [pltpu.VMEM((128, slots), B16), pltpu.VMEM((8, slots), F32)]
        + [pltpu.VMEM((slots, 128), F32)] * 2
        + [pltpu.VMEM((128, slots), F32), pltpu.VMEM((slots, 128), F32)],
        limit=14,
        flops=10 * slots * slots * 128,
    )


def sum_of(terms):
    total = terms[0]
    for term in terms[1:]:
        total = total + term
    return total


def project_kernel(count, scalars, x_ref, *refs):
    for w_ref, out_ref in zip(refs[:count], refs[count:]):
        cols = w_ref.shape[2]
        for kind in range(3):
            columns = slice(kind * cols, kind * cols + cols)
            out_ref[:, columns] = nn(x_ref[...], w_ref[kind]).astype(B16)


def project(scalars, x, ws):
    rows, depth = x.shape
    cols = ws[0].shape[2]
    return call(
        functools.partial(project_kernel, len(ws)),
        "project",
        scalars,
        [x, *ws],
        [((rows, 3 * cols), B16)] * len(ws),
        flops=6 * rows * depth * cols * len(ws),
    )


def out_kernel(count, scalars, *refs):
    xs, ws, outs = refs[:count], refs[count : 2 * count], refs[2 * count :]
    n = outs[0].shape[0]
    for index, out in enumerate(outs):
        rows = slice(index * n, index * n + n)
        total = sum_of([nn(x[rows, :], w[...]) for x, w in zip(xs, ws)])
        out[...] = total.astype(out.dtype)


def partial_shapes(share, width, split):
    return [((share, width), F32)] + ([((share, width), B16)] if split else [])


def out_project(scalars, xs, ws):
    split = len(ws) == 2
    rows, depth = xs[0].shape
    width = ws[0].shape[1]
    return call(
        functools.partial(out_kernel, len(ws)),
        "out_project",
        scalars,
        [*xs, *ws],
        partial_shapes(rows // len(ws), width, split),
        flops=2 * rows * depth * width * len(ws),
    )


def feed_kernel(count, scalars, x_ref, *refs):
    ups, downs, refs = refs[:count], refs[count : 2 * count], refs[2 * count :]
    acts, slopes, out_ref = refs[:count], refs[count : 2 * count], refs[2 * count]
    for start, size in tiles(x_ref.shape[0], 272):
        rows = slice(start, start + size)
        terms = []
        for up, down, act_ref, slope_ref in zip(ups, downs, acts, slopes):
            hidden = nn(x_ref[rows, :], up[...])
            square = hidden * hidden
            bent = jnp.tanh(hidden * (gelu_scale + (gelu_scale * gelu_cubic) * square))
            upper = 0.5 + 0.5 * bent
            act = (hidden * upper).astype(B16)
            act_ref[rows, :] = act
            slope = upper + hidden * (1.0 - bent * bent) * (
                0.5 * gelu_scale + (1.5 * gelu_scale * gelu_cubic) * square
            )
            slope_ref[rows, :] = slope.astype(B16)
            terms.append(nn(act, down[...]))
        out_ref[rows, :] = sum_of(terms).astype(out_ref.dtype)


def feed(scalars, x, ups, downs, dtype):
    rows, depth = x.shape
    units, width = downs[0].shape
    count = len(ups)
    out = call(
        functools.partial(feed_kernel, count),
        "feed",
        scalars,
        [x, *ups, *downs],
        [((rows, units), B16)] * (2 * count) + [((rows, width), dtype)],
        limit=18,
        flops=4 * rows * depth * units * count,
    )
    return out[:count], out[count : 2 * count], out[2 * count]


def feed_back_kernel(count, scalars, x_ref, *refs):
    slopes, ups, downs = (refs[i * count : (i + 1) * count] for i in range(3))
    grads, out_ref = refs[3 * count : 4 * count], refs[4 * count]
    for start, size in tiles(x_ref.shape[0], 272):
        rows = slice(start, start + size)
        terms = []
        for slope, up, down, grad_ref in zip(slopes, ups, downs, grads):
            grad = nt(x_ref[rows, :], down[...]) * slope[rows, :].astype(F32)
            grad = grad.astype(B16)
            grad_ref[rows, :] = grad
            terms.append(nt(grad, up[...]))
        out_ref[rows, :] = sum_of(terms).astype(out_ref.dtype)


def feed_back(scalars, x, slopes, ups, downs, dtype):
    rows, width = x.shape
    depth, units = ups[0].shape
    count = len(ups)
    out = call(
        functools.partial(feed_back_kernel, count),
        "feed_back",
        scalars,
        [x, *slopes, *ups, *downs],
        [((rows, units), B16)] * count + [((rows, depth), dtype)],
        limit=18,
        flops=4 * rows * depth * units * count,
    )
    return out[:count], out[count]


def out_back_kernel(count, scalars, *refs):
    xs, ws, outs = refs[: len(refs) - 2 * count], refs[-2 * count : -count], refs[-count:]
    for w_ref, out_ref in zip(ws, outs):
        for index, x in enumerate(xs):
            n = x.shape[0]
            out_ref[index * n : index * n + n, :] = nt(x[...], w_ref[...]).astype(B16)


def out_back(scalars, xs, ws):
    rows, depth = len(xs) * xs[0].shape[0], xs[0].shape[1]
    cols = ws[0].shape[0]
    return call(
        functools.partial(out_back_kernel, len(ws)),
        "out_back",
        scalars,
        [*xs, *ws],
        [((rows, cols), B16)] * len(ws),
        flops=2 * rows * depth * cols * len(ws),
    )


def project_back_kernel(pairs, count, scalars, *refs):
    sides = [refs[i * pairs : (i + 1) * pairs] for i in range(count)]
    ws, outs = refs[pairs * count : (pairs + 1) * count], refs[(pairs + 1) * count :]
    n = outs[0].shape[0]
    for index, out in enumerate(outs):
        terms = []
        for grads, w_ref in zip(sides, ws):
            for kind in range(3):
                columns = [
                    grad[index * n : index * n + n, kind * 128 : kind * 128 + 128]
                    for grad in grads
                ]
                left = columns[0] if pairs == 1 else jnp.concatenate(columns, axis=1)
                terms.append(nt(left, w_ref[kind]))
        out[...] = sum_of(terms).astype(out.dtype)


def project_back(scalars, sides, ws):
    split = len(ws) == 2
    rows = sides[0][0].shape[0]
    depth, cols = ws[0].shape[1:]
    return call(
        functools.partial(project_back_kernel, len(sides[0]), len(ws)),
        "project_back",
        scalars,
        [v for side in sides for v in side] + list(ws),
        partial_shapes(rows // len(ws), depth, split),
        limit=12,
        flops=6 * rows * depth * cols * len(ws),
    )


def turned(index):
    return 2 * lax.rem(index, 2) + index // 2


def block_of(scalars, index, staged):
    if not staged:
        return index
    z = lax.bitwise_xor(scalars[Z], turned(lax.rem(index, 4)))
    x = jnp.where(index < 4, scalars[X], 1 - scalars[X])
    return 4 * x + z


def gathered(pieces, target, sems, first):
    copies, start = [], 0
    for index, piece in enumerate(pieces):
        rows = piece.shape[0]
        spot = target.at[pl.ds(start, rows), :]
        copies.append(pltpu.make_async_copy(piece, spot, sems.at[first + index]))
        start += rows
    return copies


def outer_kernel(count, staged, scalars, *refs):
    lefts, rights = refs[:count], refs[count : 2 * count]
    outs, (left_ref, right_ref, sems) = refs[2 * count : -3], refs[-3:]
    step = pl.program_id(0)

    @pl.when(step == 0)
    def _():
        copies = gathered(lefts, left_ref, sems, 0) + gathered(rights, right_ref, sems, count)
        for copy in copies:
            copy.start()
        for copy in copies:
            copy.wait()

    if staged:
        spots = [block_of(scalars, 2 * step + i, True) for i in (0, 1)]
        columns = [pl.ds(pl.multiple_of(spot * 128, 128), 128) for spot in spots]
        left = jnp.concatenate([left_ref[:, c] for c in columns], axis=1)
    else:
        left = left_ref[:, pl.ds(pl.multiple_of(step * 256, 256), 256)]
    value = tn(left, right_ref[...]).astype(B16)
    if staged:

        @pl.when(step < 2)
        def _():
            outs[0][...] = value

        @pl.when(step >= 2)
        def _():
            outs[1][...] = value

    else:
        outs[0][...] = value


def outer_sum(scalars, lefts, rights, staged):
    slots = sum(left.shape[0] for left in lefts)
    height, width = lefts[0].shape[1], rights[0].shape[1]
    if staged:
        outs = [((height // 2, width), B16)] * 2
        specs = [
            pl.BlockSpec((256, width), lambda i, s: (jnp.minimum(i, 1), 0)),
            pl.BlockSpec((256, width), lambda i, s: (jnp.maximum(i - 2, 0), 0)),
        ]
    else:
        outs = [((height, width), B16)]
        specs = [pl.BlockSpec((256, width), lambda i, s: (i, 0))]
    inputs = [*lefts, *rights]
    return call(
        functools.partial(outer_kernel, len(lefts), staged),
        "outer_sum",
        scalars,
        inputs,
        outs,
        [anywhere() for _ in inputs],
        specs,
        (height // 256,),
        [pltpu.VMEM((slots, height), B16), pltpu.VMEM((slots, width), B16)]
        + [pltpu.SemaphoreType.DMA((len(inputs),))],
        limit=18,
        flops=2 * slots * height * width,
    )


def head_outer_kernel(counts, staged, scalars, *refs):
    products = []
    for left_count, right_count in counts:
        products.append((refs[:left_count], refs[left_count : left_count + right_count]))
        refs = refs[left_count + right_count :]
    outs, refs = refs[: 2 if staged else 1], refs[2 if staged else 1 :]
    buffers = [(refs[2 * i], refs[2 * i + 1]) for i in range(len(products))]
    total_ref, sems = refs[2 * len(products) :]
    step = pl.program_id(0)

    @pl.when(step == 0)
    def _():
        copies = []
        for sources, targets in zip(products, buffers):
            for pieces, target in zip(sources, targets):
                copies += gathered(pieces, target, sems, len(copies))
        for copy in copies:
            copy.start()
        for copy in copies:
            copy.wait()

    first = 0
    for left_ref, right_ref in buffers:
        right = right_ref[:, pl.ds(pl.multiple_of(step * 256, 256), 256)]
        height = left_ref.shape[1]
        total_ref[first : first + height, :] = tn(left_ref[...], right).astype(B16)
        first += height
    if staged:
        rows = total_ref.shape[0] // 8
        for index in range(8):
            source = pl.ds(pl.multiple_of(block_of(scalars, index, True) * rows, 16), rows)
            at = index % 4 * rows
            outs[index // 4][at : at + rows, :] = total_ref[source, :]
    else:
        outs[0][...] = total_ref[...]


def head_outer(scalars, products, staged):
    inputs, counts, scratch = [], [], []
    height, width, flops = 0, products[0][1][0].shape[1], 0
    for lefts, rights in products:
        slots = sum(left.shape[0] for left in lefts)
        inputs += [*lefts, *rights]
        counts.append((len(lefts), len(rights)))
        scratch += [pltpu.VMEM((slots, lefts[0].shape[1]), B16)]
        scratch += [pltpu.VMEM((slots, width), B16)]
        height += lefts[0].shape[1]
        flops += 2 * slots * lefts[0].shape[1] * width
    parts = 2 if staged else 1
    return call(
        functools.partial(head_outer_kernel, counts, staged),
        "head_outer",
        scalars,
        inputs,
        [((height // parts, width), B16)] * parts,
        [anywhere() for _ in inputs],
        [pl.BlockSpec((height // parts, 256), lambda i, s: (0, i))] * parts,
        (width // 256,),
        scratch + [pltpu.VMEM((height, 256), B16), pltpu.SemaphoreType.DMA((len(inputs),))],
        limit=20,
        flops=flops,
    )


def halve_kernel(scalars, keep_ref, got_ref, *outs):
    rows = outs[0].shape[0]
    for index, out in enumerate(outs):
        at = slice(index * rows, index * rows + rows)
        out[...] = (keep_ref[at, :].astype(F32) + got_ref[at, :].astype(F32)).astype(B16)


def halves_sum(scalars, keep, got):
    rows, width = keep.shape
    return call(halve_kernel, "halve", scalars, [keep, got], [((rows // 2, width), B16)] * 2)


def place_blocks(scalars, pieces):
    result = []
    for half, piece in enumerate(pieces):
        x = scalars[X] if half == 0 else 1 - scalars[X]
        rows = piece.shape[0] // 4
        for index in range(4):
            z = lax.bitwise_xor(scalars[Z], 2 * (index % 2) + index // 2)
            result.append((piece[index * rows : index * rows + rows, :], 4 * x + z))
    return result


def place_kernel(scalars, *refs):
    pieces, (out_ref, buffer, sems) = refs[:2], refs[2:]
    rows = buffer.shape[1]
    copies = []
    for index, (value, spot) in enumerate(place_blocks(scalars, pieces)):
        buffer[index] = value.astype(F32)
        target = out_ref.at[pl.ds(pl.multiple_of(spot * rows, rows), rows), :]
        copy = pltpu.make_async_copy(buffer.at[index], target, sems.at[index])
        copy.start()
        copies.append(copy)
    for copy in copies:
        copy.wait()


def place(scalars, pieces):
    rows, width = pieces[0].shape[0] // 4, pieces[0].shape[1]
    (out,) = call(
        place_kernel,
        "place",
        scalars,
        pieces,
        [((8 * rows, width), F32)],
        out_specs=[anywhere()],
        scratch=[pltpu.VMEM((8, rows, width), F32), pltpu.SemaphoreType.DMA((8,))],
    )
    return out


def place_heads_kernel(pair, has_out, aliased, scalars, *refs):
    pieces, refs = refs[:2], refs[2 + aliased :]
    qkv_ref, refs = refs[0], refs[1:]
    out_ref, (rows_ref, buffer, sems) = refs[0] if has_out else None, refs[-3:]
    for value, spot in place_blocks(scalars, pieces):
        rows = value.shape[0]
        rows_ref[pl.ds(pl.multiple_of(spot * rows, 16), rows), :] = value.astype(F32)
    copies = []
    if has_out:
        copies.append(
            pltpu.make_async_copy(
                rows_ref.at[pl.ds(384, rows_ref.shape[0] - 384), :], out_ref, sems.at[3]
            )
        )
        copies[-1].start()
    for kind in range(3):
        buffer[kind] = rows_ref[kind * 128 : kind * 128 + 128, :].T
        target = qkv_ref.at[kind, :, pl.ds(pair * 128, 128)]
        copies.append(pltpu.make_async_copy(buffer.at[kind], target, sems.at[kind]))
        copies[-1].start()
    for copy in copies:
        copy.wait()


def place_heads(scalars, pieces, pair, pairs, into):
    total, width = 2 * pieces[0].shape[0], pieces[0].shape[1]
    has_out = total > 384
    inputs = list(pieces) + ([] if into is None else [into])
    in_specs = [once(v.shape) for v in pieces]
    in_specs += [] if into is None else [anywhere()]
    outs = [((3, width, pairs * 128), F32)]
    outs += [((total - 384, width), F32)] if has_out else []
    return call(
        functools.partial(place_heads_kernel, pair, has_out, int(into is not None)),
        "place_heads",
        scalars,
        inputs,
        outs,
        in_specs,
        [anywhere() for _ in outs],
        scratch=[
            pltpu.VMEM((total, width), F32),
            pltpu.VMEM((3, width, 128), F32),
            pltpu.SemaphoreType.DMA((4,)),
        ],
        aliases={} if into is None else {3: 0},
    )


class DpSum:
    def __init__(self, scalars, order, keep, send):
        self.scalars, self.order, self.keep = scalars, order, keep
        self.got = self.exchanged(send, 1)
        self.steps = self.run()

    def exchanged(self, value, bit):
        return lax.ppermute(value, "dp", [(i, i ^ bit) for i in range(8)])

    def entered(self):
        (got,) = self.order.enter(self.got)
        return got

    def run(self):
        keep, send = halves_sum(self.scalars, self.keep, self.entered())
        self.order.leave(keep, send)
        self.got = self.exchanged(send, 2)
        yield
        keep, send = halves_sum(self.scalars, keep, self.entered())
        self.order.leave(keep, send)
        self.got = self.exchanged(send, 4)
        yield
        total = (keep.astype(F32) + self.entered().astype(F32)).astype(B16)
        self.order.leave(total)
        for bit in (4, 2):
            self.got = self.exchanged(total, bit)
            yield
            total = jnp.concatenate([total, self.entered()], axis=0)
            self.order.leave(total)
        self.total = total
        self.got = self.exchanged(total, 1)
        yield

    def pieces(self):
        return [self.total, self.entered()]


class Order:
    def __init__(self):
        self.last, self.fresh, self.due = (), (), ()

    def enter(self, *values):
        count = len(values)
        values = lax.optimization_barrier(tuple(values) + self.last + self.due)
        self.due, self.fresh = self.fresh, ()
        return values[:count]

    def leave(self, *values):
        self.last = tuple(values)

    def soon(self, values):
        self.fresh = self.fresh + tuple(values)
        return list(values)


def normalize(values):
    center = values - jnp.mean(values, axis=-1, keepdims=True)
    inverse = lax.rsqrt(jnp.mean(center * center, axis=-1, keepdims=True) + epsilon)
    return center * inverse, inverse


def values_back(grad, gain, vhat, inverse):
    scaled = grad * gain
    mean_scaled = jnp.mean(scaled, axis=-1, keepdims=True)
    mean_product = jnp.mean(scaled * vhat, axis=-1, keepdims=True)
    return (scaled - mean_scaled - vhat * mean_product) * inverse


def added(refs, rows):
    total = refs[0][rows, :].astype(F32)
    for ref in refs[1:]:
        total = total + ref[rows, :].astype(F32)
    return total


def fold(values):
    return jnp.sum(values.reshape(-1, 8, values.shape[-1]), axis=0)


def over_slots(share, width, sums, body):
    tile = 16 if share % 16 == 0 else 8
    totals = [jnp.zeros((8, width), F32)] * sums
    for start in range(0, share, tile):
        terms = body(pl.ds(start, tile), start, tile)
        totals = [total + fold(term) for total, term in zip(totals, terms)]
    return totals


def valid_rows(scalars, row, start, tile):
    slot = scalars[BASE] + start + lax.broadcasted_iota(jnp.int32, (tile, 1), 0)
    return (slot < scalars[LENGTH + row]).astype(F32)


def keep_sums(ref, totals):
    for index, total in enumerate(totals):
        ref[index : index + 1, :] = jnp.sum(total, axis=0, keepdims=True)


def first_kernel(scalars, x_ref, gains, biases, *outs):
    share, width = outs[0].shape
    for row, out in enumerate(outs):

        def body(rows, start, tile, row=row, out=out):
            vhat, _ = normalize(x_ref[row, rows, :].astype(F32))
            out[rows, :] = (vhat * gains[0:1, :] + biases[0:1, :]).astype(B16)
            return []

        over_slots(share, width, 0, body)


def middle_kernel(row, count, scalars, *refs):
    addends = refs[:count]
    x_ref, gains, biases, sum_ref, middle_ref, normed_ref, stat_ref = refs[count:]
    share, width = sum_ref.shape

    def body(rows, start, tile):
        attn_sum = added(addends, rows)
        sum_ref[rows, :] = attn_sum
        vhat, _ = normalize(attn_sum)
        branch = vhat * gains[1:2, :] + biases[1:2, :]
        middle = x_ref[0, rows, :].astype(F32) + branch
        middle_ref[rows, :] = middle
        vhat, _ = normalize(middle)
        normed_ref[rows, :] = (vhat * gains[2:3, :] + biases[2:3, :]).astype(B16)
        return [branch * branch * valid_rows(scalars, row, start, tile)]

    keep_sums(stat_ref, over_slots(share, width, 1, body))


def last_kernel(row, count, scalars, *refs):
    addends = refs[:count]
    middle_ref, cot_ref, gains, biases, out_ref, grad_ref, stat_ref = refs[count:]
    share, width = out_ref.shape

    def body(rows, start, tile):
        vhat, inverse = normalize(added(addends, rows))
        branch = vhat * gains[3:4, :] + biases[3:4, :]
        result = middle_ref[rows, :] + branch
        out_ref[rows, :] = result.astype(B16)
        valid = valid_rows(scalars, row, start, tile)
        out_grad = cot_ref[0, rows, :].astype(F32) * valid
        grad_ref[rows, :] = values_back(out_grad, gains[3:4, :], vhat, inverse).astype(B16)
        return [
            result * result * valid,
            branch * branch * valid,
            out_grad * vhat,
            out_grad,
        ]

    keep_sums(stat_ref, over_slots(share, width, 4, body))


def middle_back_kernel(row, count, scalars, *refs):
    addends = refs[:count]
    sum_ref, middle_ref, cot_ref, gains, carry_ref, grad_ref, stat_ref = refs[count:]
    share, width = sum_ref.shape

    def body(rows, start, tile):
        normed_grad = added(addends, rows)
        mhat, inverse = normalize(middle_ref[rows, :])
        out_grad = cot_ref[0, rows, :].astype(F32) * valid_rows(scalars, row, start, tile)
        carry = out_grad + values_back(normed_grad, gains[2:3, :], mhat, inverse)
        carry_ref[rows, :] = carry
        ahat, inverse = normalize(sum_ref[rows, :])
        grad_ref[rows, :] = values_back(carry, gains[1:2, :], ahat, inverse).astype(B16)
        return [normed_grad * mhat, normed_grad, carry * ahat, carry]

    keep_sums(stat_ref, over_slots(share, width, 4, body))


def first_back_kernel(row, count, scalars, *refs):
    addends = refs[:count]
    x_ref, carry_ref, gains, out_ref, stat_ref = refs[count:]
    share, width = out_ref.shape

    def body(rows, start, tile):
        grad = added(addends, rows)
        vhat, inverse = normalize(x_ref[0, rows, :].astype(F32))
        back = values_back(grad, gains[0:1, :], vhat, inverse)
        out_ref[rows, :] = (carry_ref[rows, :] + back).astype(B16)
        return [grad * vhat, grad]

    keep_sums(stat_ref, over_slots(share, width, 2, body))


def small_kernel(row_count, share, scalars, *refs):
    firsts, middles, lasts, backs = (
        refs[i * row_count : (i + 1) * row_count] for i in range(4)
    )
    out_ref = refs[4 * row_count]
    width = out_ref.shape[1]
    spots = ((firsts, 0), (backs, 2), (backs, 0), (lasts, 2))
    spots += ((firsts, 1), (backs, 3), (backs, 1), (lasts, 3))
    for index, (source, line) in enumerate(spots):
        total = source[0][line : line + 1, :]
        for ref in source[1:]:
            total = total + ref[line : line + 1, :]
        out_ref[index : index + 1, :] = total
    lane = lax.broadcasted_iota(jnp.int32, (1, width), 1)
    totals = [jnp.zeros((1, width), F32)] * GROUPS
    for row in range(row_count):
        count = jnp.clip(scalars[LENGTH + row] - scalars[BASE], 0, share).astype(F32)
        values = jnp.where(lane == 3, count, 0.0)
        sources = (lasts[row][0:1, :], middles[row][0:1, :], lasts[row][1:2, :])
        for index, source in enumerate(sources):
            values = jnp.where(lane == index, jnp.sum(source, axis=1, keepdims=True), values)
        group = scalars[LENGTH + row_count + row]
        for index in range(GROUPS):
            totals[index] = totals[index] + jnp.where(group == index, values, 0.0)
    for index, total in enumerate(totals):
        out_ref[8 + index : 9 + index, :] = total
    out_ref[12:16, :] = jnp.zeros((4, width), F32)


def swap_core(value):
    return lax.ppermute(value, "tensor", [(0, 1), (1, 0), (2, 3), (3, 2)])


def swap_chip(value):
    return lax.ppermute(value, "tensor", [(0, 2), (2, 0), (1, 3), (3, 1)])


class Row:
    def __init__(self, index, order, split, scalars, tokens, cotangent, gains, biases, pairs):
        self.index, self.order, self.split, self.scalars = index, order, split, scalars
        self.tokens, self.cotangent = tokens, cotangent
        self.gains, self.biases = gains, biases
        self.shape = tokens.shape[1:]
        self.count = 2 if split else 1
        self.projected, self.slope = [], []
        self.all = {name: [] for name in ("attn_in", "act", "ffn_in", "ffn_grad")}
        self.all.update(hidden_grad=[], attn_grad=[])
        self.projected_grad = [None] * pairs
        self.other_heads = [None] * pairs

    def gather(self, own):
        if self.split:
            return [own, swap_chip(own)]
        return [lax.all_gather(own, "tensor", axis=0, tiled=True)]

    def reduce(self, own, far):
        if self.split:
            return [own, swap_chip(far)]
        return [lax.psum_scatter(own, "tensor", scatter_dimension=0, tiled=True)]

    def keep(self, name, values):
        own = values[0]
        pair = [own]
        if self.split:
            pair += self.order.soon([swap_core(values[-1])])
        self.all[name].append(pair)

    def over_row(self, kernel, name, inputs, outs):
        addends = self.order.enter(*self.addends)
        inputs = [*addends, *inputs]
        row = pl.BlockSpec((1, *self.shape), lambda i, s: (self.index, 0, 0))
        specs = [row if v.ndim == 3 else whole(v.shape) for v in inputs]
        return call(
            functools.partial(kernel, self.index, len(addends)),
            name,
            self.scalars,
            inputs,
            outs,
            specs,
        )

    def project(self, part, ws):
        (x,) = self.order.enter(self.attn_in[part])
        own, *other = project(self.scalars, x, ws)
        self.order.leave(own, *other)
        self.projected += [own, *[swap_core(v) for v in other]]
        self.keep("attn_in", [x])

    def attend(self):
        projected = self.order.enter(*self.projected)
        *self.attended, self.lse = attend(self.scalars, self.index, projected)
        self.order.leave(*self.attended)
        self.heads = [self.attended[0]] + [swap_core(v) for v in self.attended[1:]]

    def out_project(self, ws):
        xs = self.order.enter(*self.heads)
        own, *far = out_project(self.scalars, xs, ws)
        self.order.leave(own, *far)
        self.addends = self.reduce(own, *(far or [None]))

    def middle(self):
        self.attn_sum, self.mid, normed, self.stat_middle = self.over_row(
            middle_kernel,
            "middle",
            [self.tokens, self.gains, self.biases],
            [(self.shape, F32)] * 2 + [(self.shape, B16), ((1, self.shape[1]), F32)],
        )
        self.order.leave(normed)
        self.ffn_in = self.gather(normed)

    def feed(self, part, ups, downs):
        (x,) = self.order.enter(self.ffn_in[part])
        act, slope, out = feed(self.scalars, x, ups, downs, B16 if part else F32)
        self.order.leave(out)
        self.keep("act", act)
        self.keep("ffn_in", [x])
        self.slope.append(slope)
        if part == 0:
            self.own = out
        if part == len(self.ffn_in) - 1:
            self.addends = self.reduce(self.own, out)

    def last(self):
        self.output, grad, self.stat_last = self.over_row(
            last_kernel,
            "last",
            [self.mid, self.cotangent, self.gains, self.biases],
            [(self.shape, B16)] * 2 + [((4, self.shape[1]), F32)],
        )
        self.order.leave(grad)
        self.ffn_grad = self.gather(grad)

    def feed_back(self, part, ups, downs):
        (x,) = self.order.enter(self.ffn_grad[part])
        grad, out = feed_back(
            self.scalars, x, self.slope[part], ups, downs, B16 if part else F32
        )
        self.order.leave(out)
        self.keep("hidden_grad", grad)
        self.keep("ffn_grad", [x])
        if part == 0:
            self.own = out
        if part == len(self.ffn_grad) - 1:
            self.addends = self.reduce(self.own, out)

    def middle_back(self):
        self.carry, grad, self.stat_back = self.over_row(
            middle_back_kernel,
            "middle_back",
            [self.attn_sum, self.mid, self.cotangent, self.gains],
            [(self.shape, F32), (self.shape, B16), ((4, self.shape[1]), F32)],
        )
        self.order.leave(grad)
        self.attn_grad = self.gather(grad)

    def out_back(self, ws):
        xs = self.order.enter(*self.attn_grad)
        own, *other = out_back(self.scalars, xs, ws)
        self.order.leave(own, *other)
        self.attended_grad = [own] + [swap_core(v) for v in other]
        for x in xs:
            self.keep("attn_grad", [x])

    def attend_back(self, pair):
        grads = self.order.enter(*self.attended_grad)
        out = attend_back(
            self.scalars, self.index, self.projected, self.attended, grads, self.lse, pair
        )
        self.projected_grad[pair] = out
        self.order.leave(*out)
        if self.split:
            self.other_heads[pair : pair + 1] = self.order.soon([swap_core(out[1])])

    def project_back(self, ws):
        sides = [[grad[0] for grad in self.projected_grad]]
        if self.split:
            sides.append(self.other_heads)
        flat = self.order.enter(*[v for side in sides for v in side])
        pairs = len(self.projected_grad)
        sides = [flat[i * pairs : (i + 1) * pairs] for i in range(len(sides))]
        own, *far = project_back(self.scalars, sides, ws)
        self.order.leave(own, *far)
        self.addends = self.reduce(own, *(far or [None]))

    def first_back(self):
        self.input_grad, self.stat_first = self.over_row(
            first_back_kernel,
            "first_back",
            [self.tokens, self.carry, self.gains],
            [(self.shape, B16), ((2, self.shape[1]), F32)],
        )
        self.order.leave(self.input_grad)


def doubling(values, axis, step):
    size = lax.axis_size(axis)
    return values + lax.ppermute(values, axis, [(i, i ^ step) for i in range(size)])


def per_device(tokens, cotangent, lengths, groups, w_qkv, w_out, w_up, w_down, gains, biases):
    row_count, share, width = tokens.shape
    t_size, d_size = lax.axis_size("tensor"), lax.axis_size("dp")
    pairs = w_qkv.shape[2] // 128
    split = t_size == 4 and share % 16 == 0
    staged = d_size == 8
    t, d = lax.axis_index("tensor"), lax.axis_index("dp")
    both = lambda w: [w, swap_core(w)] if split else [w]
    qkvs = [w.transpose(1, 0, 2) for w in both(w_qkv)]
    outs, ups, downs = both(w_out), both(w_up), both(w_down)
    parts = range(2 if split else 1)
    spots = jnp.stack([t * share, t, d // 2, d % 2]).astype(jnp.int32)
    scalars = jnp.concatenate([spots, lengths, groups])
    order = Order()
    rows = [
        Row(r, order, split, scalars, tokens, cotangent, gains, biases, pairs)
        for r in range(row_count)
    ]
    normed = call(
        first_kernel,
        "first",
        scalars,
        [tokens, gains, biases],
        [((share, width), B16)] * row_count,
    )
    order.leave(*normed)
    for row, own in zip(rows, normed):
        row.attn_in = row.gather(own)

    def listed(values):
        return [v for value in values for v in value]

    def kept(name):
        return [pair[i] for row in rows for i in range(row.count) for pair in row.all[name]]

    def started(out):
        order.leave(*out)
        return DpSum(scalars, order, *out) if staged else out[0]

    def summed(lefts, rights):
        values = order.enter(*lefts, *rights)
        count = len(lefts)
        return started(outer_sum(scalars, values[:count], values[count:], staged))

    def heads_summed(pair, attended):
        products = [(listed(row.projected_grad[pair] for row in rows), kept("attn_in"))]
        if attended:
            products.append((listed(row.attended for row in rows), kept("attn_grad")))
        values = list(order.enter(*[v for two in products for side in two for v in side]))
        again = []
        for two in products:
            again.append([[values.pop(0) for _ in side] for side in two])
        return started(head_outer(scalars, again, staged))

    def tick(*totals):
        if staged:
            for total in totals:
                next(total.steps, None)

    def placed(total):
        out = place(scalars, total.pieces())
        order.leave(out)
        return out

    lead, *others = rows
    lead.project(0, qkvs)
    for row in others:
        row.project(0, qkvs)
    if split:
        lead.project(1, qkvs)
    lead.attend()
    if split:
        for row in others:
            row.project(1, qkvs)
    lead.out_project(outs)
    for row in others:
        row.attend()
    lead.middle()
    for row in others:
        row.out_project(outs)
    lead.feed(0, ups, downs)
    if split:
        lead.feed(1, ups, downs)
    for row in others:
        row.middle()
        row.feed(0, ups, downs)
    lead.last()
    lead.feed_back(0, ups, downs)
    if split:
        for row in others:
            row.feed(1, ups, downs)
    if split:
        lead.feed_back(1, ups, downs)
    for row in others:
        row.last()
        row.feed_back(0, ups, downs)
    lead.middle_back()
    other = others[0]

    def attend_back(row, pair):
        if pair < pairs:
            row.attend_back(pair)

    def head_sum(pair):
        if pair < pairs:
            sums["Q" if pair else "P"] = heads_summed(pair, pair == 0)

    def small_sums():
        stats = [row.stat_first for row in rows] + [row.stat_middle for row in rows]
        stats += [row.stat_last for row in rows] + [row.stat_back for row in rows]
        (values,) = call(
            functools.partial(small_kernel, row_count, share),
            "small",
            scalars,
            list(order.enter(*stats)),
            [((16, width), F32)],
        )
        order.leave(values)
        sums["S"] = values

    powers = t_size & (t_size - 1) == 0 and d_size & (d_size - 1) == 0
    hops = [("tensor", 1 << k) for k in range(t_size.bit_length() - 1)]
    hops += [("dp", 1 << k) for k in range(1, d_size.bit_length() - 1)] + [("dp", 1)]

    def hop():
        axis, step = hops.pop(0)
        values = doubling(sums["S"], axis, step)
        if hops:
            (values,) = order.enter(values)
            order.leave(values)
        sums["S"] = values

    sums, placed_sums = {}, {}
    stages = {
        "FB1": lambda: other.feed_back(1, ups, downs) if split else None,
        "OB0": lambda: lead.out_back(outs),
        "OB1": lambda: other.out_back(outs),
        "WD": lambda: sums.update(D=summed(kept("act"), kept("ffn_grad"))),
        "WU": lambda: sums.update(U=summed(kept("ffn_in"), kept("hidden_grad"))),
        "MB1": other.middle_back,
        "AB00": lambda: attend_back(lead, 0),
        "AB01": lambda: attend_back(lead, 1),
        "AB10": lambda: attend_back(other, 0),
        "AB11": lambda: attend_back(other, 1),
        "HP": lambda: head_sum(0),
        "HQ": lambda: head_sum(1),
        "PB0": lambda: lead.project_back(qkvs),
        "PB1": lambda: other.project_back(qkvs),
        "FL0": lead.first_back,
        "FL1": other.first_back,
        "SM": small_sums,
    }
    for stage in STAGES:
        if stage in stages:
            stages[stage]()
        elif stage == "S":
            if powers and hops:
                hop()
        elif staged and stage in ("PD", "PU"):
            placed_sums[stage] = placed(sums[stage[1]])
        elif staged and stage in sums:
            tick(sums[stage])
    while powers and hops:
        hop()
    small = sums["S"] if powers else lax.psum(sums["S"], ("dp", "tensor"))
    heads = [sums[name] for name in ("P", "Q") if name in sums]
    if staged:
        grad_down, grad_up = placed_sums["PD"], placed_sums["PU"]
        pieces = heads[0].pieces()
        grad_qkv, grad_out = place_heads(scalars, pieces, 0, pairs, None)
        order.leave(grad_out)
        for pair in range(1, pairs):
            pieces = heads[pair].pieces()
            (grad_qkv,) = place_heads(scalars, pieces, pair, pairs, grad_qkv)
        grad_qkv = grad_qkv.transpose(1, 0, 2)
    else:
        grad_down, grad_up, *blocks = [
            v.astype(F32) for v in lax.psum((sums["D"], sums["U"], *heads), "dp")
        ]
        grad_out = blocks[0][384:]
        blocks = [grad[:384].reshape(3, 128, width) for grad in blocks]
        grad_qkv = jnp.concatenate(blocks, axis=1).transpose(2, 0, 1)
    group = small[8 : 8 + GROUPS]
    group_rms = jnp.sqrt(group[:, :3] / (group[:, 3:4] * width))
    return (
        jnp.stack([row.output for row in rows]),
        jnp.stack([row.input_grad for row in rows]),
        grad_qkv,
        grad_out,
        grad_up,
        grad_down,
        small[:4],
        small[4:8],
        group_rms,
    )


def solution(mesh):
    placed = (
        P("dp", "tensor", None),
        P("dp", "tensor", None),
        P("dp"),
        P("dp"),
        P(None, None, "tensor"),
        P("tensor", None),
        P(None, "tensor"),
        P("tensor", None),
        P(),
        P(),
    )
    return jax.shard_map(
        per_device,
        mesh=mesh,
        in_specs=placed,
        out_specs=(
            P("dp", "tensor", None),
            P("dp", "tensor", None),
            P(None, None, "tensor"),
            P("tensor", None),
            P(None, "tensor"),
            P("tensor", None),
            P(),
            P(),
            P(),
        ),
        check_vma=False,
    )
```

```python
import functools

import jax
import jax.numpy as jnp
from jax import lax
from jax.experimental import pallas as pl
from jax.experimental.pallas import tpu as pltpu
from jax.sharding import PartitionSpec as P

HEAD_DIM = 64
GROUPS = 4
MIN_LENGTH = 544
F32 = jnp.float32
B16 = jnp.bfloat16

epsilon = 1e-05
negative_fill = -1e30
log2_e = 1.4426950408889634
gelu_scale = 0.7978845608028654
gelu_cubic = 0.044715

BASE, TENSOR, Z, X, LENGTH = 0, 1, 2, 3, 4


STAGES = (
    "FB1",
    "OB0",
    "WD",
    "WU",
    "MB1",
    "AB00",
    "AB01",
    "D",
    "OB1",
    "AB10",
    "D",
    "HP",
    "U",
    "PB0",
    "D",
    "AB11",
    "U",
    "HQ",
    "D",
    "PB1",
    "P",
    "Q",
    "U",
    "D",
    "P",
    "U",
    "FL0",
    "P",
    "Q",
    "U",
    "FL1",
    "PD",
    "Q",
    "P",
    "SM",
    "S",
    "P",
    "Q",
    "S",
    "Q",
    "S",
    "S",
    "S",
    "PU",
)


def nt(left, right):
    return lax.dot_general(
        left, right, (((1,), (1,)), ((), ())), preferred_element_type=F32
    )


def nn(left, right):
    return lax.dot_general(
        left, right, (((1,), (0,)), ((), ())), preferred_element_type=F32
    )


def tn(left, right):
    return lax.dot_general(
        left, right, (((0,), (0,)), ((), ())), preferred_element_type=F32
    )


def tiles(extent, size):
    return [(start, min(size, extent - start)) for start in range(0, extent, size)]


def whole(shape):
    return pl.BlockSpec(shape, lambda *_: (0,) * len(shape))


def once(shape):
    return pl.BlockSpec(
        shape, lambda *_: (0,) * len(shape), pipeline_mode=pl.Buffered(buffer_count=1)
    )


def anywhere():
    return pl.BlockSpec(memory_space=pl.ANY)


def call(kernel, name, scalars, inputs, outs, in_specs=None, out_specs=None, grid=(1,), scratch=(), limit=10, flops=0, aliases={}):
    values = sum(v.size for v in inputs)
    in_specs = in_specs or [once(v.shape) for v in inputs]
    out_specs = out_specs or [whole(shape) for shape, _ in outs]
    return list(
        pl.pallas_call(
            kernel,
            out_shape=[jax.ShapeDtypeStruct(shape, dtype) for shape, dtype in outs],
            grid_spec=pltpu.PrefetchScalarGridSpec(
                num_scalar_prefetch=1,
                grid=grid,
                in_specs=in_specs,
                out_specs=out_specs,
                scratch_shapes=list(scratch),
            ),
            input_output_aliases=aliases,
            compiler_params=pltpu.CompilerParams(
                dimension_semantics=("arbitrary",) * len(grid), vmem_limit_bytes=limit << 20
            ),
            cost_estimate=pl.CostEstimate(
                flops=flops // 16, bytes_accessed=values // 16, transcendentals=0
            ),
            name=name,
        )(scalars, *inputs)
    )


def lane_half(shape, half):
    return (lax.broadcasted_iota(jnp.int32, shape, 1) // HEAD_DIM) == half


def mask_tile(scores, query_start, length):
    key_index = lax.broadcasted_iota(jnp.int32, scores.shape, 0)
    query_index = query_start + lax.broadcasted_iota(jnp.int32, scores.shape, 1)
    allowed = key_index <= query_index
    if scores.shape[0] > MIN_LENGTH:
        allowed = allowed & (key_index < length)
    return jnp.where(allowed, scores, negative_fill)


def place_of(scalars, parts, number, chunk):
    if parts == 1:
        return 0
    return pl.multiple_of(lax.bitwise_xor(scalars[TENSOR], number) * chunk, 16)


def halves_of(refs, number, chunk):
    return refs[number % len(refs)].at[pl.ds(number // len(refs) * chunk, chunk), :]


def attend_kernel(row, chunk, parts, query_tile, scalars, *refs):
    queries, keys, values = (refs[i * parts : (i + 1) * parts] for i in range(3))
    count = 1 if parts == 1 else 2
    outputs = refs[3 * parts : 3 * parts + count]
    lse_ref, q_ref, k_ref, v_ref, vt_ref, ot_ref = refs[3 * parts + count :]
    slots = q_ref.shape[0]
    length = scalars[LENGTH + row]
    for number in range(parts):
        target = pl.ds(place_of(scalars, parts, number, chunk), chunk)
        q_ref[target, :] = queries[number][...]
        k_ref[target, :] = keys[number][...]
        v_ref[target, :] = values[number][...]
    vt_ref[...] = v_ref[...].T
    scale = log2_e / HEAD_DIM**0.5
    for q0, qn in tiles(slots, query_tile):
        extent = q0 + qn
        for half in (0, 1):
            query = q_ref[q0 : q0 + qn, :]
            query = jnp.where(lane_half(query.shape, half), query, jnp.zeros_like(query))
            scores = mask_tile(nt(k_ref[0:extent, :], query), q0, length)
            top = jnp.max(scores, axis=0, keepdims=True)
            weights = jnp.exp2((scores - top) * scale)
            total = jnp.sum(weights, axis=0, keepdims=True)
            lanes = slice(half * HEAD_DIM, half * HEAD_DIM + HEAD_DIM)
            out_t = nn(vt_ref[lanes, 0:extent], weights.astype(B16))
            ot_ref[lanes, q0 : q0 + qn] = out_t * (1.0 / total)
            lse_ref[half, :, q0 : q0 + qn] = top * scale + jnp.log2(total)
    q_ref[...] = ot_ref[...].T.astype(B16)
    for number in range(parts):
        source = pl.ds(place_of(scalars, parts, number, chunk), chunk)
        halves_of(outputs, number, chunk)[...] = q_ref[source, :]


def column(rows, position):
    return pl.BlockSpec((rows, 128), position)


def attend(scalars, row, projected):
    parts = len(projected)
    chunk, width = projected[0].shape
    pairs = width // 384
    slots = chunk * parts
    count = 1 if parts == 1 else 2
    columns = []
    for kind in range(3):
        spot = column(chunk, lambda p, s, kind=kind: (0, kind * pairs + p))
        columns += [spot] * parts
    return call(
        functools.partial(attend_kernel, row, chunk, parts, 512),
        "attend",
        scalars,
        [*projected, *projected, *projected],
        [((slots // count, pairs * 128), B16)] * count + [((2 * pairs, 1, slots), F32)],
        columns,
        [column(slots // count, lambda p, s: (0, p))] * count
        + [pl.BlockSpec((2, 1, slots), lambda p, s: (p, 0, 0))],
        (pairs,),
        [pltpu.VMEM((slots, 128), B16)] * 3
        + [pltpu.VMEM((128, slots), B16), pltpu.VMEM((128, slots), F32)],
        limit=14,
        flops=4 * slots * slots * 128 * pairs,
    )


def attend_back_kernel(row, chunk, parts, query_tile, scalars, *refs):
    queries, keys, values = (refs[i * parts : (i + 1) * parts] for i in range(3))
    count = 1 if parts == 1 else 2
    refs = refs[3 * parts :]
    attended, grads, lse_ref = refs[:count], refs[count : 2 * count], refs[2 * count]
    outputs = refs[2 * count + 1 : 3 * count + 1]
    q_ref, k_ref, v_ref, g_ref, kt_ref, inner_ref, dk_ref, dv_ref, dqt_ref, t_ref = refs[
        3 * count + 1 :
    ]
    slots = q_ref.shape[0]
    half = pl.program_id(0)
    length = scalars[LENGTH + row]

    @pl.when(half == 0)
    def _():
        for number in range(parts):
            target = pl.ds(place_of(scalars, parts, number, chunk), chunk)
            grad = halves_of(grads, number, chunk)[...]
            out = halves_of(attended, number, chunk)[...]
            q_ref[target, :] = queries[number][...]
            k_ref[target, :] = keys[number][...]
            v_ref[target, :] = values[number][...]
            g_ref[target, :] = grad
            t_ref[target, :] = out.astype(F32) * grad.astype(F32)
        kt_ref[...] = k_ref[...].T
        products = t_ref[...].T
        inner_ref[0:1, :] = jnp.sum(products[0:HEAD_DIM], axis=0, keepdims=True)
        inner_ref[1:2, :] = jnp.sum(products[HEAD_DIM:], axis=0, keepdims=True)
        dk_ref[...] = jnp.zeros_like(dk_ref)
        dv_ref[...] = jnp.zeros_like(dv_ref)

    scale = log2_e / HEAD_DIM**0.5
    base = pl.multiple_of(half * HEAD_DIM, HEAD_DIM)
    for q0, qn in tiles(slots, query_tile):
        extent = q0 + qn
        keep = lane_half((qn, 128), half)
        query = q_ref[q0 : q0 + qn, :]
        query = jnp.where(keep, query, jnp.zeros_like(query))
        grad = g_ref[q0 : q0 + qn, :]
        grad = jnp.where(keep, grad, jnp.zeros_like(grad))
        lse = lse_ref[0, :, q0 : q0 + qn]
        inner = jnp.where(
            half == 0, inner_ref[0:1, q0 : q0 + qn], inner_ref[1:2, q0 : q0 + qn]
        )
        scores = mask_tile(nt(k_ref[0:extent, :], query), q0, length)
        probs = jnp.exp2(scores * scale - lse)
        dv_ref[0:extent, :] += nn(probs.astype(B16), grad)
        probs_grad = nt(v_ref[0:extent, :], grad)
        scores_grad = (probs * (probs_grad - inner)).astype(B16)
        dk_ref[0:extent, :] += nn(scores_grad, query)
        dqt_ref[pl.ds(base, HEAD_DIM), q0 : q0 + qn] = nn(
            kt_ref[pl.ds(base, HEAD_DIM), 0:extent], scores_grad
        )

    @pl.when(half == 1)
    def _():
        factor = 1.0 / HEAD_DIM**0.5
        q_ref[...] = (dqt_ref[...].T * factor).astype(B16)
        k_ref[...] = (dk_ref[...] * factor).astype(B16)
        v_ref[...] = dv_ref[...].astype(B16)
        for number in range(parts):
            source = pl.ds(place_of(scalars, parts, number, chunk), chunk)
            target = halves_of(outputs, number, chunk)
            target[:, 0:128] = q_ref[source, :]
            target[:, 128:256] = k_ref[source, :]
            target[:, 256:384] = v_ref[source, :]


def attend_back(scalars, row, projected, attended, grads, lse, pair):
    parts = len(projected)
    chunk, width = projected[0].shape
    pairs = width // 384
    slots = chunk * parts
    count = len(attended)
    rows = slots // count
    columns = []
    for kind in range(3):
        columns += [column(chunk, lambda h, s, kind=kind: (0, kind * pairs + pair))] * parts
    columns += [column(rows, lambda h, s: (0, pair))] * (2 * count)
    columns += [pl.BlockSpec((1, 1, slots), lambda h, s: (2 * pair + h, 0, 0))]
    return call(
        functools.partial(attend_back_kernel, row, chunk, parts, 384),
        "attend_back",
        scalars,
        [*projected, *projected, *projected, *attended, *grads, lse],
        [((rows, 384), B16)] * count,
        columns,
        [whole((rows, 384))] * count,
        (2,),
        [pltpu.VMEM((slots, 128), B16)] * 4
        + [pltpu.VMEM((128, slots), B16), pltpu.VMEM((8, slots), F32)]
        + [pltpu.VMEM((slots, 128), F32)] * 2
        + [pltpu.VMEM((128, slots), F32), pltpu.VMEM((slots, 128), F32)],
        limit=14,
        flops=10 * slots * slots * 128,
    )


def sum_of(terms):
    total = terms[0]
    for term in terms[1:]:
        total = total + term
    return total


def project_kernel(count, scalars, x_ref, *refs):
    for w_ref, out_ref in zip(refs[:count], refs[count:]):
        cols = w_ref.shape[2]
        for kind in range(3):
            columns = slice(kind * cols, kind * cols + cols)
            out_ref[:, columns] = nn(x_ref[...], w_ref[kind]).astype(B16)


def project(scalars, x, ws):
    rows, depth = x.shape
    cols = ws[0].shape[2]
    return call(
        functools.partial(project_kernel, len(ws)),
        "project",
        scalars,
        [x, *ws],
        [((rows, 3 * cols), B16)] * len(ws),
        flops=6 * rows * depth * cols * len(ws),
    )


def out_kernel(count, scalars, *refs):
    xs, ws, outs = refs[:count], refs[count : 2 * count], refs[2 * count :]
    n = outs[0].shape[0]
    for index, out in enumerate(outs):
        rows = slice(index * n, index * n + n)
        total = sum_of([nn(x[rows, :], w[...]) for x, w in zip(xs, ws)])
        out[...] = total.astype(out.dtype)


def partial_shapes(share, width, split):
    return [((share, width), F32)] + ([((share, width), B16)] if split else [])


def out_project(scalars, xs, ws):
    split = len(ws) == 2
    rows, depth = xs[0].shape
    width = ws[0].shape[1]
    return call(
        functools.partial(out_kernel, len(ws)),
        "out_project",
        scalars,
        [*xs, *ws],
        partial_shapes(rows // len(ws), width, split),
        flops=2 * rows * depth * width * len(ws),
    )


def feed_kernel(count, scalars, x_ref, *refs):
    ups, downs, refs = refs[:count], refs[count : 2 * count], refs[2 * count :]
    acts, slopes, out_ref = refs[:count], refs[count : 2 * count], refs[2 * count]
    for start, size in tiles(x_ref.shape[0], 272):
        rows = slice(start, start + size)
        terms = []
        for up, down, act_ref, slope_ref in zip(ups, downs, acts, slopes):
            hidden = nn(x_ref[rows, :], up[...])
            square = hidden * hidden
            bent = jnp.tanh(hidden * (gelu_scale + (gelu_scale * gelu_cubic) * square))
            upper = 0.5 + 0.5 * bent
            act = (hidden * upper).astype(B16)
            act_ref[rows, :] = act
            slope = upper + hidden * (1.0 - bent * bent) * (
                0.5 * gelu_scale + (1.5 * gelu_scale * gelu_cubic) * square
            )
            slope_ref[rows, :] = slope.astype(B16)
            terms.append(nn(act, down[...]))
        out_ref[rows, :] = sum_of(terms).astype(out_ref.dtype)


def feed(scalars, x, ups, downs, dtype):
    rows, depth = x.shape
    units, width = downs[0].shape
    count = len(ups)
    out = call(
        functools.partial(feed_kernel, count),
        "feed",
        scalars,
        [x, *ups, *downs],
        [((rows, units), B16)] * (2 * count) + [((rows, width), dtype)],
        limit=18,
        flops=4 * rows * depth * units * count,
    )
    return out[:count], out[count : 2 * count], out[2 * count]


def feed_back_kernel(count, scalars, x_ref, *refs):
    slopes, ups, downs = (refs[i * count : (i + 1) * count] for i in range(3))
    grads, out_ref = refs[3 * count : 4 * count], refs[4 * count]
    for start, size in tiles(x_ref.shape[0], 272):
        rows = slice(start, start + size)
        terms = []
        for slope, up, down, grad_ref in zip(slopes, ups, downs, grads):
            grad = nt(x_ref[rows, :], down[...]) * slope[rows, :].astype(F32)
            grad = grad.astype(B16)
            grad_ref[rows, :] = grad
            terms.append(nt(grad, up[...]))
        out_ref[rows, :] = sum_of(terms).astype(out_ref.dtype)


def feed_back(scalars, x, slopes, ups, downs, dtype):
    rows, width = x.shape
    depth, units = ups[0].shape
    count = len(ups)
    out = call(
        functools.partial(feed_back_kernel, count),
        "feed_back",
        scalars,
        [x, *slopes, *ups, *downs],
        [((rows, units), B16)] * count + [((rows, depth), dtype)],
        limit=18,
        flops=4 * rows * depth * units * count,
    )
    return out[:count], out[count]


def out_back_kernel(count, scalars, *refs):
    xs, ws, outs = refs[: len(refs) - 2 * count], refs[-2 * count : -count], refs[-count:]
    for w_ref, out_ref in zip(ws, outs):
        for index, x in enumerate(xs):
            n = x.shape[0]
            out_ref[index * n : index * n + n, :] = nt(x[...], w_ref[...]).astype(B16)


def out_back(scalars, xs, ws):
    rows, depth = len(xs) * xs[0].shape[0], xs[0].shape[1]
    cols = ws[0].shape[0]
    return call(
        functools.partial(out_back_kernel, len(ws)),
        "out_back",
        scalars,
        [*xs, *ws],
        [((rows, cols), B16)] * len(ws),
        flops=2 * rows * depth * cols * len(ws),
    )


def project_back_kernel(pairs, count, scalars, *refs):
    sides = [refs[i * pairs : (i + 1) * pairs] for i in range(count)]
    ws, outs = refs[pairs * count : (pairs + 1) * count], refs[(pairs + 1) * count :]
    n = outs[0].shape[0]
    for index, out in enumerate(outs):
        terms = []
        for grads, w_ref in zip(sides, ws):
            for kind in range(3):
                columns = [
                    grad[index * n : index * n + n, kind * 128 : kind * 128 + 128]
                    for grad in grads
                ]
                left = columns[0] if pairs == 1 else jnp.concatenate(columns, axis=1)
                terms.append(nt(left, w_ref[kind]))
        out[...] = sum_of(terms).astype(out.dtype)


def project_back(scalars, sides, ws):
    split = len(ws) == 2
    rows = sides[0][0].shape[0]
    depth, cols = ws[0].shape[1:]
    return call(
        functools.partial(project_back_kernel, len(sides[0]), len(ws)),
        "project_back",
        scalars,
        [v for side in sides for v in side] + list(ws),
        partial_shapes(rows // len(ws), depth, split),
        limit=12,
        flops=6 * rows * depth * cols * len(ws),
    )


def block_of(scalars, index, bits):
    if not bits:
        return index
    flips = [(index // 4) * bits[0], (index // 2 % 2) * bits[1], (index % 2) * bits[2]]
    owner = lax.bitwise_xor(2 * scalars[Z] + scalars[X], sum(flips))
    return 4 * lax.rem(owner, 2) + owner // 2


def gathered(pieces, target, sems, first):
    copies, start = [], 0
    for index, piece in enumerate(pieces):
        rows = piece.shape[0]
        spot = target.at[pl.ds(start, rows), :]
        copies.append(pltpu.make_async_copy(piece, spot, sems.at[first + index]))
        start += rows
    return copies


def outer_kernel(count, staged, scalars, *refs):
    lefts, rights = refs[:count], refs[count : 2 * count]
    outs, (left_ref, right_ref, sems) = refs[2 * count : -3], refs[-3:]
    step = pl.program_id(0)

    @pl.when(step == 0)
    def _():
        copies = gathered(lefts, left_ref, sems, 0) + gathered(rights, right_ref, sems, count)
        for copy in copies:
            copy.start()
        for copy in copies:
            copy.wait()

    if staged:
        spots = [block_of(scalars, 2 * step + i, (1, 2, 4)) for i in (0, 1)]
        columns = [pl.ds(pl.multiple_of(spot * 128, 128), 128) for spot in spots]
        left = jnp.concatenate([left_ref[:, c] for c in columns], axis=1)
    else:
        left = left_ref[:, pl.ds(pl.multiple_of(step * 256, 256), 256)]
    value = tn(left, right_ref[...]).astype(B16)
    if staged:

        @pl.when(step < 2)
        def _():
            outs[0][...] = value

        @pl.when(step >= 2)
        def _():
            outs[1][...] = value

    else:
        outs[0][...] = value


def outer_sum(scalars, lefts, rights, staged):
    slots = sum(left.shape[0] for left in lefts)
    height, width = lefts[0].shape[1], rights[0].shape[1]
    if staged:
        outs = [((height // 2, width), B16)] * 2
        specs = [
            pl.BlockSpec((256, width), lambda i, s: (jnp.minimum(i, 1), 0)),
            pl.BlockSpec((256, width), lambda i, s: (jnp.maximum(i - 2, 0), 0)),
        ]
    else:
        outs = [((height, width), B16)]
        specs = [pl.BlockSpec((256, width), lambda i, s: (i, 0))]
    inputs = [*lefts, *rights]
    return call(
        functools.partial(outer_kernel, len(lefts), staged),
        "outer_sum",
        scalars,
        inputs,
        outs,
        [anywhere() for _ in inputs],
        specs,
        (height // 256,),
        [pltpu.VMEM((slots, height), B16), pltpu.VMEM((slots, width), B16)]
        + [pltpu.SemaphoreType.DMA((len(inputs),))],
        limit=18,
        flops=2 * slots * height * width,
    )


def head_outer_kernel(counts, bits, scalars, *refs):
    staged = bits is not None
    products = []
    for left_count, right_count in counts:
        products.append((refs[:left_count], refs[left_count : left_count + right_count]))
        refs = refs[left_count + right_count :]
    outs, refs = refs[: 2 if staged else 1], refs[2 if staged else 1 :]
    buffers = [(refs[2 * i], refs[2 * i + 1]) for i in range(len(products))]
    total_ref, sems = refs[2 * len(products) :]
    step = pl.program_id(0)

    @pl.when(step == 0)
    def _():
        copies = []
        for sources, targets in zip(products, buffers):
            for pieces, target in zip(sources, targets):
                copies += gathered(pieces, target, sems, len(copies))
        for copy in copies:
            copy.start()
        for copy in copies:
            copy.wait()

    first = 0
    for left_ref, right_ref in buffers:
        right = right_ref[:, pl.ds(pl.multiple_of(step * 256, 256), 256)]
        height = left_ref.shape[1]
        total_ref[first : first + height, :] = tn(left_ref[...], right).astype(B16)
        first += height
    if staged:
        rows = total_ref.shape[0] // 8
        for index in range(8):
            source = pl.ds(pl.multiple_of(block_of(scalars, index, bits) * rows, 16), rows)
            at = index % 4 * rows
            outs[index // 4][at : at + rows, :] = total_ref[source, :]
    else:
        outs[0][...] = total_ref[...]


def head_outer(scalars, products, bits):
    inputs, counts, scratch = [], [], []
    height, width, flops = 0, products[0][1][0].shape[1], 0
    for lefts, rights in products:
        slots = sum(left.shape[0] for left in lefts)
        inputs += [*lefts, *rights]
        counts.append((len(lefts), len(rights)))
        scratch += [pltpu.VMEM((slots, lefts[0].shape[1]), B16)]
        scratch += [pltpu.VMEM((slots, width), B16)]
        height += lefts[0].shape[1]
        flops += 2 * slots * lefts[0].shape[1] * width
    parts = 1 if bits is None else 2
    return call(
        functools.partial(head_outer_kernel, counts, bits),
        "head_outer",
        scalars,
        inputs,
        [((height // parts, width), B16)] * parts,
        [anywhere() for _ in inputs],
        [pl.BlockSpec((height // parts, 256), lambda i, s: (0, i))] * parts,
        (width // 256,),
        scratch + [pltpu.VMEM((height, 256), B16), pltpu.SemaphoreType.DMA((len(inputs),))],
        limit=20,
        flops=flops,
    )


def halve_kernel(scalars, keep_ref, got_ref, *outs):
    rows = outs[0].shape[0]
    for index, out in enumerate(outs):
        at = slice(index * rows, index * rows + rows)
        out[...] = (keep_ref[at, :].astype(F32) + got_ref[at, :].astype(F32)).astype(B16)


def halves_sum(scalars, keep, got):
    rows, width = keep.shape
    return call(halve_kernel, "halve", scalars, [keep, got], [((rows // 2, width), B16)] * 2)


def place_blocks(scalars, pieces, bits):
    result = []
    for half, piece in enumerate(pieces):
        rows = piece.shape[0] // 4
        for index in range(4):
            value = piece[index * rows : index * rows + rows, :]
            result.append((value, block_of(scalars, 4 * half + index, bits)))
    return result


def place_kernel(scalars, *refs):
    pieces, (out_ref, buffer, sems) = refs[:2], refs[2:]
    rows = buffer.shape[1]
    copies = []
    for index, (value, spot) in enumerate(place_blocks(scalars, pieces, (1, 2, 4))):
        buffer[index] = value.astype(F32)
        target = out_ref.at[pl.ds(pl.multiple_of(spot * rows, rows), rows), :]
        copy = pltpu.make_async_copy(buffer.at[index], target, sems.at[index])
        copy.start()
        copies.append(copy)
    for copy in copies:
        copy.wait()


def place(scalars, pieces):
    rows, width = pieces[0].shape[0] // 4, pieces[0].shape[1]
    (out,) = call(
        place_kernel,
        "place",
        scalars,
        pieces,
        [((8 * rows, width), F32)],
        out_specs=[anywhere()],
        scratch=[pltpu.VMEM((8, rows, width), F32), pltpu.SemaphoreType.DMA((8,))],
    )
    return out


def place_heads_kernel(pair, bits, has_out, aliased, scalars, *refs):
    pieces, refs = refs[:2], refs[2 + aliased :]
    qkv_ref, refs = refs[0], refs[1:]
    out_ref, (rows_ref, buffer, sems) = refs[0] if has_out else None, refs[-3:]
    for value, spot in place_blocks(scalars, pieces, bits):
        rows = value.shape[0]
        rows_ref[pl.ds(pl.multiple_of(spot * rows, 16), rows), :] = value.astype(F32)
    copies = []
    if has_out:
        copies.append(
            pltpu.make_async_copy(
                rows_ref.at[pl.ds(384, rows_ref.shape[0] - 384), :], out_ref, sems.at[3]
            )
        )
        copies[-1].start()
    for kind in range(3):
        buffer[kind] = rows_ref[kind * 128 : kind * 128 + 128, :].T
        target = qkv_ref.at[kind, :, pl.ds(pair * 128, 128)]
        copies.append(pltpu.make_async_copy(buffer.at[kind], target, sems.at[kind]))
        copies[-1].start()
    for copy in copies:
        copy.wait()


def place_heads(scalars, pieces, pair, pairs, into, bits):
    total, width = 2 * pieces[0].shape[0], pieces[0].shape[1]
    has_out = total > 384
    inputs = list(pieces) + ([] if into is None else [into])
    in_specs = [once(v.shape) for v in pieces]
    in_specs += [] if into is None else [anywhere()]
    outs = [((3, width, pairs * 128), F32)]
    outs += [((total - 384, width), F32)] if has_out else []
    return call(
        functools.partial(place_heads_kernel, pair, bits, has_out, int(into is not None)),
        "place_heads",
        scalars,
        inputs,
        outs,
        in_specs,
        [anywhere() for _ in outs],
        scratch=[
            pltpu.VMEM((total, width), F32),
            pltpu.VMEM((3, width, 128), F32),
            pltpu.SemaphoreType.DMA((4,)),
        ],
        aliases={} if into is None else {3: 0},
    )


class DpSum:
    def __init__(self, scalars, order, bits, keep, send):
        self.scalars, self.order, self.bits, self.keep = scalars, order, bits, keep
        self.got = self.exchanged(send, bits[0])
        self.steps = self.run()

    def exchanged(self, value, bit):
        return lax.ppermute(value, "dp", [(i, i ^ bit) for i in range(8)])

    def entered(self):
        (got,) = self.order.enter(self.got)
        return got

    def run(self):
        keep, send = halves_sum(self.scalars, self.keep, self.entered())
        self.order.leave(keep, send)
        self.got = self.exchanged(send, self.bits[1])
        yield
        keep, send = halves_sum(self.scalars, keep, self.entered())
        self.order.leave(keep, send)
        self.got = self.exchanged(send, self.bits[2])
        yield
        total = (keep.astype(F32) + self.entered().astype(F32)).astype(B16)
        self.order.leave(total)
        for bit in self.bits[:0:-1]:
            self.got = self.exchanged(total, bit)
            yield
            total = jnp.concatenate([total, self.entered()], axis=0)
            self.order.leave(total)
        self.total = total
        self.got = self.exchanged(total, self.bits[0])
        yield

    def pieces(self):
        return [self.total, self.entered()]


class Order:
    def __init__(self):
        self.last, self.fresh, self.due = (), (), ()

    def enter(self, *values):
        count = len(values)
        values = lax.optimization_barrier(tuple(values) + self.last + self.due)
        self.due, self.fresh = self.fresh, ()
        return values[:count]

    def leave(self, *values):
        self.last = tuple(values)

    def soon(self, values):
        self.fresh = self.fresh + tuple(values)
        return list(values)


def normalize(values):
    center = values - jnp.mean(values, axis=-1, keepdims=True)
    inverse = lax.rsqrt(jnp.mean(center * center, axis=-1, keepdims=True) + epsilon)
    return center * inverse, inverse


def values_back(grad, gain, vhat, inverse):
    scaled = grad * gain
    mean_scaled = jnp.mean(scaled, axis=-1, keepdims=True)
    mean_product = jnp.mean(scaled * vhat, axis=-1, keepdims=True)
    return (scaled - mean_scaled - vhat * mean_product) * inverse


def added(refs, rows):
    total = refs[0][rows, :].astype(F32)
    for ref in refs[1:]:
        total = total + ref[rows, :].astype(F32)
    return total


def fold(values):
    return jnp.sum(values.reshape(-1, 8, values.shape[-1]), axis=0)


def over_slots(share, width, sums, body):
    tile = 16 if share % 16 == 0 else 8
    totals = [jnp.zeros((8, width), F32)] * sums
    for start in range(0, share, tile):
        terms = body(pl.ds(start, tile), start, tile)
        totals = [total + fold(term) for total, term in zip(totals, terms)]
    return totals


def valid_rows(scalars, row, start, tile):
    slot = scalars[BASE] + start + lax.broadcasted_iota(jnp.int32, (tile, 1), 0)
    return (slot < scalars[LENGTH + row]).astype(F32)


def keep_sums(ref, totals):
    for index, total in enumerate(totals):
        ref[index : index + 1, :] = jnp.sum(total, axis=0, keepdims=True)


def first_kernel(scalars, x_ref, gains, biases, *outs):
    share, width = outs[0].shape
    for row, out in enumerate(outs):

        def body(rows, start, tile, row=row, out=out):
            vhat, _ = normalize(x_ref[row, rows, :].astype(F32))
            out[rows, :] = (vhat * gains[0:1, :] + biases[0:1, :]).astype(B16)
            return []

        over_slots(share, width, 0, body)


def middle_kernel(row, count, scalars, *refs):
    addends = refs[:count]
    x_ref, gains, biases, sum_ref, middle_ref, normed_ref, stat_ref = refs[count:]
    share, width = sum_ref.shape

    def body(rows, start, tile):
        attn_sum = added(addends, rows)
        sum_ref[rows, :] = attn_sum
        vhat, _ = normalize(attn_sum)
        branch = vhat * gains[1:2, :] + biases[1:2, :]
        middle = x_ref[0, rows, :].astype(F32) + branch
        middle_ref[rows, :] = middle
        vhat, _ = normalize(middle)
        normed_ref[rows, :] = (vhat * gains[2:3, :] + biases[2:3, :]).astype(B16)
        return [branch * branch * valid_rows(scalars, row, start, tile)]

    keep_sums(stat_ref, over_slots(share, width, 1, body))


def last_kernel(row, count, scalars, *refs):
    addends = refs[:count]
    middle_ref, cot_ref, gains, biases, out_ref, grad_ref, stat_ref = refs[count:]
    share, width = out_ref.shape

    def body(rows, start, tile):
        vhat, inverse = normalize(added(addends, rows))
        branch = vhat * gains[3:4, :] + biases[3:4, :]
        result = middle_ref[rows, :] + branch
        out_ref[rows, :] = result.astype(B16)
        valid = valid_rows(scalars, row, start, tile)
        out_grad = cot_ref[0, rows, :].astype(F32) * valid
        grad_ref[rows, :] = values_back(out_grad, gains[3:4, :], vhat, inverse).astype(B16)
        return [
            result * result * valid,
            branch * branch * valid,
            out_grad * vhat,
            out_grad,
        ]

    keep_sums(stat_ref, over_slots(share, width, 4, body))


def middle_back_kernel(row, count, scalars, *refs):
    addends = refs[:count]
    sum_ref, middle_ref, cot_ref, gains, carry_ref, grad_ref, stat_ref = refs[count:]
    share, width = sum_ref.shape

    def body(rows, start, tile):
        normed_grad = added(addends, rows)
        mhat, inverse = normalize(middle_ref[rows, :])
        out_grad = cot_ref[0, rows, :].astype(F32) * valid_rows(scalars, row, start, tile)
        carry = out_grad + values_back(normed_grad, gains[2:3, :], mhat, inverse)
        carry_ref[rows, :] = carry
        ahat, inverse = normalize(sum_ref[rows, :])
        grad_ref[rows, :] = values_back(carry, gains[1:2, :], ahat, inverse).astype(B16)
        return [normed_grad * mhat, normed_grad, carry * ahat, carry]

    keep_sums(stat_ref, over_slots(share, width, 4, body))


def first_back_kernel(row, count, scalars, *refs):
    addends = refs[:count]
    x_ref, carry_ref, gains, out_ref, stat_ref = refs[count:]
    share, width = out_ref.shape

    def body(rows, start, tile):
        grad = added(addends, rows)
        vhat, inverse = normalize(x_ref[0, rows, :].astype(F32))
        back = values_back(grad, gains[0:1, :], vhat, inverse)
        out_ref[rows, :] = (carry_ref[rows, :] + back).astype(B16)
        return [grad * vhat, grad]

    keep_sums(stat_ref, over_slots(share, width, 2, body))


def small_kernel(row_count, share, scalars, *refs):
    firsts, middles, lasts, backs = (
        refs[i * row_count : (i + 1) * row_count] for i in range(4)
    )
    out_ref = refs[4 * row_count]
    width = out_ref.shape[1]
    spots = ((firsts, 0), (backs, 2), (backs, 0), (lasts, 2))
    spots += ((firsts, 1), (backs, 3), (backs, 1), (lasts, 3))
    for index, (source, line) in enumerate(spots):
        total = source[0][line : line + 1, :]
        for ref in source[1:]:
            total = total + ref[line : line + 1, :]
        out_ref[index : index + 1, :] = total
    lane = lax.broadcasted_iota(jnp.int32, (1, width), 1)
    totals = [jnp.zeros((1, width), F32)] * GROUPS
    for row in range(row_count):
        count = jnp.clip(scalars[LENGTH + row] - scalars[BASE], 0, share).astype(F32)
        values = jnp.where(lane == 3, count, 0.0)
        sources = (lasts[row][0:1, :], middles[row][0:1, :], lasts[row][1:2, :])
        for index, source in enumerate(sources):
            values = jnp.where(lane == index, jnp.sum(source, axis=1, keepdims=True), values)
        group = scalars[LENGTH + row_count + row]
        for index in range(GROUPS):
            totals[index] = totals[index] + jnp.where(group == index, values, 0.0)
    for index, total in enumerate(totals):
        out_ref[8 + index : 9 + index, :] = total
    out_ref[12:16, :] = jnp.zeros((4, width), F32)


def swap_core(value):
    return lax.ppermute(value, "tensor", [(0, 1), (1, 0), (2, 3), (3, 2)])


def swap_chip(value):
    return lax.ppermute(value, "tensor", [(0, 2), (2, 0), (1, 3), (3, 1)])


class Row:
    def __init__(self, index, order, split, scalars, tokens, cotangent, gains, biases, pairs):
        self.index, self.order, self.split, self.scalars = index, order, split, scalars
        self.tokens, self.cotangent = tokens, cotangent
        self.gains, self.biases = gains, biases
        self.shape = tokens.shape[1:]
        self.count = 2 if split else 1
        self.projected, self.slope = [], []
        self.all = {name: [] for name in ("attn_in", "act", "ffn_in", "ffn_grad")}
        self.all.update(hidden_grad=[], attn_grad=[])
        self.projected_grad = [None] * pairs
        self.other_heads = [None] * pairs

    def gather(self, own):
        if self.split:
            return [own, swap_chip(own)]
        return [lax.all_gather(own, "tensor", axis=0, tiled=True)]

    def reduce(self, own, far):
        if self.split:
            return [own, swap_chip(far)]
        return [lax.psum_scatter(own, "tensor", scatter_dimension=0, tiled=True)]

    def keep(self, name, values):
        own = values[0]
        pair = [own]
        if self.split:
            pair += self.order.soon([swap_core(values[-1])])
        self.all[name].append(pair)

    def over_row(self, kernel, name, inputs, outs):
        addends = self.order.enter(*self.addends)
        inputs = [*addends, *inputs]
        row = pl.BlockSpec((1, *self.shape), lambda i, s: (self.index, 0, 0))
        specs = [row if v.ndim == 3 else whole(v.shape) for v in inputs]
        return call(
            functools.partial(kernel, self.index, len(addends)),
            name,
            self.scalars,
            inputs,
            outs,
            specs,
        )

    def project(self, part, ws):
        (x,) = self.order.enter(self.attn_in[part])
        own, *other = project(self.scalars, x, ws)
        self.order.leave(own, *other)
        self.projected += [own, *[swap_core(v) for v in other]]
        self.keep("attn_in", [x])

    def attend(self):
        projected = self.order.enter(*self.projected)
        *self.attended, self.lse = attend(self.scalars, self.index, projected)
        self.order.leave(*self.attended)
        self.heads = [self.attended[0]] + [swap_core(v) for v in self.attended[1:]]

    def out_project(self, ws):
        xs = self.order.enter(*self.heads)
        own, *far = out_project(self.scalars, xs, ws)
        self.order.leave(own, *far)
        self.addends = self.reduce(own, *(far or [None]))

    def middle(self):
        self.attn_sum, self.mid, normed, self.stat_middle = self.over_row(
            middle_kernel,
            "middle",
            [self.tokens, self.gains, self.biases],
            [(self.shape, F32)] * 2 + [(self.shape, B16), ((1, self.shape[1]), F32)],
        )
        self.order.leave(normed)
        self.ffn_in = self.gather(normed)

    def feed(self, part, ups, downs):
        (x,) = self.order.enter(self.ffn_in[part])
        act, slope, out = feed(self.scalars, x, ups, downs, B16 if part else F32)
        self.order.leave(out)
        self.keep("act", act)
        self.keep("ffn_in", [x])
        self.slope.append(slope)
        if part == 0:
            self.own = out
        if part == len(self.ffn_in) - 1:
            self.addends = self.reduce(self.own, out)

    def last(self):
        self.output, grad, self.stat_last = self.over_row(
            last_kernel,
            "last",
            [self.mid, self.cotangent, self.gains, self.biases],
            [(self.shape, B16)] * 2 + [((4, self.shape[1]), F32)],
        )
        self.order.leave(grad)
        self.ffn_grad = self.gather(grad)

    def feed_back(self, part, ups, downs):
        (x,) = self.order.enter(self.ffn_grad[part])
        grad, out = feed_back(
            self.scalars, x, self.slope[part], ups, downs, B16 if part else F32
        )
        self.order.leave(out)
        self.keep("hidden_grad", grad)
        self.keep("ffn_grad", [x])
        if part == 0:
            self.own = out
        if part == len(self.ffn_grad) - 1:
            self.addends = self.reduce(self.own, out)

    def middle_back(self):
        self.carry, grad, self.stat_back = self.over_row(
            middle_back_kernel,
            "middle_back",
            [self.attn_sum, self.mid, self.cotangent, self.gains],
            [(self.shape, F32), (self.shape, B16), ((4, self.shape[1]), F32)],
        )
        self.order.leave(grad)
        self.attn_grad = self.gather(grad)

    def out_back(self, ws):
        xs = self.order.enter(*self.attn_grad)
        own, *other = out_back(self.scalars, xs, ws)
        self.order.leave(own, *other)
        self.attended_grad = [own] + [swap_core(v) for v in other]
        for x in xs:
            self.keep("attn_grad", [x])

    def attend_back(self, pair):
        grads = self.order.enter(*self.attended_grad)
        out = attend_back(
            self.scalars, self.index, self.projected, self.attended, grads, self.lse, pair
        )
        self.projected_grad[pair] = out
        self.order.leave(*out)
        if self.split:
            self.other_heads[pair : pair + 1] = self.order.soon([swap_core(out[1])])

    def project_back(self, ws):
        sides = [[grad[0] for grad in self.projected_grad]]
        if self.split:
            sides.append(self.other_heads)
        flat = self.order.enter(*[v for side in sides for v in side])
        pairs = len(self.projected_grad)
        sides = [flat[i * pairs : (i + 1) * pairs] for i in range(len(sides))]
        own, *far = project_back(self.scalars, sides, ws)
        self.order.leave(own, *far)
        self.addends = self.reduce(own, *(far or [None]))

    def first_back(self):
        self.input_grad, self.stat_first = self.over_row(
            first_back_kernel,
            "first_back",
            [self.tokens, self.carry, self.gains],
            [(self.shape, B16), ((2, self.shape[1]), F32)],
        )
        self.order.leave(self.input_grad)


def doubling(values, axis, step):
    size = lax.axis_size(axis)
    return values + lax.ppermute(values, axis, [(i, i ^ step) for i in range(size)])


def per_device(tokens, cotangent, lengths, groups, w_qkv, w_out, w_up, w_down, gains, biases):
    row_count, share, width = tokens.shape
    t_size, d_size = lax.axis_size("tensor"), lax.axis_size("dp")
    pairs = w_qkv.shape[2] // 128
    split = t_size == 4 and share % 16 == 0
    staged = d_size == 8
    t, d = lax.axis_index("tensor"), lax.axis_index("dp")
    both = lambda w: [w, swap_core(w)] if split else [w]
    qkvs = [w.transpose(1, 0, 2) for w in both(w_qkv)]
    outs, ups, downs = both(w_out), both(w_up), both(w_down)
    parts = range(2 if split else 1)
    spots = jnp.stack([t * share, t, d // 2, d % 2]).astype(jnp.int32)
    scalars = jnp.concatenate([spots, lengths, groups])
    order = Order()
    rows = [
        Row(r, order, split, scalars, tokens, cotangent, gains, biases, pairs)
        for r in range(row_count)
    ]
    normed = call(
        first_kernel,
        "first",
        lengths,
        [tokens, gains, biases],
        [((share, width), B16)] * row_count,
    )
    order.leave(*normed)
    for row, own in zip(rows, normed):
        row.attn_in = row.gather(own)

    def listed(values):
        return [v for value in values for v in value]

    def kept(name):
        return [pair[i] for row in rows for i in range(row.count) for pair in row.all[name]]

    head_bits = [(2, 1, 4), (1, 2, 4)][:pairs] if staged else [None] * pairs

    def started(out, bits):
        order.leave(*out)
        return DpSum(scalars, order, bits, *out) if staged else out[0]

    def summed(lefts, rights):
        values = order.enter(*lefts, *rights)
        count = len(lefts)
        out = outer_sum(scalars, values[:count], values[count:], staged)
        return started(out, (1, 2, 4))

    def heads_summed(pair, attended):
        products = [(listed(row.projected_grad[pair] for row in rows), kept("attn_in"))]
        if attended:
            products.append((listed(row.attended for row in rows), kept("attn_grad")))
        values = list(order.enter(*[v for two in products for side in two for v in side]))
        again = []
        for two in products:
            again.append([[values.pop(0) for _ in side] for side in two])
        return started(head_outer(scalars, again, head_bits[pair]), head_bits[pair])

    def tick(*totals):
        if staged:
            for total in totals:
                next(total.steps, None)

    def placed(total):
        out = place(scalars, total.pieces())
        order.leave(out)
        return out

    lead, *others = rows
    lead.project(0, qkvs)
    for row in others:
        row.project(0, qkvs)
    if split:
        lead.project(1, qkvs)
    lead.attend()
    if split:
        for row in others:
            row.project(1, qkvs)
    lead.out_project(outs)
    for row in others:
        row.attend()
    for row in others:
        row.out_project(outs)
    lead.middle()
    lead.feed(0, ups, downs)
    if split:
        lead.feed(1, ups, downs)
    for row in others:
        row.middle()
        row.feed(0, ups, downs)
    lead.last()
    lead.feed_back(0, ups, downs)
    if split:
        for row in others:
            row.feed(1, ups, downs)
    if split:
        lead.feed_back(1, ups, downs)
    for row in others:
        row.last()
        row.feed_back(0, ups, downs)
    lead.middle_back()
    other = others[0]

    def attend_back(row, pair):
        if pair < pairs:
            row.attend_back(pair)

    def head_sum(pair):
        if pair < pairs:
            sums["Q" if pair else "P"] = heads_summed(pair, pair == 0)

    def small_sums():
        stats = [row.stat_first for row in rows] + [row.stat_middle for row in rows]
        stats += [row.stat_last for row in rows] + [row.stat_back for row in rows]
        (values,) = call(
            functools.partial(small_kernel, row_count, share),
            "small",
            scalars,
            list(order.enter(*stats)),
            [((16, width), F32)],
        )
        order.leave(values)
        sums["S"] = values

    powers = t_size & (t_size - 1) == 0 and d_size & (d_size - 1) == 0
    hops = [("tensor", 1 << k) for k in range(t_size.bit_length() - 1)]
    hops += [("dp", 1 << k) for k in range(1, d_size.bit_length() - 1)] + [("dp", 1)]

    def hop():
        axis, step = hops.pop(0)
        values = doubling(sums["S"], axis, step)
        if hops:
            (values,) = order.enter(values)
            order.leave(values)
        sums["S"] = values

    sums, placed_sums = {}, {}
    stages = {
        "FB1": lambda: other.feed_back(1, ups, downs) if split else None,
        "OB0": lambda: lead.out_back(outs),
        "OB1": lambda: other.out_back(outs),
        "WD": lambda: sums.update(D=summed(kept("act"), kept("ffn_grad"))),
        "WU": lambda: sums.update(U=summed(kept("ffn_in"), kept("hidden_grad"))),
        "MB1": other.middle_back,
        "AB00": lambda: attend_back(lead, 0),
        "AB01": lambda: attend_back(lead, 1),
        "AB10": lambda: attend_back(other, 0),
        "AB11": lambda: attend_back(other, 1),
        "HP": lambda: head_sum(0),
        "HQ": lambda: head_sum(1),
        "PB0": lambda: lead.project_back(qkvs),
        "PB1": lambda: other.project_back(qkvs),
        "FL0": lead.first_back,
        "FL1": other.first_back,
        "SM": small_sums,
    }
    for stage in STAGES:
        if stage in stages:
            stages[stage]()
        elif stage == "S":
            if powers and hops:
                hop()
        elif staged and stage in ("PD", "PU"):
            placed_sums[stage] = placed(sums[stage[1]])
        elif staged and stage in sums:
            tick(sums[stage])
    while powers and hops:
        hop()
    small = sums["S"] if powers else lax.psum(sums["S"], ("dp", "tensor"))
    heads = [sums[name] for name in ("P", "Q") if name in sums]
    if staged:
        grad_down, grad_up = placed_sums["PD"], placed_sums["PU"]
        pieces = heads[0].pieces()
        grad_qkv, grad_out = place_heads(scalars, pieces, 0, pairs, None, head_bits[0])
        order.leave(grad_out)
        for pair in range(1, pairs):
            pieces = heads[pair].pieces()
            (grad_qkv,) = place_heads(
                scalars, pieces, pair, pairs, grad_qkv, head_bits[pair]
            )
        grad_qkv = grad_qkv.transpose(1, 0, 2)
    else:
        grad_down, grad_up, *blocks = [
            v.astype(F32) for v in lax.psum((sums["D"], sums["U"], *heads), "dp")
        ]
        grad_out = blocks[0][384:]
        blocks = [grad[:384].reshape(3, 128, width) for grad in blocks]
        grad_qkv = jnp.concatenate(blocks, axis=1).transpose(2, 0, 1)
    group = small[8 : 8 + GROUPS]
    group_rms = jnp.sqrt(group[:, :3] / (group[:, 3:4] * width))
    return (
        jnp.stack([row.output for row in rows]),
        jnp.stack([row.input_grad for row in rows]),
        grad_qkv,
        grad_out,
        grad_up,
        grad_down,
        small[:4],
        small[4:8],
        group_rms,
    )


def solution(mesh):
    placed = (
        P("dp", "tensor", None),
        P("dp", "tensor", None),
        P("dp"),
        P("dp"),
        P(None, None, "tensor"),
        P("tensor", None),
        P(None, "tensor"),
        P("tensor", None),
        P(),
        P(),
    )
    return jax.shard_map(
        per_device,
        mesh=mesh,
        in_specs=placed,
        out_specs=(
            P("dp", "tensor", None),
            P("dp", "tensor", None),
            P(None, None, "tensor"),
            P("tensor", None),
            P(None, "tensor"),
            P("tensor", None),
            P(),
            P(),
            P(),
        ),
        check_vma=False,
    )
```
